32 devices in a mesh: ctx: 8 (over y, x, core), fsdp: 4 (over z).
Axes of the slice: x: 2, y: 2, z: 4, core: 2. Of those that a mesh axis runs over, the one named last changes fastest.
Arguments:
- block_input: bfloat16 [2, 4, 512, 1536], P(None, 'fsdp', 'ctx'), may hold values from -6 to 6
- positions: int32 [2, 4, 512], P(None, 'fsdp', 'ctx'), may hold values from 0 to 511, as said below
- segments: int32 [2, 4, 512], P(None, 'fsdp', 'ctx'), may hold values from 0 to 2, as said below
- out_cotangent: bfloat16 [2, 4, 512, 1536], P(None, 'fsdp', 'ctx'), may hold values from -6 to 6
- attn_gain: bfloat16 [1536], P(('ctx', 'fsdp')), may hold values from 0.5 to 1.5
- w_query: bfloat16 [1536, 1536], P(('ctx', 'fsdp')), may hold values from -0.15625 to 0.15625
- w_key: bfloat16 [1536, 768], P(('ctx', 'fsdp')), may hold values from -0.15625 to 0.15625
- w_value: bfloat16 [1536, 768], P(('ctx', 'fsdp')), may hold values from -0.15625 to 0.15625
- w_out: bfloat16 [1536, 1536], P(('ctx', 'fsdp')), may hold values from -0.625 to 0.625
- mlp_gain: bfloat16 [1536], P(('ctx', 'fsdp')), may hold values from 0.5 to 1.5
- w_gate: bfloat16 [1536, 4096], P(('ctx', 'fsdp')), may hold values from -0.15625 to 0.15625
- w_up: bfloat16 [1536, 4096], P(('ctx', 'fsdp')), may hold values from -0.15625 to 0.15625
- w_down: bfloat16 [4096, 1536], P(('ctx', 'fsdp')), may hold values from -0.09375 to 0.09375
Outputs:
- block_output: bfloat16 [2, 4, 512, 1536], P(None, 'fsdp', 'ctx')
- input_grad: bfloat16 [2, 4, 512, 1536], P(None, 'fsdp', 'ctx')
- grad_attn_gain: float32 [1536], P(('ctx', 'fsdp'))
- grad_query: float32 [1536, 1536], P(('ctx', 'fsdp'))
- grad_key: float32 [1536, 768], P(('ctx', 'fsdp'))
- grad_value: float32 [1536, 768], P(('ctx', 'fsdp'))
- grad_out: float32 [1536, 1536], P(('ctx', 'fsdp'))
- grad_mlp_gain: float32 [1536], P(('ctx', 'fsdp'))
- grad_gate: float32 [1536, 4096], P(('ctx', 'fsdp'))
- grad_up: float32 [1536, 4096], P(('ctx', 'fsdp'))
- grad_down: float32 [4096, 1536], P(('ctx', 'fsdp'))
The draws below stay inside these ranges and needn't reach their ends.
Inputs may be any that keep to these rules, and one draw needn't show every extreme that they name: In each sequence every position appears once; the 64 tokens of one index of ctx are 32 consecutive positions starting at c * 32 followed by 32 starting at (15 - c) * 32, for some c below 8. `segments`: ordered by position, segment ids start at 0 and rise by one at each new document, except that the last document of each sequence has the id 512 // 200; every document has 200 to 2000 positions except that the last of a sequence may have fewer.
All inputs are finite; a program needn't handle non-finite values.
Results may differ from the reference program's by a relative error of at most 0.02.
Values may be sent and summed in bfloat16 or wider, within the bound.
No kernel may reach another device: no remote copies, remote signals or barrier semaphores. Data moves between devices by JAX's collectives and lax.ppermute only.
A program may use at most 192 MiB of HBM per device.

```python
import math
import jax
import jax.numpy as jnp
from jax import lax

D = 1536
FF = 4096
HEADS = 16
KV_HEADS = 8
HEAD = 96
TOK = 64
MB = 2
DOC_MIN = 200
DOC_MAX = 2000
SEQ = 512
BATCH = 4


def layout_tables(key):
    span_len = TOK // 2
    rank_count = SEQ // TOK
    seq_count = MB * BATCH
    perm_keys = jax.random.split(jax.random.fold_in(key, 11), seq_count)
    orders = jax.vmap(lambda subkey: jax.random.permutation(subkey, rank_count))(perm_keys)
    slot_ids = jnp.arange(TOK)[None, None, :]
    first_block = orders[:, :, None] * span_len + slot_ids
    second_block = (2 * rank_count - 1 - orders[:, :, None]) * span_len + slot_ids - span_len
    placed = jnp.where(slot_ids < span_len, first_block, second_block).reshape(seq_count, SEQ).astype(jnp.int32)
    doc_count = SEQ // DOC_MIN + 1
    lengths_drawn = jax.random.randint(jax.random.fold_in(key, 23), (seq_count, doc_count), DOC_MIN, DOC_MAX + 1)
    doc_ends = jnp.cumsum(lengths_drawn, axis=1)
    ordered = jnp.sum((doc_ends[:, None, :] <= jnp.arange(SEQ)[None, :, None]).astype(jnp.int32), axis=2)
    last_doc = ordered[:, SEQ - 1:SEQ]
    ordered = jnp.where(ordered == last_doc, SEQ // DOC_MIN, ordered).astype(jnp.int32)
    labels = jnp.take_along_axis(ordered, placed, axis=1)
    return (placed.reshape(MB, BATCH, SEQ), labels.reshape(MB, BATCH, SEQ).astype(jnp.int32))


def draw_positions(key, part):
    return layout_tables(key)[0]


def draw_segments(key, part):
    return layout_tables(key)[1]


def block_levels(own_key, dims, cuts, smallest, high):
    gain, own = 1.0, jax.random.fold_in(own_key, 6)
    for axis_at, shards_of in cuts:
        steps = jnp.exp(jax.random.uniform(jax.random.fold_in(own, axis_at), (shards_of,), jnp.float32, smallest / len(cuts), high / len(cuts)))
        gain = gain * jnp.repeat(steps, dims[axis_at] // shards_of).reshape([-1 if axis == axis_at else 1 for axis in range(len(dims))])
    return gain


def centred(own_key, extent, scale, limit, pieces=(), kind=jnp.bfloat16):
    values = scale * jax.random.normal(own_key, extent, jnp.float32)
    if pieces:
        values = values * block_levels(own_key, extent, pieces, -0.22, 0.18)
    return jnp.clip(values, -limit, limit).astype(kind)


def setup_inputs(seed: int = 0) -> dict:
    streams_of = jax.random.split(jax.random.key(seed), 14)
    block_input = centred(streams_of[0], (MB, BATCH, SEQ, D), 1.0, 6.0, ((1, 4), (2, 8)))
    positions = draw_positions(jax.random.fold_in(streams_of[13], 71), 0)
    segments = draw_segments(jax.random.fold_in(streams_of[13], 71), 0)
    out_cotangent = centred(streams_of[3], (MB, BATCH, SEQ, D), 1.0, 6.0, ((1, 4), (2, 8)))
    attn_gain = jnp.clip(1.0 + 0.1 * jax.random.normal(streams_of[4], (D,), jnp.float32), 0.5, 1.5).astype(jnp.bfloat16)
    w_query = centred(streams_of[5], (D, D), D ** -0.5, 0.15625, ((0, 32),))
    w_key = centred(streams_of[6], (D, KV_HEADS * HEAD), D ** -0.5, 0.15625, ((0, 32),))
    w_value = centred(streams_of[7], (D, KV_HEADS * HEAD), D ** -0.5, 0.15625, ((0, 32),))
    w_out = centred(streams_of[8], (D, D), (D // 16) ** -0.5, 0.625, ((0, 32),))
    mlp_gain = jnp.clip(1.0 + 0.1 * jax.random.normal(streams_of[9], (D,), jnp.float32), 0.5, 1.5).astype(jnp.bfloat16)
    w_gate = centred(streams_of[10], (D, FF), D ** -0.5, 0.15625, ((0, 32),))
    w_up = centred(streams_of[11], (D, FF), D ** -0.5, 0.15625, ((0, 32),))
    w_down = centred(streams_of[12], (FF, D), FF ** -0.5, 0.09375, ((0, 32),))
    return {"block_input": block_input, "positions": positions, "segments": segments, "out_cotangent": out_cotangent, "attn_gain": attn_gain, "w_query": w_query, "w_key": w_key, "w_value": w_value, "w_out": w_out, "mlp_gain": mlp_gain, "w_gate": w_gate, "w_up": w_up, "w_down": w_down}


@jax.custom_vjp
def low(v):
    return lax.optimization_barrier(v.astype(jnp.bfloat16)).astype(jnp.float32)

@jax.custom_vjp
def low_back(v):
    return v

def low_keep(v):
    return (low(v), None)

def low_pass(kept, grad):
    return (grad,)

def back_keep(v):
    return (v, None)

def back_low(kept, grad):
    return (low(grad),)
low.defvjp(low_keep, low_pass)
low_back.defvjp(back_keep, back_low)
epsilon = 1e-05
theta_base = 100000.0
highest_precision = lax.Precision.HIGHEST

def rope_tables(position_ids, head_size):
    half_size = head_size // 2
    ladder = jnp.arange(half_size).astype(jnp.float32) * (2.0 / head_size)
    inverse = jnp.exp(-math.log(theta_base) * ladder)
    angles = position_ids.astype(jnp.float32)[:, None] * inverse[None, :]
    return (jnp.cos(angles)[:, None, :], jnp.sin(angles)[:, None, :])

def rotate(vectors, cosine_part, sine_part):
    half_size = vectors.shape[-1] // 2
    first_half = vectors[..., :half_size]
    second_half = vectors[..., half_size:]
    return jnp.concatenate([first_half * cosine_part - second_half * sine_part, second_half * cosine_part + first_half * sine_part], axis=-1)

def rms_scale(values_in):
    return lax.rsqrt(lax.optimization_barrier(jnp.mean(values_in * values_in, axis=-1, keepdims=True)) + epsilon)

def product(left_side, right_side):
    return jnp.einsum('td,de->te', left_side, right_side, precision=highest_precision)

def attend(query_rot, key_rot, value_rows, position_ids, segment_ids):
    block_len = math.gcd(SEQ, 512)
    block_count = SEQ // block_len
    factor = HEAD ** (-0.5)
    every_key_row = key_rot.reshape(SEQ, KV_HEADS, HEAD)
    every_value_row = value_rows.reshape(SEQ, KV_HEADS, HEAD)

    def one_block(block_item):
        query_block, pos_block, seg_block = block_item
        grouped_heads = query_block.reshape(block_len, KV_HEADS, 2, HEAD)
        unscaled_scores = jnp.einsum('emlp,ump->mleu', grouped_heads, every_key_row, precision=highest_precision)
        scores = low_back(unscaled_scores * factor)
        allowed = (seg_block[:, None] == segment_ids[None, :]) & (position_ids[None, :] <= pos_block[:, None])
        scores = jnp.where(allowed[None, None], scores, -1e+30)
        row_max = lax.optimization_barrier(jnp.max(scores, axis=-1, keepdims=True))
        raised = jnp.exp(scores - row_max)
        softmax_rows = low(raised / lax.optimization_barrier(jnp.sum(raised, axis=-1, keepdims=True)))
        mixed_values = jnp.einsum('mudo,omf->dmuf', softmax_rows, every_value_row, precision=highest_precision)
        return mixed_values.reshape(block_len, HEADS * HEAD)
    blocks = lax.map(jax.checkpoint(one_block), (query_rot.reshape(block_count, block_len, HEADS * HEAD), position_ids.reshape(block_count, block_len), segment_ids.reshape(block_count, block_len)))
    return blocks.reshape(SEQ, HEADS * HEAD)

def forward_sequence(residual, params, position_ids, segment_ids):
    gain_one, query_w, key_w, value_w, out_w, gain_two, gate_w, up_w, down_w = params
    cosine_part, sine_part = rope_tables(position_ids, HEAD)
    normed_one = residual * rms_scale(residual)
    hidden_one = low(normed_one * gain_one)
    queries = low_back(product(hidden_one, query_w))
    keys_pre = low_back(product(hidden_one, key_w))
    value_rows = low(low_back(product(hidden_one, value_w)))
    query_rot = low(rotate(queries.reshape(SEQ, HEADS, HEAD), cosine_part, sine_part)).reshape(SEQ, HEADS * HEAD)
    key_rot = low(rotate(keys_pre.reshape(SEQ, KV_HEADS, HEAD), cosine_part, sine_part)).reshape(SEQ, KV_HEADS * HEAD)
    attended = low(low_back(attend(query_rot, key_rot, value_rows, position_ids, segment_ids)))
    middle = residual + low_back(product(attended, out_w))
    normed_two = middle * rms_scale(middle)
    hidden_two = low(normed_two * gain_two)
    gate_rows = low_back(product(hidden_two, gate_w))
    up_rows = low_back(product(hidden_two, up_w))
    activated = low(jax.nn.silu(gate_rows) * up_rows)
    return middle + low_back(product(activated, down_w))

def reference(block_input, positions, segments, out_cotangent, attn_gain, w_query, w_key, w_value, w_out, mlp_gain, w_gate, w_up, w_down):
    seq_count = MB * BATCH
    params = tuple((weight.astype(jnp.float32) for weight in (attn_gain, w_query, w_key, w_value, w_out, mlp_gain, w_gate, w_up, w_down)))
    inputs_all = block_input.reshape(seq_count, SEQ, D).astype(jnp.float32)
    cotangents = out_cotangent.reshape(seq_count, SEQ, D).astype(jnp.float32)
    pos_all = positions.reshape(seq_count, SEQ)
    seg_all = segments.reshape(seq_count, SEQ)

    def one_sequence(totals, seq_item):
        residual, cotangent, position_ids, segment_ids = seq_item

        def apply_layer(resid_in, param_in):
            return forward_sequence(resid_in, param_in, position_ids, segment_ids)
        result, pullback = jax.vjp(apply_layer, residual, params)
        grad_input, grad_params = pullback(cotangent)
        totals = tuple((total_old + grad_new for total_old, grad_new in zip(totals, grad_params)))
        return (totals, (result.astype(jnp.bfloat16), grad_input.astype(jnp.bfloat16)))
    zeros_start = tuple((jnp.zeros(weight.shape, jnp.float32) for weight in params))
    totals, (outputs_all, grads_all) = lax.scan(one_sequence, zeros_start, (inputs_all, cotangents, pos_all, seg_all))
    block_output = outputs_all.reshape(MB, BATCH, SEQ, D)
    input_grad = grads_all.reshape(MB, BATCH, SEQ, D)
    return (block_output, input_grad, totals[0], totals[1], totals[2], totals[3], totals[4], totals[5], totals[6], totals[7], totals[8])
```

```python
import math

import jax
import jax.numpy as jnp
from jax import lax
from jax.sharding import Mesh, PartitionSpec as P

HEADS = 16
KV_HEADS = 8
HEAD = 96
EPS = 1e-05
THETA = 100000.0
f32 = jnp.float32
bf16 = jnp.bfloat16


def rope_tables(position_ids):
    half = HEAD // 2
    ladder = jnp.arange(half).astype(f32) * (2.0 / HEAD)
    inverse = jnp.exp(-math.log(THETA) * ladder)
    angles = position_ids.astype(f32)[:, None] * inverse[None, :]
    return jnp.cos(angles)[:, None, :], jnp.sin(angles)[:, None, :]


def rotate(vectors, cosine, sine):
    half = HEAD // 2
    a, b = vectors[..., :half], vectors[..., half:]
    return jnp.concatenate([a * cosine - b * sine, b * cosine + a * sine], axis=-1)


def unrotate(grads, cosine, sine):
    half = HEAD // 2
    a, b = grads[..., :half], grads[..., half:]
    return jnp.concatenate([a * cosine + b * sine, b * cosine - a * sine], axis=-1)


def rms_scale(values):
    return lax.rsqrt(jnp.mean(values * values, axis=-1, keepdims=True) + EPS)


def norm_back(grad, normed, scale):
    return scale * (grad - normed * jnp.mean(grad * normed, axis=-1, keepdims=True))


def mm(a, b):
    return jnp.dot(a, b, preferred_element_type=f32)


def mm_tn(a, b):
    return jnp.einsum("td,te->de", a, b, preferred_element_type=f32)


def mm_nt(a, b):
    return jnp.einsum("te,de->td", a, b, preferred_element_type=f32)


def on_device(
    block_input,
    positions,
    segments,
    out_cotangent,
    attn_gain,
    w_query,
    w_key,
    w_value,
    w_out,
    mlp_gain,
    w_gate,
    w_up,
    w_down,
):
    chips = lax.axis_size("chip")
    rows_z = lax.axis_size("fsdp")
    chip = lax.axis_index("chip")
    core = lax.axis_index("core")
    place = lax.axis_index("fsdp")
    tok = block_input.shape[2]
    width = block_input.shape[3]
    d_rows = w_query.shape[0]
    q_cols = w_query.shape[1] // chips
    kv_cols = w_key.shape[1] // chips
    ff_cols = w_gate.shape[1] // chips
    kv_heads = KV_HEADS // chips
    factor = HEAD ** (-0.5)

    def core_swap(a):
        return lax.ppermute(a, "core", [(0, 1), (1, 0)])

    def chip_xor(a, j):
        return lax.ppermute(a, "chip", [(i, i ^ j) for i in range(chips)])

    def pick(a, index, axis=0):
        return lax.dynamic_index_in_dim(a, index, axis, keepdims=False)

    def gather_chips(a, axis=0):
        return jnp.concatenate([a] + [chip_xor(a, j) for j in range(1, chips)], axis=axis)

    def scatter_chips(a):
        step = a.shape[0] // chips
        total = a[:step]
        for j in range(1, chips):
            total = total + chip_xor(a[j * step : (j + 1) * step].astype(bf16), j).astype(f32)
        return total

    def by_chip(pieces):
        stacked = jnp.stack(pieces)
        bit = 1
        while bit < chips:
            view = stacked.reshape((chips // (2 * bit), 2, bit) + stacked.shape[1:])
            flipped = jnp.flip(view, axis=1)
            stacked = jnp.where((chip & bit) != 0, flipped, view).reshape(stacked.shape)
            bit *= 2
        return stacked

    def exchange_chips(pack):
        pieces = [pick(pack, chip)]
        for j in range(1, chips):
            pieces.append(chip_xor(pick(pack, chip ^ j), j))
        return by_chip(pieces)

    def both_cores(a):
        other = core_swap(a)
        first = core == 0
        return jnp.where(first, a, other), jnp.where(first, other, a)

    def chip_slices(weights, cols):
        return jnp.stack(
            [
                jnp.concatenate([w[:, k * n : (k + 1) * n] for w, n in zip(weights, cols)], axis=1)
                for k in range(chips)
            ]
        )

    def fetch_columns(pack):
        mine = exchange_chips(pack)
        cols = mine.shape[-1]
        along = lax.all_gather(mine.reshape(-1, cols), "fsdp", axis=0, tiled=True)
        along = along.reshape(rows_z, chips, d_rows, cols)
        zero, one = both_cores(along)
        full = jnp.stack([zero, one])
        return jnp.transpose(full, (2, 0, 1, 3, 4)).reshape(chips * 2 * rows_z * d_rows, cols)

    def fetch_rows(weight):
        along = lax.all_gather(weight, "fsdp", axis=0, tiled=True)
        return jnp.concatenate(both_cores(along), axis=0)

    pair = jnp.stack([block_input[:, 0], out_cotangent[:, 0]], axis=1)
    pair = jnp.concatenate([pick(pair, core), core_swap(pick(pair, 1 - core))], axis=1)
    x_low, dy_low = pair[0], pair[1]
    marks = jnp.stack([positions[:, 0], segments[:, 0]], axis=1)
    marks = jnp.concatenate([pick(marks, core), core_swap(pick(marks, 1 - core))], axis=1)

    owner = (chip * 2 + core) * rows_z + place
    gains = jnp.zeros((2, width), bf16)
    gains = lax.dynamic_update_slice(
        gains, jnp.stack([attn_gain, mlp_gain]), (0, owner * d_rows)
    )

    def sum_everywhere(a):
        a = a + core_swap(a)
        bit = 1
        while bit < chips:
            a = a + chip_xor(a, bit)
            bit *= 2
        bit = 1
        while bit < rows_z:
            a = a + lax.ppermute(a, "fsdp", [(i, i ^ bit) for i in range(rows_z)])
            bit *= 2
        return a

    w_qkv = fetch_columns(chip_slices((w_query, w_key, w_value), (q_cols, kv_cols, kv_cols)))
    x_all = gather_chips(x_low)
    marks_all = gather_chips(marks, axis=1)
    gains = sum_everywhere(gains).astype(f32)
    gain_one, gain_two = gains[0], gains[1]
    out_w = fetch_rows(w_out)
    w_gu = fetch_columns(chip_slices((w_gate, w_up), (ff_cols, ff_cols)))
    down_w = fetch_rows(w_down)
    dy_all = gather_chips(dy_low)
    own = x_low.shape[0]
    seq = x_all.shape[0]

    pos_all, seg_all = marks_all[0], marks_all[1]
    allowed = (seg_all[:, None] == seg_all[None, :]) & (pos_all[None, :] <= pos_all[:, None])
    cosine, sine = rope_tables(pos_all)
    x_full = x_all.astype(f32)
    h_one = (x_full * rms_scale(x_full) * gain_one).astype(bf16)
    qkv = mm(h_one, w_qkv)
    q_rot = rotate(qkv[:, :q_cols].reshape(seq, kv_heads * 2, HEAD), cosine, sine)
    q_rot = q_rot.astype(bf16).reshape(seq, kv_heads, 2, HEAD)
    k_rot = rotate(
        qkv[:, q_cols : q_cols + kv_cols].reshape(seq, kv_heads, HEAD), cosine, sine
    ).astype(bf16)
    value = qkv[:, q_cols + kv_cols :].astype(bf16).reshape(seq, kv_heads, HEAD)
    scores = jnp.einsum("sgrh,tgh->grst", q_rot, k_rot, preferred_element_type=f32) * factor
    scores = jnp.where(allowed, scores, -1e30)
    raised = jnp.exp(scores - jnp.max(scores, axis=-1, keepdims=True))
    soft = raised / jnp.sum(raised, axis=-1, keepdims=True)
    soft_low = soft.astype(bf16)
    mixed = jnp.einsum("grst,tgh->sgrh", soft_low, value, preferred_element_type=f32)
    mixed = mixed.astype(bf16).reshape(seq, q_cols)
    x_own = x_low.astype(f32)
    middle = x_own + scatter_chips(mm(mixed, out_w))

    scale_two = rms_scale(middle)
    n_two = middle * scale_two
    h_two = gather_chips((n_two * gain_two).astype(bf16))
    gu = mm(h_two, w_gu)
    gate, up = gu[:, :ff_cols], gu[:, ff_cols:]
    sigma = jax.nn.sigmoid(gate)
    act = (gate * sigma * up).astype(bf16)
    result = (middle + scatter_chips(mm(act, down_w))).astype(bf16)

    d_act = mm_nt(dy_all, down_w)
    d_gate = (d_act * up * sigma * (1.0 + gate * (1.0 - sigma))).astype(bf16)
    d_up = (d_act * gate * sigma).astype(bf16)
    d_gu = jnp.concatenate([d_gate, d_up], axis=1)
    d_h_two = scatter_chips(mm_nt(d_gu, w_gu))

    def reduce_columns(left, right):
        grad = mm_tn(left, right).astype(bf16)
        cols = grad.shape[1]
        grad = grad.reshape(chips, 2, rows_z, d_rows, cols)
        other = core_swap(pick(grad, 1 - core, 1))
        total = pick(grad, core, 1) + other
        total = jnp.transpose(total, (1, 0, 2, 3)).reshape(rows_z * chips * d_rows, cols)
        total = lax.psum_scatter(total, "fsdp", scatter_dimension=0, tiled=True)
        return exchange_chips(total.reshape(chips, d_rows, cols))

    def reduce_rows(left, right):
        grad = mm_tn(left, right).astype(bf16)
        grad = grad.reshape(2, grad.shape[0] // 2, grad.shape[1])
        total = pick(grad, core) + core_swap(pick(grad, 1 - core))
        return lax.psum_scatter(total, "fsdp", scatter_dimension=0, tiled=True).astype(f32)

    g_gu = reduce_columns(h_two, d_gu)
    g_down = reduce_rows(act, dy_all)
    dy_own = dy_low.astype(f32)
    gain_two_part = jnp.sum(d_h_two * n_two, axis=0)
    d_middle = dy_own + norm_back(d_h_two * gain_two, n_two, scale_two)
    branch = gather_chips(d_middle.astype(bf16))

    g_out = reduce_rows(mixed, branch)
    d_mixed = mm_nt(branch, out_w).astype(bf16).reshape(seq, kv_heads, 2, HEAD)
    d_soft = jnp.einsum("sgrh,tgh->grst", d_mixed, value, preferred_element_type=f32)
    d_value = jnp.einsum("grst,sgrh->tgh", soft_low, d_mixed, preferred_element_type=f32)
    inner = jnp.sum(soft * d_soft, axis=-1, keepdims=True)
    d_scores = (soft * (d_soft - inner)).astype(bf16)
    d_q = jnp.einsum("grst,tgh->sgrh", d_scores, k_rot, preferred_element_type=f32) * factor
    d_k = jnp.einsum("grst,sgrh->tgh", d_scores, q_rot, preferred_element_type=f32) * factor
    d_q = unrotate(d_q.reshape(seq, kv_heads * 2, HEAD), cosine, sine)
    d_k = unrotate(d_k, cosine, sine)
    d_qkv = jnp.concatenate(
        [
            d_q.reshape(seq, q_cols).astype(bf16),
            d_k.reshape(seq, kv_cols).astype(bf16),
            d_value.reshape(seq, kv_cols).astype(bf16),
        ],
        axis=1,
    )
    d_h_one = scatter_chips(mm_nt(d_qkv, w_qkv))
    g_qkv = reduce_columns(h_one, d_qkv)
    scale_one = rms_scale(x_own)
    n_one = x_own * scale_one
    gain_one_part = jnp.sum(d_h_one * n_one, axis=0)
    d_input = (d_middle + norm_back(d_h_one * gain_one, n_one, scale_one)).astype(bf16)

    def give_back(a):
        mine, theirs = a[:tok], core_swap(a[tok:])
        first = core == 0
        return jnp.stack([jnp.where(first, mine, theirs), jnp.where(first, theirs, mine)])[:, None]

    def spread(grad, start, cols):
        part = grad[:, :, start : start + cols].astype(f32)
        return jnp.transpose(part, (1, 0, 2)).reshape(d_rows, chips * cols)

    gain_parts = sum_everywhere(jnp.stack([gain_one_part, gain_two_part]))
    gain_parts = lax.dynamic_slice_in_dim(gain_parts, owner * d_rows, d_rows, 1)
    return (
        give_back(result),
        give_back(d_input),
        gain_parts[0],
        spread(g_qkv, 0, q_cols),
        spread(g_qkv, q_cols, kv_cols),
        spread(g_qkv, q_cols + kv_cols, kv_cols),
        g_out,
        gain_parts[1],
        spread(g_gu, 0, ff_cols),
        spread(g_gu, ff_cols, ff_cols),
        g_down,
    )


def solution(mesh):
    ctx, fsdp = mesh.shape["ctx"], mesh.shape["fsdp"]
    split = Mesh(mesh.devices.reshape(ctx // 2, 2, fsdp), ("chip", "core", "fsdp"))
    ctx_axes = ("chip", "core")
    all_axes = ("chip", "core", "fsdp")
    tokens = P(None, "fsdp", ctx_axes, None)
    marks = P(None, "fsdp", ctx_axes)
    vector, matrix = P(all_axes), P(all_axes, None)
    return jax.shard_map(
        on_device,
        mesh=split,
        in_specs=(
            tokens, marks, marks, tokens, vector, matrix, matrix, matrix, matrix,
            vector, matrix, matrix, matrix,
        ),
        out_specs=(
            tokens, tokens, vector, matrix, matrix, matrix, matrix, vector,
            matrix, matrix, matrix,
        ),
        check_vma=False,
    )
```

```python
import math

import jax
import jax.numpy as jnp
from jax import lax
from jax.sharding import Mesh, PartitionSpec as P

HEADS = 16
KV_HEADS = 8
HEAD = 96
EPS = 1e-05
THETA = 100000.0
f32 = jnp.float32
bf16 = jnp.bfloat16


def rope_tables(position_ids):
    half = HEAD // 2
    ladder = jnp.arange(half).astype(f32) * (2.0 / HEAD)
    inverse = jnp.exp(-math.log(THETA) * ladder)
    angles = position_ids.astype(f32)[:, None] * inverse[None, :]
    return jnp.cos(angles)[:, None, :], jnp.sin(angles)[:, None, :]


def rotate(vectors, cosine, sine):
    half = HEAD // 2
    a, b = vectors[..., :half], vectors[..., half:]
    return jnp.concatenate([a * cosine - b * sine, b * cosine + a * sine], axis=-1)


def unrotate(grads, cosine, sine):
    half = HEAD // 2
    a, b = grads[..., :half], grads[..., half:]
    return jnp.concatenate([a * cosine + b * sine, b * cosine - a * sine], axis=-1)


def rms_scale(values):
    return lax.rsqrt(jnp.mean(values * values, axis=-1, keepdims=True) + EPS)


def norm_back(grad, normed, scale):
    return scale * (grad - normed * jnp.mean(grad * normed, axis=-1, keepdims=True))


def mm(a, b):
    return jnp.dot(a, b, preferred_element_type=f32)


def mm_tn(a, b):
    return jnp.einsum("td,te->de", a, b, preferred_element_type=f32)


def mm_nt(a, b):
    return jnp.einsum("te,de->td", a, b, preferred_element_type=f32)


def on_device(
    block_input,
    positions,
    segments,
    out_cotangent,
    attn_gain,
    w_query,
    w_key,
    w_value,
    w_out,
    mlp_gain,
    w_gate,
    w_up,
    w_down,
):
    chips = lax.axis_size("chip")
    rows_z = lax.axis_size("fsdp")
    chip = lax.axis_index("chip")
    core = lax.axis_index("core")
    place = lax.axis_index("fsdp")
    tok = block_input.shape[2]
    width = block_input.shape[3]
    d_rows = w_query.shape[0]
    q_cols = w_query.shape[1] // chips
    kv_cols = w_key.shape[1] // chips
    ff_cols = w_gate.shape[1] // (2 * chips)
    kv_heads = KV_HEADS // chips
    factor = HEAD ** (-0.5)

    def core_swap(a):
        return lax.ppermute(a, "core", [(0, 1), (1, 0)])

    def chip_xor(a, j):
        return lax.ppermute(a, "chip", [(i, i ^ j) for i in range(chips)])

    def pick(a, index, axis=0):
        return lax.dynamic_index_in_dim(a, index, axis, keepdims=False)

    def gather_chips(a, axis=0):
        return jnp.concatenate([a] + [chip_xor(a, j) for j in range(1, chips)], axis=axis)

    def scatter_chips(a):
        step = a.shape[0] // chips
        total = a[:step]
        for j in range(1, chips):
            total = total + chip_xor(a[j * step : (j + 1) * step].astype(bf16), j).astype(f32)
        return total

    def by_chip(pieces):
        stacked = jnp.stack(pieces)
        bit = 1
        while bit < chips:
            view = stacked.reshape((chips // (2 * bit), 2, bit) + stacked.shape[1:])
            flipped = jnp.flip(view, axis=1)
            stacked = jnp.where((chip & bit) != 0, flipped, view).reshape(stacked.shape)
            bit *= 2
        return stacked

    def exchange_chips(pack):
        pieces = [pick(pack, chip)]
        for j in range(1, chips):
            pieces.append(chip_xor(pick(pack, chip ^ j), j))
        return by_chip(pieces)

    def core_pair(mine, other, axis):
        first = core == 0
        return jnp.stack([jnp.where(first, mine, other), jnp.where(first, other, mine)], axis)

    def both_cores(a):
        return core_pair(a, core_swap(a), 0)

    def chip_slices(weights, cols):
        return jnp.stack(
            [
                jnp.concatenate([w[:, k * n : (k + 1) * n] for w, n in zip(weights, cols)], axis=1)
                for k in range(chips)
            ]
        )

    def after(value, *others):
        return lax.optimization_barrier((value,) + others)[0]

    def along_z(a, step):
        return lax.ppermute(a, "fsdp", [(i, (i + step) % rows_z) for i in range(rows_z)])

    def ring_gather(a):
        found = {0: a}
        right, left = a, a
        for step in range(1, rows_z // 2 + 1):
            if 2 * step == rows_z:
                half = a.shape[-1] // 2
                low = along_z(right[..., :half], 1)
                high = along_z(left[..., half:], -1)
                found[step] = jnp.concatenate([low, high], axis=-1)
            else:
                right, left = along_z(right, 1), along_z(left, -1)
                found[rows_z - step], found[step] = right, left
        return jnp.stack([found[step] for step in range(rows_z)])

    def by_place(a):
        doubled = jnp.concatenate([a, a])
        return lax.dynamic_slice_in_dim(doubled, rows_z - place, rows_z, 0)

    def order_columns(along):
        cols = along.shape[-1]
        full = both_cores(along.reshape(rows_z, chips, d_rows, cols))
        return jnp.transpose(full, (2, 0, 1, 3, 4)).reshape(chips * 2 * rows_z * d_rows, cols)

    pair = jnp.stack([block_input[:, 0], out_cotangent[:, 0]], axis=1)
    pair = jnp.concatenate([pick(pair, core), core_swap(pick(pair, 1 - core))], axis=1)
    x_low, dy_low = pair[0], pair[1]

    owner = (chip * 2 + core) * rows_z + place
    spot = chip * 2 + core
    gains = lax.dynamic_update_slice(
        jnp.zeros((2, width), f32),
        jnp.stack([attn_gain, mlp_gain]).astype(f32),
        (0, owner * d_rows),
    )
    marks = lax.dynamic_update_slice(
        jnp.zeros((4, chips * 2 * tok), f32),
        jnp.concatenate([positions[:, 0], segments[:, 0]]).astype(f32),
        (0, spot * tok),
    )
    table = jnp.concatenate([gains.reshape(-1), marks.reshape(-1)]).reshape(-1, 128)

    def sum_plane(a):
        a = a + core_swap(a)
        bit = 1
        while bit < chips:
            a = a + chip_xor(a, bit)
            bit *= 2
        return a

    def sum_z(a):
        bit = 1
        while bit < rows_z:
            a = a + lax.ppermute(a, "fsdp", [(i, i ^ bit) for i in range(rows_z)])
            bit *= 2
        return a

    pack_qkv = chip_slices((w_query, w_key, w_value), (q_cols, kv_cols, kv_cols))
    piece_qkv = exchange_chips(pack_qkv).reshape(-1, pack_qkv.shape[-1])
    out_rel = ring_gather(w_out)
    qkv_rel = ring_gather(piece_qkv)
    along_down = lax.all_gather(w_down, "fsdp", axis=0, tiled=True)
    x_all = gather_chips(x_low)
    w_qkv = order_columns(by_place(qkv_rel))
    out_w = both_cores(by_place(out_rel)).reshape(-1, width)
    pack_gu = jnp.stack(
        [
            jnp.concatenate([w[:, n * ff_cols : (n + 1) * ff_cols] for w in (w_gate, w_up)], axis=1)
            for n in range(2 * chips)
        ]
    ).reshape(chips, 2, d_rows, 2 * ff_cols)
    piece_gu = exchange_chips(after(pack_gu, piece_qkv))
    piece_gu = core_pair(pick(piece_gu, core, 1), core_swap(pick(piece_gu, 1 - core, 1)), 1)
    along_gu = lax.all_gather(
        piece_gu.reshape(2 * chips * d_rows, 2 * ff_cols), "fsdp", axis=0, tiled=True
    )
    table = sum_plane(table).reshape(-1)
    gain_one, gain_two = sum_z(table[: 2 * width].reshape(2, width))
    marks = table[2 * width :].reshape(2, 2, chips, 2, tok)
    marks = pick(marks, core, 1)
    marks = jnp.where(core == 0, marks, jnp.flip(marks, axis=2)).reshape(2, chips, 2 * tok)
    marks_all = by_chip([marks[:, k] for k in range(chips)])
    marks_all = jnp.transpose(marks_all, (1, 0, 2)).reshape(2, chips * 2 * tok)
    dy_all = gather_chips(dy_low)
    own = x_low.shape[0]
    seq = x_all.shape[0]

    pos_all, seg_all = marks_all[0], marks_all[1]
    allowed = (seg_all[:, None] == seg_all[None, :]) & (pos_all[None, :] <= pos_all[:, None])
    cosine, sine = rope_tables(pos_all)
    x_full = x_all.astype(f32)
    h_one = (x_full * rms_scale(x_full) * gain_one).astype(bf16)
    qkv = mm(h_one, w_qkv)
    q_rot = rotate(qkv[:, :q_cols].reshape(seq, kv_heads * 2, HEAD), cosine, sine)
    q_rot = q_rot.astype(bf16).reshape(seq, kv_heads, 2, HEAD)
    k_rot = rotate(
        qkv[:, q_cols : q_cols + kv_cols].reshape(seq, kv_heads, HEAD), cosine, sine
    ).astype(bf16)
    value = qkv[:, q_cols + kv_cols :].astype(bf16).reshape(seq, kv_heads, HEAD)
    scores = jnp.einsum("sgrh,tgh->grst", q_rot, k_rot, preferred_element_type=f32) * factor
    scores = jnp.where(allowed, scores, -1e30)
    raised = jnp.exp(scores - jnp.max(scores, axis=-1, keepdims=True))
    soft = raised / jnp.sum(raised, axis=-1, keepdims=True)
    soft_low = soft.astype(bf16)
    mixed = jnp.einsum("grst,tgh->sgrh", soft_low, value, preferred_element_type=f32)
    mixed = mixed.astype(bf16).reshape(seq, q_cols)
    x_own = x_low.astype(f32)
    middle = x_own + scatter_chips(mm(mixed, out_w))

    scale_two = rms_scale(middle)
    n_two = middle * scale_two
    h_two = gather_chips((n_two * gain_two).astype(bf16))
    dy_other = core_swap(dy_all)
    h_two, along_down, along_gu = lax.optimization_barrier((h_two, along_down, along_gu))
    h_other = core_swap(h_two)
    down_w = along_down
    w_gu = along_gu.reshape(rows_z, 2 * chips, d_rows, 2 * ff_cols)
    w_gu = jnp.transpose(w_gu, (1, 0, 2, 3)).reshape(width, 2 * ff_cols)

    def mlp_forward(h):
        gu = mm(h, w_gu)
        gate, up = gu[:, :ff_cols], gu[:, ff_cols:]
        sigma = jax.nn.sigmoid(gate)
        return gate, up, sigma, (gate * sigma * up).astype(bf16)

    def mlp_backward(dy, gate, up, sigma):
        d_act = mm_nt(dy, down_w)
        d_gate = (d_act * up * sigma * (1.0 + gate * (1.0 - sigma))).astype(bf16)
        d_up = (d_act * gate * sigma).astype(bf16)
        return jnp.concatenate([d_gate, d_up], axis=1)

    def give_partial(other_part, own_part):
        return scatter_chips(own_part + core_swap(other_part.astype(bf16)).astype(f32))

    *keep, act = mlp_forward(h_two)
    *keep_other, act_other = mlp_forward(h_other)
    d_gu_other = mlp_backward(dy_other, *keep_other)
    d_gu = mlp_backward(dy_all, *keep)
    d_h_two = give_partial(mm_nt(d_gu_other, w_gu), mm_nt(d_gu, w_gu))
    result = middle + give_partial(mm(act_other, down_w), mm(act, down_w))
    result = result.astype(bf16)

    act_both = jnp.concatenate([act, act_other])
    dy_both = jnp.concatenate([dy_all, dy_other])
    g_down = mm_tn(act_both, dy_both).astype(bf16)
    g_down = lax.psum_scatter(g_down, "fsdp", scatter_dimension=0, tiled=True).astype(f32)
    g_gu = mm_tn(jnp.concatenate([h_two, h_other]), jnp.concatenate([d_gu, d_gu_other]))
    g_gu = g_gu.astype(bf16).reshape(2 * chips, rows_z, d_rows, 2 * ff_cols)
    g_gu = jnp.transpose(g_gu, (1, 0, 2, 3)).reshape(width, 2 * ff_cols)
    g_gu = lax.psum_scatter(g_gu, "fsdp", scatter_dimension=0, tiled=True)
    g_gu = g_gu.reshape(chips, 2, d_rows, 2 * ff_cols)
    g_gu = core_pair(pick(g_gu, core, 1), core_swap(pick(g_gu, 1 - core, 1)), 1)
    g_gu = exchange_chips(g_gu)

    def reduce_columns(left, right):
        grad = mm_tn(left, right).astype(bf16)
        cols = grad.shape[1]
        grad = grad.reshape(chips, 2, rows_z, d_rows, cols)
        other = core_swap(pick(grad, 1 - core, 1))
        total = pick(grad, core, 1) + other
        total = jnp.transpose(total, (1, 0, 2, 3)).reshape(rows_z * chips * d_rows, cols)
        total = lax.psum_scatter(total, "fsdp", scatter_dimension=0, tiled=True)
        return exchange_chips(total.reshape(chips, d_rows, cols))

    def reduce_rows(left, right):
        grad = mm_tn(left, right).astype(bf16)
        grad = grad.reshape(2, grad.shape[0] // 2, grad.shape[1])
        total = pick(grad, core) + core_swap(pick(grad, 1 - core))
        return lax.psum_scatter(total, "fsdp", scatter_dimension=0, tiled=True).astype(f32)

    dy_own = dy_low.astype(f32)
    gain_two_part = jnp.sum(d_h_two * n_two, axis=0)
    d_middle = dy_own + norm_back(d_h_two * gain_two, n_two, scale_two)
    branch = gather_chips(d_middle.astype(bf16))

    g_out = reduce_rows(mixed, branch)
    d_mixed = mm_nt(branch, out_w).astype(bf16).reshape(seq, kv_heads, 2, HEAD)
    d_soft = jnp.einsum("sgrh,tgh->grst", d_mixed, value, preferred_element_type=f32)
    d_value = jnp.einsum("grst,sgrh->tgh", soft_low, d_mixed, preferred_element_type=f32)
    inner = jnp.sum(soft * d_soft, axis=-1, keepdims=True)
    d_scores = (soft * (d_soft - inner)).astype(bf16)
    d_q = jnp.einsum("grst,tgh->sgrh", d_scores, k_rot, preferred_element_type=f32) * factor
    d_k = jnp.einsum("grst,sgrh->tgh", d_scores, q_rot, preferred_element_type=f32) * factor
    d_q = unrotate(d_q.reshape(seq, kv_heads * 2, HEAD), cosine, sine)
    d_k = unrotate(d_k, cosine, sine)
    d_qkv = jnp.concatenate(
        [
            d_q.reshape(seq, q_cols).astype(bf16),
            d_k.reshape(seq, kv_cols).astype(bf16),
            d_value.reshape(seq, kv_cols).astype(bf16),
        ],
        axis=1,
    )
    d_h_one = scatter_chips(mm_nt(d_qkv, w_qkv))
    g_qkv = reduce_columns(h_one, d_qkv)
    scale_one = rms_scale(x_own)
    n_one = x_own * scale_one
    gain_one_part = jnp.sum(d_h_one * n_one, axis=0)
    d_input = (d_middle + norm_back(d_h_one * gain_one, n_one, scale_one)).astype(bf16)

    def give_back(a):
        mine, theirs = a[:tok], core_swap(a[tok:])
        first = core == 0
        return jnp.stack([jnp.where(first, mine, theirs), jnp.where(first, theirs, mine)])[:, None]

    def spread(grad, start, cols):
        part = grad[:, :, start : start + cols].astype(f32)
        return jnp.transpose(part, (1, 0, 2)).reshape(d_rows, chips * cols)

    def spread_ff(grad):
        grad = jnp.transpose(grad.astype(f32), (2, 0, 1, 3))
        return grad.reshape(d_rows, 2 * chips * ff_cols)

    gain_parts = sum_z(sum_plane(jnp.stack([gain_one_part, gain_two_part])))
    gain_parts = lax.dynamic_slice_in_dim(gain_parts, owner * d_rows, d_rows, 1)
    return (
        give_back(result),
        give_back(d_input),
        gain_parts[0],
        spread(g_qkv, 0, q_cols),
        spread(g_qkv, q_cols, kv_cols),
        spread(g_qkv, q_cols + kv_cols, kv_cols),
        g_out,
        gain_parts[1],
        spread_ff(g_gu[..., :ff_cols]),
        spread_ff(g_gu[..., ff_cols:]),
        g_down,
    )


def solution(mesh):
    ctx, fsdp = mesh.shape["ctx"], mesh.shape["fsdp"]
    split = Mesh(mesh.devices.reshape(ctx // 2, 2, fsdp), ("chip", "core", "fsdp"))
    ctx_axes = ("chip", "core")
    all_axes = ("chip", "core", "fsdp")
    tokens = P(None, "fsdp", ctx_axes, None)
    marks = P(None, "fsdp", ctx_axes)
    vector, matrix = P(all_axes), P(all_axes, None)
    return jax.shard_map(
        on_device,
        mesh=split,
        in_specs=(
            tokens, marks, marks, tokens, vector, matrix, matrix, matrix, matrix,
            vector, matrix, matrix, matrix,
        ),
        out_specs=(
            tokens, tokens, vector, matrix, matrix, matrix, matrix, vector,
            matrix, matrix, matrix,
        ),
        check_vma=False,
    )
```

```python
import math

import jax
import jax.numpy as jnp
from jax import lax
from jax.sharding import Mesh, PartitionSpec as P

HEADS = 16
KV_HEADS = 8
HEAD = 96
EPS = 1e-05
THETA = 100000.0
f32 = jnp.float32
bf16 = jnp.bfloat16


def rope_tables(position_ids):
    half = HEAD // 2
    ladder = jnp.arange(half).astype(f32) * (2.0 / HEAD)
    inverse = jnp.exp(-math.log(THETA) * ladder)
    angles = position_ids.astype(f32)[:, None] * inverse[None, :]
    return jnp.cos(angles)[:, None, :], jnp.sin(angles)[:, None, :]


def rotate(vectors, cosine, sine):
    half = HEAD // 2
    a, b = vectors[..., :half], vectors[..., half:]
    return jnp.concatenate([a * cosine - b * sine, b * cosine + a * sine], axis=-1)


def unrotate(grads, cosine, sine):
    half = HEAD // 2
    a, b = grads[..., :half], grads[..., half:]
    return jnp.concatenate([a * cosine + b * sine, b * cosine - a * sine], axis=-1)


def rms_scale(values):
    return lax.rsqrt(jnp.mean(values * values, axis=-1, keepdims=True) + EPS)


def norm_back(grad, normed, scale):
    return scale * (grad - normed * jnp.mean(grad * normed, axis=-1, keepdims=True))


def mm(a, b):
    return jnp.dot(a, b, preferred_element_type=f32)


def mm_tn(a, b):
    return jnp.einsum("td,te->de", a, b, preferred_element_type=f32)


def mm_nt(a, b):
    return jnp.einsum("te,de->td", a, b, preferred_element_type=f32)


def on_device(
    block_input,
    positions,
    segments,
    out_cotangent,
    attn_gain,
    w_query,
    w_key,
    w_value,
    w_out,
    mlp_gain,
    w_gate,
    w_up,
    w_down,
):
    chips = lax.axis_size("chip")
    rows_z = lax.axis_size("fsdp")
    chip = lax.axis_index("chip")
    core = lax.axis_index("core")
    place = lax.axis_index("fsdp")
    tok = block_input.shape[2]
    width = block_input.shape[3]
    d_rows = w_query.shape[0]
    q_cols = w_query.shape[1] // chips
    kv_cols = w_key.shape[1] // chips
    ff_cols = w_gate.shape[1] // (2 * chips)
    kv_heads = KV_HEADS // chips
    factor = HEAD ** (-0.5)

    def core_swap(a):
        return lax.ppermute(a, "core", [(0, 1), (1, 0)])

    def chip_xor(a, j):
        return lax.ppermute(a, "chip", [(i, i ^ j) for i in range(chips)])

    def pick(a, index, axis=0):
        return lax.dynamic_index_in_dim(a, index, axis, keepdims=False)

    def gather_chips(a, axis=0):
        return jnp.concatenate([a] + [chip_xor(a, j) for j in range(1, chips)], axis=axis)

    def scatter_chips(a):
        step = a.shape[0] // chips
        total = a[:step]
        for j in range(1, chips):
            total = total + chip_xor(a[j * step : (j + 1) * step].astype(bf16), j).astype(f32)
        return total

    def by_chip(pieces):
        stacked = jnp.stack(pieces)
        bit = 1
        while bit < chips:
            view = stacked.reshape((chips // (2 * bit), 2, bit) + stacked.shape[1:])
            flipped = jnp.flip(view, axis=1)
            stacked = jnp.where((chip & bit) != 0, flipped, view).reshape(stacked.shape)
            bit *= 2
        return stacked

    def exchange_chips(pack):
        pieces = [pick(pack, chip)]
        for j in range(1, chips):
            pieces.append(chip_xor(pick(pack, chip ^ j), j))
        return by_chip(pieces)

    def core_pair(mine, other, axis):
        first = core == 0
        return jnp.stack([jnp.where(first, mine, other), jnp.where(first, other, mine)], axis)

    def both_cores(a):
        return core_pair(a, core_swap(a), 0)

    def chip_slices(weights, cols):
        return jnp.stack(
            [
                jnp.concatenate([w[:, k * n : (k + 1) * n] for w, n in zip(weights, cols)], axis=1)
                for k in range(chips)
            ]
        )

    def tie(*values):
        return lax.optimization_barrier(values)

    def along_z(a, step):
        return lax.ppermute(a, "fsdp", [(i, (i + step) % rows_z) for i in range(rows_z)])

    def ring_first(a):
        return along_z(a, 1), along_z(a, -1)

    def ring_rest(a, right, left):
        found = {0: a, rows_z - 1: right, 1: left}
        for step in range(2, rows_z // 2 + 1):
            if 2 * step == rows_z:
                half = a.shape[-1] // 2
                low = along_z(right[..., :half], 1)
                high = along_z(left[..., half:], -1)
                found[step] = jnp.concatenate([low, high], axis=-1)
            else:
                right, left = along_z(right, 1), along_z(left, -1)
                found[rows_z - step], found[step] = right, left
        return jnp.stack([found[step] for step in range(rows_z)])

    def by_place(a):
        doubled = jnp.concatenate([a, a])
        return lax.dynamic_slice_in_dim(doubled, rows_z - place, rows_z, 0)

    def order_columns(along):
        cols = along.shape[-1]
        full = both_cores(along.reshape(rows_z, chips, d_rows, cols))
        return jnp.transpose(full, (2, 0, 1, 3, 4)).reshape(chips * 2 * rows_z * d_rows, cols)

    owner = (chip * 2 + core) * rows_z + place
    spot = chip * 2 + core
    gains = lax.dynamic_update_slice(
        jnp.zeros((2, width), f32),
        jnp.stack([attn_gain, mlp_gain]).astype(f32),
        (0, owner * d_rows),
    )
    marks = lax.dynamic_update_slice(
        jnp.zeros((4, chips * 2 * tok), f32),
        jnp.concatenate([positions[:, 0], segments[:, 0]]).astype(f32),
        (0, spot * tok),
    )
    table = jnp.concatenate([gains.reshape(-1), marks.reshape(-1)]).reshape(-1, 128)

    def sum_chips(a):
        bit = 1
        while bit < chips:
            a = a + chip_xor(a, bit)
            bit *= 2
        return a

    def sum_z(a):
        bit = 1
        while bit < rows_z:
            a = a + lax.ppermute(a, "fsdp", [(i, i ^ bit) for i in range(rows_z)])
            bit *= 2
        return a

    along_down = lax.all_gather(w_down, "fsdp", axis=0, tiled=True)
    pair = jnp.stack([block_input[:, 0], out_cotangent[:, 0]], axis=1)
    pair = jnp.concatenate([pick(pair, core), core_swap(pick(pair, 1 - core))], axis=1)
    pack_qkv = chip_slices((w_query, w_key, w_value), (q_cols, kv_cols, kv_cols))
    piece_qkv = exchange_chips(pack_qkv).reshape(-1, pack_qkv.shape[-1])
    out_right, out_left = ring_first(w_out)
    table = table + core_swap(table)
    pack_gu = jnp.stack(
        [
            jnp.concatenate([w[:, n * ff_cols : (n + 1) * ff_cols] for w in (w_gate, w_up)], axis=1)
            for n in range(2 * chips)
        ]
    ).reshape(chips, 2, d_rows, 2 * ff_cols)
    pair, piece_qkv, out_right, out_left, table, pack_gu = tie(
        pair, piece_qkv, out_right, out_left, table, pack_gu
    )

    x_low, dy_low = pair[0], pair[1]
    x_all = gather_chips(x_low)
    qkv_right, qkv_left = ring_first(piece_qkv)
    x_all, qkv_right, qkv_left, pack_gu, table = tie(x_all, qkv_right, qkv_left, pack_gu, table)

    piece_gu = exchange_chips(pack_gu)
    qkv_rel = ring_rest(piece_qkv, qkv_right, qkv_left)
    piece_gu, qkv_rel, table = tie(piece_gu, qkv_rel, table)
    piece_gu = core_pair(pick(piece_gu, core, 1), core_swap(pick(piece_gu, 1 - core, 1)), 1)
    along_gu = lax.all_gather(
        piece_gu.reshape(2 * chips * d_rows, 2 * ff_cols), "fsdp", axis=0, tiled=True
    )
    table = sum_chips(table).reshape(-1)
    w_qkv = order_columns(by_place(qkv_rel))
    w_qkv, table, piece_gu, out_right, out_left, dy_low = tie(
        w_qkv, table, piece_gu, out_right, out_left, dy_low
    )
    out_rel = ring_rest(w_out, out_right, out_left)
    out_w = both_cores(by_place(out_rel)).reshape(-1, width)
    gain_one, gain_two = sum_z(table[: 2 * width].reshape(2, width))
    marks = table[2 * width :].reshape(2, 2, chips, 2, tok)
    marks = pick(marks, core, 1)
    marks = jnp.where(core == 0, marks, jnp.flip(marks, axis=2)).reshape(2, chips, 2 * tok)
    marks_all = by_chip([marks[:, k] for k in range(chips)])
    marks_all = jnp.transpose(marks_all, (1, 0, 2)).reshape(2, chips * 2 * tok)
    own = x_low.shape[0]
    seq = x_all.shape[0]

    dy_all = gather_chips(dy_low)
    pos_all, seg_all = marks_all[0], marks_all[1]
    allowed = (seg_all[:, None] == seg_all[None, :]) & (pos_all[None, :] <= pos_all[:, None])
    cosine, sine = rope_tables(pos_all)
    x_full = x_all.astype(f32)
    h_one = (x_full * rms_scale(x_full) * gain_one).astype(bf16)
    qkv = mm(h_one, w_qkv)
    q_rot = rotate(qkv[:, :q_cols].reshape(seq, kv_heads * 2, HEAD), cosine, sine)
    q_rot = q_rot.astype(bf16).reshape(seq, kv_heads, 2, HEAD)
    k_rot = rotate(
        qkv[:, q_cols : q_cols + kv_cols].reshape(seq, kv_heads, HEAD), cosine, sine
    ).astype(bf16)
    value = qkv[:, q_cols + kv_cols :].astype(bf16).reshape(seq, kv_heads, HEAD)
    scores = jnp.einsum("sgrh,tgh->grst", q_rot, k_rot, preferred_element_type=f32) * factor
    scores = jnp.where(allowed, scores, -1e30)
    raised = jnp.exp(scores - jnp.max(scores, axis=-1, keepdims=True))
    soft = raised / jnp.sum(raised, axis=-1, keepdims=True)
    soft_low = soft.astype(bf16)
    mixed = jnp.einsum("grst,tgh->sgrh", soft_low, value, preferred_element_type=f32)
    mixed = mixed.astype(bf16).reshape(seq, q_cols)
    mixed, dy_all = tie(mixed, dy_all)
    x_own = x_low.astype(f32)
    middle = x_own + scatter_chips(mm(mixed, out_w))

    dy_both = jnp.concatenate([dy_all, core_swap(dy_all)])
    d_act = mm_nt(dy_both, along_down)
    middle, dy_both, d_act = tie(middle, dy_both, d_act)
    scale_two = rms_scale(middle)
    n_two = middle * scale_two
    h_two = gather_chips((n_two * gain_two).astype(bf16))
    h_both = jnp.concatenate([h_two, core_swap(h_two)])
    h_both, along_gu = tie(h_both, along_gu)
    w_gu = along_gu.reshape(rows_z, 2 * chips, d_rows, 2 * ff_cols)
    w_gu = jnp.transpose(w_gu, (1, 0, 2, 3)).reshape(width, 2 * ff_cols)
    gu = mm(h_both, w_gu)
    gate, up = gu[:, :ff_cols], gu[:, ff_cols:]
    sigma = jax.nn.sigmoid(gate)
    act = (gate * sigma * up).astype(bf16)
    d_gate = (d_act * up * sigma * (1.0 + gate * (1.0 - sigma))).astype(bf16)
    d_up = (d_act * gate * sigma).astype(bf16)
    d_gu = jnp.concatenate([d_gate, d_up], axis=1)
    g_down = mm_tn(act, dy_both).astype(bf16)
    g_down, d_gu, act = tie(g_down, d_gu, act)
    g_down = lax.psum_scatter(g_down, "fsdp", scatter_dimension=0, tiled=True)

    def give_partial(rows, weights, product):
        other = core_swap(product(rows[seq:], weights).astype(bf16)).astype(f32)
        return product(rows[:seq], weights) + other

    d_h_two = scatter_chips(give_partial(d_gu, w_gu, mm_nt))
    g_gu = mm_tn(h_both, d_gu).astype(bf16).reshape(2 * chips, rows_z, d_rows, 2 * ff_cols)
    g_gu = jnp.transpose(g_gu, (1, 0, 2, 3)).reshape(width, 2 * ff_cols)
    d_h_two, g_gu = tie(d_h_two, g_gu)
    g_gu = lax.psum_scatter(g_gu, "fsdp", scatter_dimension=0, tiled=True)

    dy_own = dy_low.astype(f32)
    gain_two_part = jnp.sum(d_h_two * n_two, axis=0)
    d_middle = dy_own + norm_back(d_h_two * gain_two, n_two, scale_two)
    branch = gather_chips(d_middle.astype(bf16))
    partial = give_partial(act, along_down, mm)
    branch, partial = tie(branch, partial)
    result = (middle + scatter_chips(partial)).astype(bf16)

    g_out = mm_tn(mixed, branch).astype(bf16)
    g_out = g_out.reshape(2, g_out.shape[0] // 2, g_out.shape[1])
    g_out = pick(g_out, core) + core_swap(pick(g_out, 1 - core))
    d_mixed = mm_nt(branch, out_w).astype(bf16).reshape(seq, kv_heads, 2, HEAD)
    d_soft = jnp.einsum("sgrh,tgh->grst", d_mixed, value, preferred_element_type=f32)
    d_value = jnp.einsum("grst,sgrh->tgh", soft_low, d_mixed, preferred_element_type=f32)
    inner = jnp.sum(soft * d_soft, axis=-1, keepdims=True)
    d_scores = (soft * (d_soft - inner)).astype(bf16)
    d_q = jnp.einsum("grst,tgh->sgrh", d_scores, k_rot, preferred_element_type=f32) * factor
    d_k = jnp.einsum("grst,sgrh->tgh", d_scores, q_rot, preferred_element_type=f32) * factor
    d_q = unrotate(d_q.reshape(seq, kv_heads * 2, HEAD), cosine, sine)
    d_k = unrotate(d_k, cosine, sine)
    d_qkv = jnp.concatenate(
        [
            d_q.reshape(seq, q_cols).astype(bf16),
            d_k.reshape(seq, kv_cols).astype(bf16),
            d_value.reshape(seq, kv_cols).astype(bf16),
        ],
        axis=1,
    )
    d_qkv, result, g_out = tie(d_qkv, result, g_out)
    cols_qkv = d_qkv.shape[1]
    g_qkv = mm_tn(h_one, d_qkv).astype(bf16).reshape(chips, 2, rows_z, d_rows, cols_qkv)
    g_qkv = pick(g_qkv, core, 1) + core_swap(pick(g_qkv, 1 - core, 1))
    g_qkv = jnp.transpose(g_qkv, (1, 0, 2, 3)).reshape(rows_z, chips * d_rows, cols_qkv)
    folds = width // cols_qkv
    g_out = g_out.reshape(rows_z, d_rows, width)
    g_rest = [g_out[:, :, k * cols_qkv : (k + 1) * cols_qkv] for k in range(folds)]
    g_rest = jnp.concatenate([g_qkv] + g_rest, axis=1)
    g_rest, d_qkv = tie(g_rest.reshape(-1, cols_qkv), d_qkv)
    g_rest = lax.psum_scatter(g_rest, "fsdp", scatter_dimension=0, tiled=True)
    d_h_one = scatter_chips(mm_nt(d_qkv, w_qkv))
    scale_one = rms_scale(x_own)
    n_one = x_own * scale_one
    gain_one_part = jnp.sum(d_h_one * n_one, axis=0)
    d_input = (d_middle + norm_back(d_h_one * gain_one, n_one, scale_one)).astype(bf16)

    def give_back(a):
        mine, theirs = a[:tok], core_swap(a[tok:])
        first = core == 0
        return jnp.stack([jnp.where(first, mine, theirs), jnp.where(first, theirs, mine)])[:, None]

    def spread(grad, start, cols):
        part = grad[:, :, start : start + cols].astype(f32)
        return jnp.transpose(part, (1, 0, 2)).reshape(d_rows, chips * cols)

    def spread_ff(grad):
        grad = jnp.transpose(grad.astype(f32), (2, 0, 1, 3))
        return grad.reshape(d_rows, 2 * chips * ff_cols)

    g_down = g_down.astype(f32)
    g_gu = g_gu.reshape(chips, 2, d_rows, 2 * ff_cols)
    g_gu = core_pair(pick(g_gu, core, 1), core_swap(pick(g_gu, 1 - core, 1)), 1)
    g_gu = exchange_chips(g_gu)
    g_gate, g_up = spread_ff(g_gu[..., :ff_cols]), spread_ff(g_gu[..., ff_cols:])
    gain_parts = jnp.stack([gain_one_part, gain_two_part])
    gain_parts = sum_z(sum_chips(gain_parts + core_swap(gain_parts)))
    gain_parts = lax.dynamic_slice_in_dim(gain_parts, owner * d_rows, d_rows, 1)
    result, d_input = give_back(result), give_back(d_input)
    g_rest, g_gate, g_up, g_down, gain_parts, result, d_input = tie(
        g_rest, g_gate, g_up, g_down, gain_parts, result, d_input
    )
    g_qkv = exchange_chips(g_rest[: chips * d_rows].reshape(chips, d_rows, cols_qkv))
    g_out = g_rest[chips * d_rows :].reshape(folds, d_rows, cols_qkv)
    g_out = jnp.transpose(g_out, (1, 0, 2)).reshape(d_rows, width).astype(f32)
    return (
        result,
        d_input,
        gain_parts[0],
        spread(g_qkv, 0, q_cols),
        spread(g_qkv, q_cols, kv_cols),
        spread(g_qkv, q_cols + kv_cols, kv_cols),
        g_out,
        gain_parts[1],
        g_gate,
        g_up,
        g_down,
    )


def solution(mesh):
    ctx, fsdp = mesh.shape["ctx"], mesh.shape["fsdp"]
    split = Mesh(mesh.devices.reshape(ctx // 2, 2, fsdp), ("chip", "core", "fsdp"))
    ctx_axes = ("chip", "core")
    all_axes = ("chip", "core", "fsdp")
    tokens = P(None, "fsdp", ctx_axes, None)
    marks = P(None, "fsdp", ctx_axes)
    vector, matrix = P(all_axes), P(all_axes, None)
    return jax.shard_map(
        on_device,
        mesh=split,
        in_specs=(
            tokens, marks, marks, tokens, vector, matrix, matrix, matrix, matrix,
            vector, matrix, matrix, matrix,
        ),
        out_specs=(
            tokens, tokens, vector, matrix, matrix, matrix, matrix, vector,
            matrix, matrix, matrix,
        ),
        check_vma=False,
    )
```

```python
import math

import jax
import jax.numpy as jnp
from jax import lax
from jax.sharding import Mesh, PartitionSpec as P

HEADS = 16
KV_HEADS = 8
HEAD = 96
EPS = 1e-05
THETA = 100000.0
f32 = jnp.float32
bf16 = jnp.bfloat16


def rope_tables(position_ids):
    half = HEAD // 2
    ladder = jnp.arange(half).astype(f32) * (2.0 / HEAD)
    inverse = jnp.exp(-math.log(THETA) * ladder)
    angles = position_ids.astype(f32)[:, None] * inverse[None, :]
    return jnp.cos(angles)[:, None, :], jnp.sin(angles)[:, None, :]


def rotate(vectors, cosine, sine):
    half = HEAD // 2
    a, b = vectors[..., :half], vectors[..., half:]
    return jnp.concatenate([a * cosine - b * sine, b * cosine + a * sine], axis=-1)


def unrotate(grads, cosine, sine):
    half = HEAD // 2
    a, b = grads[..., :half], grads[..., half:]
    return jnp.concatenate([a * cosine + b * sine, b * cosine - a * sine], axis=-1)


def rms_scale(values):
    return lax.rsqrt(jnp.mean(values * values, axis=-1, keepdims=True) + EPS)


def norm_back(grad, normed, scale):
    return scale * (grad - normed * jnp.mean(grad * normed, axis=-1, keepdims=True))


def mm(a, b):
    return jnp.dot(a, b, preferred_element_type=f32)


def mm_tn(a, b):
    return jnp.einsum("td,te->de", a, b, preferred_element_type=f32)


def mm_nt(a, b):
    return jnp.einsum("te,de->td", a, b, preferred_element_type=f32)


def on_device(
    block_input,
    positions,
    segments,
    out_cotangent,
    attn_gain,
    w_query,
    w_key,
    w_value,
    w_out,
    mlp_gain,
    w_gate,
    w_up,
    w_down,
):
    chips = lax.axis_size("chip")
    rows_z = lax.axis_size("fsdp")
    chip = lax.axis_index("chip")
    core = lax.axis_index("core")
    place = lax.axis_index("fsdp")
    tok = block_input.shape[2]
    width = block_input.shape[3]
    d_rows = w_query.shape[0]
    q_cols = w_query.shape[1] // chips
    kv_cols = w_key.shape[1] // chips
    ff_cols = w_gate.shape[1] // (2 * chips)
    kv_heads = KV_HEADS // chips
    factor = HEAD ** (-0.5)

    def core_swap(a):
        return lax.ppermute(a, "core", [(0, 1), (1, 0)])

    def chip_xor(a, j):
        return lax.ppermute(a, "chip", [(i, i ^ j) for i in range(chips)])

    def pick(a, index, axis=0):
        return lax.dynamic_index_in_dim(a, index, axis, keepdims=False)

    def gather_chips(a, axis=0):
        return jnp.concatenate([a] + [chip_xor(a, j) for j in range(1, chips)], axis=axis)

    def scatter_chips(a):
        step = a.shape[0] // chips
        total = a[:step]
        for j in range(1, chips):
            total = total + chip_xor(a[j * step : (j + 1) * step].astype(bf16), j).astype(f32)
        return total

    def by_chip(pieces):
        stacked = jnp.stack(pieces)
        bit = 1
        while bit < chips:
            view = stacked.reshape((chips // (2 * bit), 2, bit) + stacked.shape[1:])
            flipped = jnp.flip(view, axis=1)
            stacked = jnp.where((chip & bit) != 0, flipped, view).reshape(stacked.shape)
            bit *= 2
        return stacked

    def exchange_chips(pack):
        pieces = [pick(pack, chip)]
        for j in range(1, chips):
            pieces.append(chip_xor(pick(pack, chip ^ j), j))
        return by_chip(pieces)

    def core_pair(mine, other, axis):
        first = core == 0
        return jnp.stack([jnp.where(first, mine, other), jnp.where(first, other, mine)], axis)

    def both_cores(a):
        return core_pair(a, core_swap(a), 0)

    def chip_slices(weights, cols):
        return jnp.stack(
            [
                jnp.concatenate([w[:, k * n : (k + 1) * n] for w, n in zip(weights, cols)], axis=1)
                for k in range(chips)
            ]
        )

    def tie(*values):
        return lax.optimization_barrier(values)

    def along_z(a, step):
        return lax.ppermute(a, "fsdp", [(i, (i + step) % rows_z) for i in range(rows_z)])

    def ring_first(a):
        return along_z(a, 1), along_z(a, -1)

    def ring_rest(a, right, left):
        found = [(a, 0, 0), (right, -1, 0), (left, 1, 0)]
        for step in range(2, rows_z // 2 + 1):
            if 2 * step == rows_z:
                half = a.shape[-1] // 2
                found.append((along_z(right[..., :half], 1), -step, 0))
                found.append((along_z(left[..., half:], -1), step, half))
            else:
                right, left = along_z(right, 1), along_z(left, -1)
                found += [(right, -step, 0), (left, step, 0)]
        return found

    def assemble(found, groups):
        rows, cols = found[0][0].shape
        whole = jnp.zeros((groups, rows_z, rows // groups, cols), bf16)
        for piece, offset, column in found:
            piece = piece.reshape(groups, 1, rows // groups, piece.shape[-1])
            index = lax.rem(place + offset + rows_z, rows_z)
            whole = lax.dynamic_update_slice(whole, piece, (0, index, 0, column))
        return whole

    owner = (chip * 2 + core) * rows_z + place
    gains = lax.all_gather(
        jnp.stack([attn_gain, mlp_gain]), ("chip", "core", "fsdp"), axis=1, tiled=True
    )
    marks = jnp.stack([positions[:, 0], segments[:, 0]])
    marks = lax.all_gather(marks, ("chip", "core"), axis=0)

    def sum_chips(a):
        bit = 1
        while bit < chips:
            a = a + chip_xor(a, bit)
            bit *= 2
        return a

    def sum_z(a):
        bit = 1
        while bit < rows_z:
            a = a + lax.ppermute(a, "fsdp", [(i, i ^ bit) for i in range(rows_z)])
            bit *= 2
        return a

    down_right, down_left = ring_first(w_down)
    pair = jnp.stack([block_input[:, 0], out_cotangent[:, 0]], axis=1)
    pair = jnp.concatenate([pick(pair, core), core_swap(pick(pair, 1 - core))], axis=1)
    pack_qkv = chip_slices((w_query, w_key, w_value), (q_cols, kv_cols, kv_cols))
    piece_qkv = exchange_chips(pack_qkv).reshape(-1, pack_qkv.shape[-1])
    pack_gu = jnp.stack(
        [
            jnp.concatenate([w[:, n * ff_cols : (n + 1) * ff_cols] for w in (w_gate, w_up)], axis=1)
            for n in range(2 * chips)
        ]
    ).reshape(chips, 2, d_rows, 2 * ff_cols)
    pair, piece_qkv, pack_gu = tie(pair, piece_qkv, pack_gu)

    x_low, dy_low = pair[0], pair[1]
    x_all = gather_chips(x_low)
    piece_qkv, down_right, down_left = tie(piece_qkv, down_right, down_left)
    qkv_right, qkv_left = ring_first(piece_qkv)
    x_all, qkv_right, qkv_left, pack_gu = tie(x_all, qkv_right, qkv_left, pack_gu)

    piece_gu = exchange_chips(pack_gu)
    found_qkv = ring_rest(piece_qkv, qkv_right, qkv_left)
    *late, piece_gu, w_out = tie(*[f[0] for f in found_qkv], piece_gu, w_out)
    found_qkv = [(piece,) + f[1:] for piece, f in zip(late, found_qkv)]
    out_right, out_left = ring_first(w_out)
    piece_gu = core_pair(pick(piece_gu, core, 1), core_swap(pick(piece_gu, 1 - core, 1)), 1)
    piece_gu = piece_gu.reshape(2 * chips * d_rows, 2 * ff_cols)
    w_qkv = assemble(found_qkv, chips)
    w_qkv = core_pair(w_qkv, core_swap(w_qkv), 1).reshape(width, -1)
    w_qkv, piece_gu, out_right, out_left, dy_low = tie(w_qkv, piece_gu, out_right, out_left, dy_low)
    gu_right, gu_left = ring_first(piece_gu)
    gain_one, gain_two = gains.astype(f32)
    marks = pick(marks.reshape(chips, 2, 2, 2, tok), core, 3).astype(f32)
    marks = jnp.where(core == 0, marks, jnp.flip(marks, axis=1))
    marks_all = by_chip([marks[k] for k in range(chips)])
    marks_all = jnp.transpose(marks_all, (2, 0, 1, 3)).reshape(2, chips * 2 * tok)
    own = x_low.shape[0]
    seq = x_all.shape[0]

    dy_all = gather_chips(dy_low)
    pos_all, seg_all = marks_all[0], marks_all[1]
    allowed = (seg_all[:, None] == seg_all[None, :]) & (pos_all[None, :] <= pos_all[:, None])
    cosine, sine = rope_tables(pos_all)
    x_full = x_all.astype(f32)
    h_one = (x_full * rms_scale(x_full) * gain_one).astype(bf16)
    qkv = mm(h_one, w_qkv)
    q_rot = rotate(qkv[:, :q_cols].reshape(seq, kv_heads * 2, HEAD), cosine, sine)
    q_rot = q_rot.astype(bf16).reshape(seq, kv_heads, 2, HEAD)
    k_rot = rotate(
        qkv[:, q_cols : q_cols + kv_cols].reshape(seq, kv_heads, HEAD), cosine, sine
    ).astype(bf16)
    value = qkv[:, q_cols + kv_cols :].astype(bf16).reshape(seq, kv_heads, HEAD)
    q_rot, dy_all, out_right, out_left = tie(q_rot, dy_all, out_right, out_left)
    out_w = assemble(ring_rest(w_out, out_right, out_left), 1).reshape(rows_z * d_rows, width)
    out_w = both_cores(out_w).reshape(-1, width)
    scores = jnp.einsum("sgrh,tgh->grst", q_rot, k_rot, preferred_element_type=f32) * factor
    scores = jnp.where(allowed, scores, -1e30)
    raised = jnp.exp(scores - jnp.max(scores, axis=-1, keepdims=True))
    soft = raised / jnp.sum(raised, axis=-1, keepdims=True)
    soft_low, out_w, down_right, down_left = tie(
        soft.astype(bf16), out_w, down_right, down_left
    )
    found_down = ring_rest(w_down, down_right, down_left)
    mixed = jnp.einsum("grst,tgh->sgrh", soft_low, value, preferred_element_type=f32)
    mixed = mixed.astype(bf16).reshape(seq, q_cols)
    mixed, gu_right, gu_left, *late = tie(mixed, gu_right, gu_left, *[f[0] for f in found_down])
    found_down = [(piece,) + f[1:] for piece, f in zip(late, found_down)]
    found_gu = ring_rest(piece_gu, gu_right, gu_left)
    x_own = x_low.astype(f32)
    middle = x_own + scatter_chips(mm(mixed, out_w))

    dy_both = jnp.concatenate([dy_all, core_swap(dy_all)])
    down_w = assemble(found_down, 1).reshape(-1, width)
    d_act = mm_nt(dy_both, down_w)
    middle, dy_both, d_act, *late = tie(middle, dy_both, d_act, *[f[0] for f in found_gu])
    found_gu = [(piece,) + f[1:] for piece, f in zip(late, found_gu)]
    scale_two = rms_scale(middle)
    n_two = middle * scale_two
    h_two = gather_chips((n_two * gain_two).astype(bf16))
    h_both = jnp.concatenate([h_two, core_swap(h_two)])
    w_gu = assemble(found_gu, 2 * chips).reshape(width, 2 * ff_cols)
    gu = mm(h_both, w_gu)
    gate, up = gu[:, :ff_cols], gu[:, ff_cols:]
    sigma = jax.nn.sigmoid(gate)
    act = (gate * sigma * up).astype(bf16)
    d_gate = (d_act * up * sigma * (1.0 + gate * (1.0 - sigma))).astype(bf16)
    d_up = (d_act * gate * sigma).astype(bf16)
    d_gu = jnp.concatenate([d_gate, d_up], axis=1)
    g_down = mm_tn(act, dy_both).astype(bf16)
    g_down, d_gu, act = tie(g_down, d_gu, act)
    g_down = lax.psum_scatter(g_down, "fsdp", scatter_dimension=0, tiled=True)

    def give_partial(rows, weights, product):
        other = core_swap(product(rows[seq:], weights).astype(bf16)).astype(f32)
        return product(rows[:seq], weights) + other

    d_h_two = scatter_chips(give_partial(d_gu, w_gu, mm_nt))
    g_gu = mm_tn(h_both, d_gu).astype(bf16).reshape(2 * chips, rows_z, d_rows, 2 * ff_cols)
    g_gu = jnp.transpose(g_gu, (1, 0, 2, 3)).reshape(width, 2 * ff_cols)
    d_h_two, g_gu = tie(d_h_two, g_gu)
    g_gu = lax.psum_scatter(g_gu, "fsdp", scatter_dimension=0, tiled=True)

    dy_own = dy_low.astype(f32)
    gain_two_part = jnp.sum(d_h_two * n_two, axis=0)
    d_middle = dy_own + norm_back(d_h_two * gain_two, n_two, scale_two)
    branch = gather_chips(d_middle.astype(bf16))
    partial = give_partial(act, down_w, mm)
    branch, partial = tie(branch, partial)
    result = (middle + scatter_chips(partial)).astype(bf16)

    g_out = mm_tn(mixed, branch).astype(bf16)
    g_out = g_out.reshape(2, g_out.shape[0] // 2, g_out.shape[1])
    g_out = pick(g_out, core) + core_swap(pick(g_out, 1 - core))
    d_mixed = mm_nt(branch, out_w).astype(bf16).reshape(seq, kv_heads, 2, HEAD)
    d_soft = jnp.einsum("sgrh,tgh->grst", d_mixed, value, preferred_element_type=f32)
    d_value = jnp.einsum("grst,sgrh->tgh", soft_low, d_mixed, preferred_element_type=f32)
    inner = jnp.sum(soft * d_soft, axis=-1, keepdims=True)
    d_scores = (soft * (d_soft - inner)).astype(bf16)
    d_q = jnp.einsum("grst,tgh->sgrh", d_scores, k_rot, preferred_element_type=f32) * factor
    d_k = jnp.einsum("grst,sgrh->tgh", d_scores, q_rot, preferred_element_type=f32) * factor
    d_q = unrotate(d_q.reshape(seq, kv_heads * 2, HEAD), cosine, sine)
    d_k = unrotate(d_k, cosine, sine)
    d_qkv = jnp.concatenate(
        [
            d_q.reshape(seq, q_cols).astype(bf16),
            d_k.reshape(seq, kv_cols).astype(bf16),
            d_value.reshape(seq, kv_cols).astype(bf16),
        ],
        axis=1,
    )
    d_qkv, result, g_out = tie(d_qkv, result, g_out)
    cols_qkv = d_qkv.shape[1]
    g_qkv = mm_tn(h_one, d_qkv).astype(bf16).reshape(chips, 2, rows_z, d_rows, cols_qkv)
    g_qkv = pick(g_qkv, core, 1) + core_swap(pick(g_qkv, 1 - core, 1))
    g_qkv = jnp.transpose(g_qkv, (1, 0, 2, 3)).reshape(rows_z, chips * d_rows, cols_qkv)
    folds = width // cols_qkv
    g_out = g_out.reshape(rows_z, d_rows, width)
    g_rest = [g_out[:, :, k * cols_qkv : (k + 1) * cols_qkv] for k in range(folds)]
    g_rest = jnp.concatenate([g_qkv] + g_rest, axis=1)
    g_rest, d_qkv = tie(g_rest.reshape(-1, cols_qkv), d_qkv)
    g_rest = lax.psum_scatter(g_rest, "fsdp", scatter_dimension=0, tiled=True)
    d_h_one = scatter_chips(mm_nt(d_qkv, w_qkv))
    scale_one = rms_scale(x_own)
    n_one = x_own * scale_one
    gain_one_part = jnp.sum(d_h_one * n_one, axis=0)
    d_input = (d_middle + norm_back(d_h_one * gain_one, n_one, scale_one)).astype(bf16)

    def give_back(a):
        mine, theirs = a[:tok], core_swap(a[tok:])
        first = core == 0
        return jnp.stack([jnp.where(first, mine, theirs), jnp.where(first, theirs, mine)])[:, None]

    def spread(grad, start, cols):
        part = grad[:, :, start : start + cols].astype(f32)
        return jnp.transpose(part, (1, 0, 2)).reshape(d_rows, chips * cols)

    def spread_ff(grad):
        grad = jnp.transpose(grad.astype(f32), (2, 0, 1, 3))
        return grad.reshape(d_rows, 2 * chips * ff_cols)

    g_down = g_down.astype(f32)
    g_gu = g_gu.reshape(chips, 2, d_rows, 2 * ff_cols)
    g_gu = core_pair(pick(g_gu, core, 1), core_swap(pick(g_gu, 1 - core, 1)), 1)
    g_gu = exchange_chips(g_gu)
    g_gate, g_up = spread_ff(g_gu[..., :ff_cols]), spread_ff(g_gu[..., ff_cols:])
    gain_parts = jnp.stack([gain_one_part, gain_two_part])
    gain_parts = sum_z(sum_chips(gain_parts + core_swap(gain_parts)))
    gain_parts = lax.dynamic_slice_in_dim(gain_parts, owner * d_rows, d_rows, 1)
    result, d_input = give_back(result), give_back(d_input)
    g_rest, g_gate, g_up, g_down, gain_parts, result, d_input = tie(
        g_rest, g_gate, g_up, g_down, gain_parts, result, d_input
    )
    g_qkv = exchange_chips(g_rest[: chips * d_rows].reshape(chips, d_rows, cols_qkv))
    g_out = g_rest[chips * d_rows :].reshape(folds, d_rows, cols_qkv)
    g_out = jnp.transpose(g_out, (1, 0, 2)).reshape(d_rows, width).astype(f32)
    return (
        result,
        d_input,
        gain_parts[0],
        spread(g_qkv, 0, q_cols),
        spread(g_qkv, q_cols, kv_cols),
        spread(g_qkv, q_cols + kv_cols, kv_cols),
        g_out,
        gain_parts[1],
        g_gate,
        g_up,
        g_down,
    )


def solution(mesh):
    ctx, fsdp = mesh.shape["ctx"], mesh.shape["fsdp"]
    split = Mesh(mesh.devices.reshape(ctx // 2, 2, fsdp), ("chip", "core", "fsdp"))
    ctx_axes = ("chip", "core")
    all_axes = ("chip", "core", "fsdp")
    tokens = P(None, "fsdp", ctx_axes, None)
    marks = P(None, "fsdp", ctx_axes)
    vector, matrix = P(all_axes), P(all_axes, None)
    return jax.shard_map(
        on_device,
        mesh=split,
        in_specs=(
            tokens, marks, marks, tokens, vector, matrix, matrix, matrix, matrix,
            vector, matrix, matrix, matrix,
        ),
        out_specs=(
            tokens, tokens, vector, matrix, matrix, matrix, matrix, vector,
            matrix, matrix, matrix,
        ),
        check_vma=False,
    )
```

```python
import math

import jax
import jax.numpy as jnp
from jax import lax
from jax.sharding import Mesh, PartitionSpec as P

HEADS = 16
KV_HEADS = 8
HEAD = 96
EPS = 1e-05
THETA = 100000.0
f32 = jnp.float32
bf16 = jnp.bfloat16


def rope_tables(position_ids):
    half = HEAD // 2
    ladder = jnp.arange(half).astype(f32) * (2.0 / HEAD)
    inverse = jnp.exp(-math.log(THETA) * ladder)
    angles = position_ids.astype(f32)[:, None] * inverse[None, :]
    return jnp.cos(angles)[:, None, :], jnp.sin(angles)[:, None, :]


def rotate(vectors, cosine, sine):
    half = HEAD // 2
    a, b = vectors[..., :half], vectors[..., half:]
    return jnp.concatenate([a * cosine - b * sine, b * cosine + a * sine], axis=-1)


def unrotate(grads, cosine, sine):
    half = HEAD // 2
    a, b = grads[..., :half], grads[..., half:]
    return jnp.concatenate([a * cosine + b * sine, b * cosine - a * sine], axis=-1)


def rms_scale(values):
    return lax.rsqrt(jnp.mean(values * values, axis=-1, keepdims=True) + EPS)


def norm_back(grad, normed, scale):
    return scale * (grad - normed * jnp.mean(grad * normed, axis=-1, keepdims=True))


def mm(a, b):
    return jnp.dot(a, b, preferred_element_type=f32)


def mm_tn(a, b):
    return jnp.einsum("td,te->de", a, b, preferred_element_type=f32)


def mm_nt(a, b):
    return jnp.einsum("te,de->td", a, b, preferred_element_type=f32)


def on_device(
    block_input,
    positions,
    segments,
    out_cotangent,
    attn_gain,
    w_query,
    w_key,
    w_value,
    w_out,
    mlp_gain,
    w_gate,
    w_up,
    w_down,
):
    chips = lax.axis_size("chip")
    rows_z = lax.axis_size("fsdp")
    chip = lax.axis_index("chip")
    core = lax.axis_index("core")
    place = lax.axis_index("fsdp")
    tok = block_input.shape[2]
    width = block_input.shape[3]
    d_rows = w_query.shape[0]
    q_cols = w_query.shape[1] // chips
    kv_cols = w_key.shape[1] // chips
    ff_cols = w_gate.shape[1] // (2 * chips)
    kv_heads = KV_HEADS // chips
    factor = HEAD ** (-0.5)

    def core_swap(a):
        return lax.ppermute(a, "core", [(0, 1), (1, 0)])

    def chip_xor(a, j):
        return lax.ppermute(a, "chip", [(i, i ^ j) for i in range(chips)])

    def pick(a, index, axis=0):
        return lax.dynamic_index_in_dim(a, index, axis, keepdims=False)

    def gather_chips(a, axis=0):
        return jnp.concatenate([a] + [chip_xor(a, j) for j in range(1, chips)], axis=axis)

    def scatter_chips(a):
        step = a.shape[0] // chips
        total = a[:step]
        for j in range(1, chips):
            total = total + chip_xor(a[j * step : (j + 1) * step].astype(bf16), j).astype(f32)
        return total

    def by_chip(pieces):
        stacked = jnp.stack(pieces)
        bit = 1
        while bit < chips:
            view = stacked.reshape((chips // (2 * bit), 2, bit) + stacked.shape[1:])
            flipped = jnp.flip(view, axis=1)
            stacked = jnp.where((chip & bit) != 0, flipped, view).reshape(stacked.shape)
            bit *= 2
        return stacked

    def exchange_chips(pack):
        pieces = [pick(pack, chip)]
        for j in range(1, chips):
            pieces.append(chip_xor(pick(pack, chip ^ j), j))
        return by_chip(pieces)

    def core_pair(mine, other, axis):
        first = core == 0
        return jnp.stack([jnp.where(first, mine, other), jnp.where(first, other, mine)], axis)

    def both_cores(a):
        return core_pair(a, core_swap(a), 0)

    def chip_slices(weights, cols):
        return jnp.stack(
            [
                jnp.concatenate([w[:, k * n : (k + 1) * n] for w, n in zip(weights, cols)], axis=1)
                for k in range(chips)
            ]
        )

    def tie(*values):
        return lax.optimization_barrier(values)

    def along_z(a, step):
        return lax.ppermute(a, "fsdp", [(i, (i + step) % rows_z) for i in range(rows_z)])

    def ring_first(a):
        return along_z(a, 1), along_z(a, -1)

    def second_right(right):
        return along_z(right[..., : right.shape[-1] // 2] if rows_z == 4 else right, 1)

    def ring_rest(a, right, left, following=None):
        found = [(a, 0, 0), (right, -1, 0), (left, 1, 0)]
        for step in range(2, rows_z // 2 + 1):
            if 2 * step == rows_z:
                half = a.shape[-1] // 2
                low = along_z(right[..., :half], 1) if following is None else following
                found.append((low, -step, 0))
                found.append((along_z(left[..., half:], -1), step, half))
            else:
                right = along_z(right, 1) if following is None else following
                left = along_z(left, -1)
                found += [(right, -step, 0), (left, step, 0)]
            following = None
        return found

    windows = [2 + (rows_z - 1) * w // 3 for w in range(4)]

    def part(a, index, start):
        index = lax.rem(index + 2 * rows_z, rows_z)
        size = (a.shape[0], 1, a.shape[2], a.shape[3] // 2)
        return lax.dynamic_slice(a, (0, index, 0, start), size)

    def scatter_begin(a):
        return part(a, place - 1, 0), part(a, place + 1, a.shape[3] // 2)

    def scatter_window(a, sums, window):
        low, high = sums
        for step in range(windows[window], windows[window + 1]):
            low = along_z(low, 1) + part(a, place - step, 0)
            high = along_z(high, -1) + part(a, place + step, a.shape[3] // 2)
        return low, high

    def assemble(found, groups):
        rows, cols = found[0][0].shape
        whole = jnp.zeros((groups, rows_z, rows // groups, cols), bf16)
        for piece, offset, column in found:
            piece = piece.reshape(groups, 1, rows // groups, piece.shape[-1])
            index = lax.rem(place + offset + rows_z, rows_z)
            whole = lax.dynamic_update_slice(whole, piece, (0, index, 0, column))
        return whole

    owner = (chip * 2 + core) * rows_z + place
    spot = chip * 2 + core
    spots = chips * 2
    gains = lax.dynamic_update_slice(
        jnp.zeros((2, width), f32),
        jnp.stack([attn_gain, mlp_gain]).astype(f32),
        (0, owner * d_rows),
    )
    marks = lax.dynamic_update_slice(
        jnp.zeros((4, spots * tok), f32),
        jnp.concatenate([positions[:, 0], segments[:, 0]]).astype(f32),
        (0, spot * tok),
    )
    table = jnp.concatenate([gains.reshape(-1), marks.reshape(-1)]).reshape(-1, 128)

    def sum_chips(a):
        bit = 1
        while bit < chips:
            a = a + chip_xor(a, bit)
            bit *= 2
        return a

    def sum_z(a):
        bit = 1
        while bit < rows_z:
            a = a + lax.ppermute(a, "fsdp", [(i, i ^ bit) for i in range(rows_z)])
            bit *= 2
        return a

    out_right, out_left = ring_first(w_out)
    along_down = lax.all_gather(w_down, "fsdp", axis=0, tiled=True)
    pack_qkv = chip_slices((w_query, w_key, w_value), (q_cols, kv_cols, kv_cols))
    piece_qkv = exchange_chips(pack_qkv).reshape(-1, pack_qkv.shape[-1])
    pair = jnp.stack([block_input[:, 0], out_cotangent[:, 0]], axis=1)
    pair = jnp.concatenate([pick(pair, core), core_swap(pick(pair, 1 - core))], axis=1)
    table = table + core_swap(table)
    pair, piece_qkv, table = tie(pair, piece_qkv, table)
    x_low, dy_low = pair[0], pair[1]

    x_all = gather_chips(x_low)
    qkv_right, qkv_left = ring_first(piece_qkv)
    pack_gu = jnp.stack(
        [
            jnp.concatenate([w[:, n * ff_cols : (n + 1) * ff_cols] for w in (w_gate, w_up)], axis=1)
            for n in range(2 * chips)
        ]
    ).reshape(chips, 2, d_rows, 2 * ff_cols)
    table = sum_chips(table)
    qkv_right, qkv_left, pack_gu, out_right, out_left, table = tie(
        qkv_right, qkv_left, pack_gu, out_right, out_left, table
    )
    gains = sum_z(table.reshape(-1)[: 2 * width].reshape(2, width))
    marks = pick(table.reshape(-1)[2 * width :].reshape(2, 2, spots, tok), core, 1)
    marks = jnp.concatenate(
        [pick(marks, (chip ^ k) * 2 + (core ^ c), 1) for k in range(chips) for c in range(2)],
        axis=1,
    )
    found_qkv = ring_rest(piece_qkv, qkv_right, qkv_left)
    x_all, pack_gu, out_right, out_left, gains, marks, *late = tie(
        x_all, pack_gu, out_right, out_left, gains, marks, *[f[0] for f in found_qkv]
    )
    found_qkv = [(piece,) + f[1:] for piece, f in zip(late, found_qkv)]

    piece_gu = exchange_chips(pack_gu)
    found_out = ring_rest(w_out, out_right, out_left)
    w_qkv = assemble(found_qkv, chips)
    w_qkv = core_pair(w_qkv, core_swap(w_qkv), 1).reshape(width, -1)
    piece_gu = core_pair(pick(piece_gu, core, 1), core_swap(pick(piece_gu, 1 - core, 1)), 1)
    piece_gu = piece_gu.reshape(2 * chips * d_rows, 2 * ff_cols)
    gain_one, gain_two = gains
    pos_all, seg_all = marks
    allowed = (seg_all[:, None] == seg_all[None, :]) & (pos_all[None, :] <= pos_all[:, None])
    cosine, sine = rope_tables(pos_all)
    w_qkv, piece_gu, dy_low, cosine, sine, allowed, *late = tie(
        w_qkv, piece_gu, dy_low, cosine, sine, allowed, *[f[0] for f in found_out]
    )
    found_out = [(piece,) + f[1:] for piece, f in zip(late, found_out)]
    gu_right = along_z(piece_gu, 1)
    own = x_low.shape[0]
    seq = x_all.shape[0]

    dy_all = gather_chips(dy_low)
    x_full = x_all.astype(f32)
    h_one = (x_full * rms_scale(x_full) * gain_one).astype(bf16)
    qkv = mm(h_one, w_qkv)
    q_rot = rotate(qkv[:, :q_cols].reshape(seq, kv_heads * 2, HEAD), cosine, sine)
    q_rot = q_rot.astype(bf16).reshape(seq, kv_heads, 2, HEAD)
    k_rot = rotate(
        qkv[:, q_cols : q_cols + kv_cols].reshape(seq, kv_heads, HEAD), cosine, sine
    ).astype(bf16)
    value = qkv[:, q_cols + kv_cols :].astype(bf16).reshape(seq, kv_heads, HEAD)
    out_w = assemble(found_out, 1).reshape(rows_z * d_rows, width)
    out_w = both_cores(out_w).reshape(-1, width)
    scores = jnp.einsum("sgrh,tgh->grst", q_rot, k_rot, preferred_element_type=f32) * factor
    scores = jnp.where(allowed, scores, -1e30)
    raised = jnp.exp(scores - jnp.max(scores, axis=-1, keepdims=True))
    soft = raised / jnp.sum(raised, axis=-1, keepdims=True)
    soft_low = soft.astype(bf16)
    mixed = jnp.einsum("grst,tgh->sgrh", soft_low, value, preferred_element_type=f32)
    mixed = mixed.astype(bf16).reshape(seq, q_cols)
    mixed, dy_all, out_w, gu_right, piece_gu = tie(mixed, dy_all, out_w, gu_right, piece_gu)
    gu_left = along_z(piece_gu, -1)
    gu_next = second_right(gu_right)
    x_own = x_low.astype(f32)
    middle = x_own + scatter_chips(mm(mixed, out_w))

    dy_both = jnp.concatenate([dy_all, core_swap(dy_all)])
    d_act = mm_nt(dy_both, along_down)
    middle, dy_both, d_act, gu_left, gu_next = tie(middle, dy_both, d_act, gu_left, gu_next)
    found_gu = ring_rest(piece_gu, gu_right, gu_left, gu_next)
    scale_two = rms_scale(middle)
    n_two = middle * scale_two
    h_two = gather_chips((n_two * gain_two).astype(bf16))
    h_both = jnp.concatenate([h_two, core_swap(h_two)])
    w_gu = assemble(found_gu, 2 * chips).reshape(width, 2 * ff_cols)
    gu = mm(h_both, w_gu)
    gate, up = gu[:, :ff_cols], gu[:, ff_cols:]
    sigma = jax.nn.sigmoid(gate)
    act = (gate * sigma * up).astype(bf16)
    d_gate = (d_act * up * sigma * (1.0 + gate * (1.0 - sigma))).astype(bf16)
    d_up = (d_act * gate * sigma).astype(bf16)
    d_gu = jnp.concatenate([d_gate, d_up], axis=1)
    g_down = mm_tn(act, dy_both).astype(bf16)
    g_down, d_gu, act = tie(g_down, d_gu, act)
    g_down = lax.psum_scatter(g_down, "fsdp", scatter_dimension=0, tiled=True)

    def give_partial(rows, weights, product):
        other = core_swap(product(rows[seq:], weights).astype(bf16)).astype(f32)
        return product(rows[:seq], weights) + other

    d_h_two = give_partial(d_gu, w_gu, mm_nt)
    g_gu = mm_tn(h_both, d_gu).astype(bf16).reshape(2 * chips, rows_z, d_rows, 2 * ff_cols)
    d_h_two, g_gu = tie(d_h_two, g_gu)
    sums = scatter_window(g_gu, scatter_begin(g_gu), 0)
    d_h_two, *sums = tie(scatter_chips(d_h_two), *sums)

    dy_own = dy_low.astype(f32)
    gain_two_part = jnp.sum(d_h_two * n_two, axis=0)
    d_middle = dy_own + norm_back(d_h_two * gain_two, n_two, scale_two)
    branch = gather_chips(d_middle.astype(bf16))
    partial = give_partial(act, along_down, mm)
    sums = scatter_window(g_gu, sums, 1)
    branch, partial, g_down, *sums = tie(branch, partial, g_down, *sums)
    sums = scatter_window(g_gu, sums, 2)
    result = partial

    g_out = mm_tn(mixed, branch).astype(bf16)
    g_out = g_out.reshape(2, g_out.shape[0] // 2, g_out.shape[1])
    g_out = pick(g_out, core) + core_swap(pick(g_out, 1 - core))
    d_mixed = mm_nt(branch, out_w).astype(bf16).reshape(seq, kv_heads, 2, HEAD)
    d_soft = jnp.einsum("sgrh,tgh->grst", d_mixed, value, preferred_element_type=f32)
    d_value = jnp.einsum("grst,sgrh->tgh", soft_low, d_mixed, preferred_element_type=f32)
    inner = jnp.sum(soft * d_soft, axis=-1, keepdims=True)
    d_scores = (soft * (d_soft - inner)).astype(bf16)
    d_q = jnp.einsum("grst,tgh->sgrh", d_scores, k_rot, preferred_element_type=f32) * factor
    d_k = jnp.einsum("grst,sgrh->tgh", d_scores, q_rot, preferred_element_type=f32) * factor
    d_q = unrotate(d_q.reshape(seq, kv_heads * 2, HEAD), cosine, sine)
    d_k = unrotate(d_k, cosine, sine)
    d_qkv = jnp.concatenate(
        [
            d_q.reshape(seq, q_cols).astype(bf16),
            d_k.reshape(seq, kv_cols).astype(bf16),
            d_value.reshape(seq, kv_cols).astype(bf16),
        ],
        axis=1,
    )
    d_qkv, g_out, *sums = tie(d_qkv, g_out, *sums)
    g_gu = jnp.concatenate(sums, axis=-1)
    cols_qkv = d_qkv.shape[1]
    g_qkv = mm_tn(h_one, d_qkv).astype(bf16).reshape(chips, 2, rows_z, d_rows, cols_qkv)
    g_qkv = pick(g_qkv, core, 1) + core_swap(pick(g_qkv, 1 - core, 1))
    g_qkv = jnp.transpose(g_qkv, (1, 0, 2, 3)).reshape(1, rows_z, chips * d_rows, cols_qkv)
    folds = width // cols_qkv
    g_out = g_out.reshape(1, rows_z, d_rows, width)
    g_rest = [g_out[..., k * cols_qkv : (k + 1) * cols_qkv] for k in range(folds)]
    g_rest = jnp.concatenate([g_qkv] + g_rest, axis=2)
    d_h_one = mm_nt(d_qkv, w_qkv)
    g_rest, d_h_one = tie(g_rest, d_h_one)
    sums = scatter_window(g_rest, scatter_begin(g_rest), 0)
    d_h_one, result, *sums = tie(scatter_chips(d_h_one), result, *sums)
    sums = scatter_window(g_rest, sums, 1)
    result, *sums = tie(scatter_chips(result), *sums)
    result = (middle + result).astype(bf16)
    sums = scatter_window(g_rest, sums, 2)
    g_rest = jnp.concatenate(sums, axis=-1).reshape(-1, cols_qkv)
    scale_one = rms_scale(x_own)
    n_one = x_own * scale_one
    gain_one_part = jnp.sum(d_h_one * n_one, axis=0)
    d_input = (d_middle + norm_back(d_h_one * gain_one, n_one, scale_one)).astype(bf16)

    def give_back(a):
        mine, theirs = a[:tok], core_swap(a[tok:])
        first = core == 0
        return jnp.stack([jnp.where(first, mine, theirs), jnp.where(first, theirs, mine)])[:, None]

    def spread(grad, start, cols):
        part = grad[:, :, start : start + cols].astype(f32)
        return jnp.transpose(part, (1, 0, 2)).reshape(d_rows, chips * cols)

    def spread_ff(grad):
        grad = jnp.transpose(grad.astype(f32), (2, 0, 1, 3))
        return grad.reshape(d_rows, 2 * chips * ff_cols)

    g_down = g_down.astype(f32)
    g_gu = g_gu.reshape(chips, 2, d_rows, 2 * ff_cols)
    g_gu = core_pair(pick(g_gu, core, 1), core_swap(pick(g_gu, 1 - core, 1)), 1)
    g_gu = exchange_chips(g_gu)
    g_gate, g_up = spread_ff(g_gu[..., :ff_cols]), spread_ff(g_gu[..., ff_cols:])
    gain_parts = jnp.stack([gain_one_part, gain_two_part])
    gain_parts = sum_z(sum_chips(gain_parts + core_swap(gain_parts)))
    gain_parts = lax.dynamic_slice_in_dim(gain_parts, owner * d_rows, d_rows, 1)
    result, d_input = give_back(result), give_back(d_input)
    g_rest, g_gate, g_up, g_down, gain_parts, result, d_input = tie(
        g_rest, g_gate, g_up, g_down, gain_parts, result, d_input
    )
    g_qkv = exchange_chips(g_rest[: chips * d_rows].reshape(chips, d_rows, cols_qkv))
    g_out = g_rest[chips * d_rows :].reshape(folds, d_rows, cols_qkv)
    g_out = jnp.transpose(g_out, (1, 0, 2)).reshape(d_rows, width).astype(f32)
    return (
        result,
        d_input,
        gain_parts[0],
        spread(g_qkv, 0, q_cols),
        spread(g_qkv, q_cols, kv_cols),
        spread(g_qkv, q_cols + kv_cols, kv_cols),
        g_out,
        gain_parts[1],
        g_gate,
        g_up,
        g_down,
    )


def solution(mesh):
    ctx, fsdp = mesh.shape["ctx"], mesh.shape["fsdp"]
    split = Mesh(mesh.devices.reshape(ctx // 2, 2, fsdp), ("chip", "core", "fsdp"))
    ctx_axes = ("chip", "core")
    all_axes = ("chip", "core", "fsdp")
    tokens = P(None, "fsdp", ctx_axes, None)
    marks = P(None, "fsdp", ctx_axes)
    vector, matrix = P(all_axes), P(all_axes, None)
    return jax.shard_map(
        on_device,
        mesh=split,
        in_specs=(
            tokens, marks, marks, tokens, vector, matrix, matrix, matrix, matrix,
            vector, matrix, matrix, matrix,
        ),
        out_specs=(
            tokens, tokens, vector, matrix, matrix, matrix, matrix, vector,
            matrix, matrix, matrix,
        ),
        check_vma=False,
    )
```

```python
import math

import jax
import jax.numpy as jnp
from jax import lax
from jax.sharding import Mesh, PartitionSpec as P

HEADS = 16
KV_HEADS = 8
HEAD = 96
EPS = 1e-05
THETA = 100000.0
f32 = jnp.float32
bf16 = jnp.bfloat16


def rope_tables(position_ids):
    half = HEAD // 2
    ladder = jnp.arange(half).astype(f32) * (2.0 / HEAD)
    inverse = jnp.exp(-math.log(THETA) * ladder)
    angles = position_ids.astype(f32)[:, None] * inverse[None, :]
    return jnp.cos(angles)[:, None, :], jnp.sin(angles)[:, None, :]


def rotate(vectors, cosine, sine):
    half = HEAD // 2
    a, b = vectors[..., :half], vectors[..., half:]
    return jnp.concatenate([a * cosine - b * sine, b * cosine + a * sine], axis=-1)


def unrotate(grads, cosine, sine):
    half = HEAD // 2
    a, b = grads[..., :half], grads[..., half:]
    return jnp.concatenate([a * cosine + b * sine, b * cosine - a * sine], axis=-1)


def rms_scale(values):
    return lax.rsqrt(jnp.mean(values * values, axis=-1, keepdims=True) + EPS)


def norm_back(grad, normed, scale):
    return scale * (grad - normed * jnp.mean(grad * normed, axis=-1, keepdims=True))


def mm(a, b):
    return jnp.dot(a, b, preferred_element_type=f32)


def mm_tn(a, b):
    return jnp.einsum("td,te->de", a, b, preferred_element_type=f32)


def mm_nt(a, b):
    return jnp.einsum("te,de->td", a, b, preferred_element_type=f32)


def on_device(
    block_input,
    positions,
    segments,
    out_cotangent,
    attn_gain,
    w_query,
    w_key,
    w_value,
    w_out,
    mlp_gain,
    w_gate,
    w_up,
    w_down,
):
    chips = lax.axis_size("chip")
    rows_z = lax.axis_size("fsdp")
    chip = lax.axis_index("chip")
    core = lax.axis_index("core")
    place = lax.axis_index("fsdp")
    tok = block_input.shape[2]
    width = block_input.shape[3]
    d_rows = w_query.shape[0]
    q_cols = w_query.shape[1] // chips
    kv_cols = w_key.shape[1] // chips
    ff_cols = w_gate.shape[1] // (2 * chips)
    kv_heads = KV_HEADS // chips
    factor = HEAD ** (-0.5)

    def core_swap(a):
        return lax.ppermute(a, "core", [(0, 1), (1, 0)])

    def chip_xor(a, j):
        return lax.ppermute(a, "chip", [(i, i ^ j) for i in range(chips)])

    def pick(a, index, axis=0):
        return lax.dynamic_index_in_dim(a, index, axis, keepdims=False)

    def gather_chips(a, axis=0):
        return jnp.concatenate([a] + [chip_xor(a, j) for j in range(1, chips)], axis=axis)

    def scatter_chips(a):
        step = a.shape[0] // chips
        total = a[:step]
        for j in range(1, chips):
            total = total + chip_xor(a[j * step : (j + 1) * step].astype(bf16), j).astype(f32)
        return total

    def by_chip(pieces):
        stacked = jnp.stack(pieces)
        bit = 1
        while bit < chips:
            view = stacked.reshape((chips // (2 * bit), 2, bit) + stacked.shape[1:])
            flipped = jnp.flip(view, axis=1)
            stacked = jnp.where((chip & bit) != 0, flipped, view).reshape(stacked.shape)
            bit *= 2
        return stacked

    def exchange_chips(pack):
        pieces = [pick(pack, chip)]
        for j in range(1, chips):
            pieces.append(chip_xor(pick(pack, chip ^ j), j))
        return by_chip(pieces)

    def core_pair(mine, other, axis):
        first = core == 0
        return jnp.stack([jnp.where(first, mine, other), jnp.where(first, other, mine)], axis)

    def both_cores(a):
        return core_pair(a, core_swap(a), 0)

    def chip_slices(weights, cols):
        return jnp.stack(
            [
                jnp.concatenate([w[:, k * n : (k + 1) * n] for w, n in zip(weights, cols)], axis=1)
                for k in range(chips)
            ]
        )

    def tie(*values):
        return lax.optimization_barrier(values)

    def along_z(a, step):
        return lax.ppermute(a, "fsdp", [(i, (i + step) % rows_z) for i in range(rows_z)])

    def ring_first(a):
        return along_z(a, 1), along_z(a, -1)

    def ring_rest(a, right, left):
        found = [(a, 0, 0), (right, -1, 0), (left, 1, 0)]
        for step in range(2, rows_z // 2 + 1):
            if 2 * step == rows_z:
                half = a.shape[-1] // 2
                found.append((along_z(right[..., :half], 1), -step, 0))
                found.append((along_z(left[..., half:], -1), step, half))
            else:
                right, left = along_z(right, 1), along_z(left, -1)
                found += [(right, -step, 0), (left, step, 0)]
        return found

    windows = [2 + (rows_z - 1) * w // 3 for w in range(4)]

    def part(a, index, start):
        index = lax.rem(index + 2 * rows_z, rows_z)
        size = (a.shape[0], 1, a.shape[2], a.shape[3] // 2)
        return lax.dynamic_slice(a, (0, index, 0, start), size)

    def scatter_begin(a):
        return part(a, place - 1, 0), part(a, place + 1, a.shape[3] // 2)

    def scatter_window(a, sums, window):
        low, high = sums
        for step in range(windows[window], windows[window + 1]):
            low = along_z(low, 1) + part(a, place - step, 0)
            high = along_z(high, -1) + part(a, place + step, a.shape[3] // 2)
        return low, high

    def assemble(found, groups):
        rows, cols = found[0][0].shape
        whole = jnp.zeros((groups, rows_z, rows // groups, cols), bf16)
        for piece, offset, column in found:
            piece = piece.reshape(groups, 1, rows // groups, piece.shape[-1])
            index = lax.rem(place + offset + rows_z, rows_z)
            whole = lax.dynamic_update_slice(whole, piece, (0, index, 0, column))
        return whole

    owner = (chip * 2 + core) * rows_z + place
    spot = chip * 2 + core
    spots = chips * 2
    gains = lax.dynamic_update_slice(
        jnp.zeros((2, width), f32),
        jnp.stack([attn_gain, mlp_gain]).astype(f32),
        (0, owner * d_rows),
    )
    marks = lax.dynamic_update_slice(
        jnp.zeros((4, spots * tok), f32),
        jnp.concatenate([positions[:, 0], segments[:, 0]]).astype(f32),
        (0, spot * tok),
    )
    table = jnp.concatenate([gains.reshape(-1), marks.reshape(-1)]).reshape(-1, 128)

    def sum_chips(a):
        bit = 1
        while bit < chips:
            a = a + chip_xor(a, bit)
            bit *= 2
        return a

    def sum_z(a):
        bit = 1
        while bit < rows_z:
            a = a + lax.ppermute(a, "fsdp", [(i, i ^ bit) for i in range(rows_z)])
            bit *= 2
        return a

    def again(found, pieces):
        return [(piece,) + f[1:] for piece, f in zip(pieces, found)]

    def pieces_of(found):
        return [f[0] for f in found]

    out_right, out_left = ring_first(w_out)
    pack_qkv = chip_slices((w_query, w_key, w_value), (q_cols, kv_cols, kv_cols))
    piece_qkv = exchange_chips(pack_qkv).reshape(-1, pack_qkv.shape[-1])
    pair = jnp.stack([block_input[:, 0], out_cotangent[:, 0]], axis=1)
    pair = jnp.concatenate([pick(pair, core), core_swap(pick(pair, 1 - core))], axis=1)
    table = table + core_swap(table)
    pack_gu = jnp.stack(
        [
            jnp.concatenate([w[:, n * ff_cols : (n + 1) * ff_cols] for w in (w_gate, w_up)], axis=1)
            for n in range(2 * chips)
        ]
    ).reshape(chips, 2, d_rows, 2 * ff_cols)
    pair, piece_qkv, table, pack_gu, out_right, out_left = tie(
        pair, piece_qkv, table, pack_gu, out_right, out_left
    )
    x_low, dy_low = pair[0], pair[1]

    qkv_right, qkv_left = ring_first(piece_qkv)
    piece_gu = exchange_chips(pack_gu)
    table = sum_chips(table)
    found_out = ring_rest(w_out, out_right, out_left)
    qkv_right, qkv_left, piece_gu, table, x_low, *late = tie(
        qkv_right, qkv_left, piece_gu, table, x_low, *pieces_of(found_out)
    )
    found_out = again(found_out, late)

    near = [j for j in range(1, chips) if j & (j - 1) == 0]
    far = [j for j in range(1, chips) if j & (j - 1) != 0]
    x_parts = {0: x_low, **{j: chip_xor(x_low, j) for j in near}}
    found_qkv = ring_rest(piece_qkv, qkv_right, qkv_left)
    piece_gu = core_pair(pick(piece_gu, core, 1), core_swap(pick(piece_gu, 1 - core, 1)), 1)
    piece_gu = piece_gu.reshape(2 * chips * d_rows, 2 * ff_cols)
    order = sorted(x_parts)
    piece_gu, *late = tie(piece_gu, *[x_parts[j] for j in order], *pieces_of(found_qkv))
    x_parts = dict(zip(order, late))
    x_parts.update({j: chip_xor(x_parts[0], j) for j in far})
    x_all = jnp.concatenate([x_parts[j] for j in range(chips)])
    found_qkv = again(found_qkv, late[len(order) :])
    gu_right = along_z(piece_gu, 1)
    gains = sum_z(table.reshape(-1)[: 2 * width].reshape(2, width))
    marks = pick(table.reshape(-1)[2 * width :].reshape(2, 2, spots, tok), core, 1)
    marks = jnp.concatenate(
        [pick(marks, (chip ^ k) * 2 + (core ^ c), 1) for k in range(chips) for c in range(2)],
        axis=1,
    )
    pos_all, seg_all = marks
    allowed = (seg_all[:, None] == seg_all[None, :]) & (pos_all[None, :] <= pos_all[:, None])
    cosine, sine = rope_tables(pos_all)
    w_qkv = assemble(found_qkv, chips)
    w_qkv = core_pair(w_qkv, core_swap(w_qkv), 1).reshape(width, -1)
    w_qkv, x_all, gains, dy_low, cosine, sine, allowed = tie(
        w_qkv, x_all, gains, dy_low, cosine, sine, allowed
    )
    gain_one, gain_two = gains
    own = x_low.shape[0]
    seq = x_all.shape[0]

    dy_all = gather_chips(dy_low)
    x_full = x_all.astype(f32)
    h_one = (x_full * rms_scale(x_full) * gain_one).astype(bf16)
    qkv = mm(h_one, w_qkv)
    q_rot = rotate(qkv[:, :q_cols].reshape(seq, kv_heads * 2, HEAD), cosine, sine)
    q_rot = q_rot.astype(bf16).reshape(seq, kv_heads, 2, HEAD)
    k_rot = rotate(
        qkv[:, q_cols : q_cols + kv_cols].reshape(seq, kv_heads, HEAD), cosine, sine
    ).astype(bf16)
    value = qkv[:, q_cols + kv_cols :].astype(bf16).reshape(seq, kv_heads, HEAD)
    q_rot, gu_right, piece_gu = tie(q_rot, gu_right, piece_gu)
    gu_left = along_z(piece_gu, -1)
    out_w = assemble(found_out, 1).reshape(rows_z * d_rows, width)
    out_w = both_cores(out_w).reshape(-1, width)
    scores = jnp.einsum("sgrh,tgh->grst", q_rot, k_rot, preferred_element_type=f32) * factor
    scores = jnp.where(allowed, scores, -1e30)
    raised = jnp.exp(scores - jnp.max(scores, axis=-1, keepdims=True))
    soft = raised / jnp.sum(raised, axis=-1, keepdims=True)
    soft_low = soft.astype(bf16)
    mixed = jnp.einsum("grst,tgh->sgrh", soft_low, value, preferred_element_type=f32)
    mixed = mixed.astype(bf16).reshape(seq, q_cols)
    mixed, dy_all, out_w, gu_left, w_down = tie(mixed, dy_all, out_w, gu_left, w_down)
    along_down = lax.all_gather(w_down, "fsdp", axis=0, tiled=True)
    found_gu = ring_rest(piece_gu, gu_right, gu_left)
    x_own = x_low.astype(f32)
    middle = x_own + scatter_chips(mm(mixed, out_w))

    dy_both = jnp.concatenate([dy_all, core_swap(dy_all)])
    middle, dy_both, *late = tie(middle, dy_both, *pieces_of(found_gu))
    found_gu = again(found_gu, late)
    scale_two = rms_scale(middle)
    n_two = middle * scale_two
    h_two = gather_chips((n_two * gain_two).astype(bf16))
    h_two, along_down = tie(h_two, along_down)
    h_both = jnp.concatenate([h_two, core_swap(h_two)])
    w_gu = assemble(found_gu, 2 * chips).reshape(width, 2 * ff_cols)
    gu = mm(h_both, w_gu)
    gate, up = gu[:, :ff_cols], gu[:, ff_cols:]
    sigma = jax.nn.sigmoid(gate)
    act = (gate * sigma * up).astype(bf16)
    g_down = mm_tn(act, dy_both).astype(bf16)
    g_down, act = tie(g_down, act)
    g_down = lax.psum_scatter(g_down, "fsdp", scatter_dimension=0, tiled=True)
    d_act = mm_nt(dy_both, along_down)
    d_gate = (d_act * up * sigma * (1.0 + gate * (1.0 - sigma))).astype(bf16)
    d_up = (d_act * gate * sigma).astype(bf16)
    d_gu = jnp.concatenate([d_gate, d_up], axis=1)

    def give_partial(rows, weights, product):
        other = core_swap(product(rows[seq:], weights).astype(bf16)).astype(f32)
        return product(rows[:seq], weights) + other

    d_h_two = give_partial(d_gu, w_gu, mm_nt)
    g_gu = mm_tn(h_both, d_gu).astype(bf16).reshape(2 * chips, rows_z, d_rows, 2 * ff_cols)
    g_gu = jnp.transpose(g_gu, (1, 0, 2, 3)).reshape(width, 2 * ff_cols)
    d_h_two, g_gu = tie(scatter_chips(d_h_two), g_gu)
    g_gu = lax.psum_scatter(g_gu, "fsdp", scatter_dimension=0, tiled=True)

    dy_own = dy_low.astype(f32)
    gain_two_part = jnp.sum(d_h_two * n_two, axis=0)
    d_middle = dy_own + norm_back(d_h_two * gain_two, n_two, scale_two)
    branch = gather_chips(d_middle.astype(bf16))
    partial = give_partial(act, along_down, mm)
    branch, partial, g_down = tie(branch, partial, g_down)
    result = partial

    g_out = mm_tn(mixed, branch).astype(bf16)
    g_out = g_out.reshape(2, g_out.shape[0] // 2, g_out.shape[1])
    g_out = pick(g_out, core) + core_swap(pick(g_out, 1 - core))
    d_mixed = mm_nt(branch, out_w).astype(bf16).reshape(seq, kv_heads, 2, HEAD)
    d_soft = jnp.einsum("sgrh,tgh->grst", d_mixed, value, preferred_element_type=f32)
    d_value = jnp.einsum("grst,sgrh->tgh", soft_low, d_mixed, preferred_element_type=f32)
    inner = jnp.sum(soft * d_soft, axis=-1, keepdims=True)
    d_scores = (soft * (d_soft - inner)).astype(bf16)
    d_q = jnp.einsum("grst,tgh->sgrh", d_scores, k_rot, preferred_element_type=f32) * factor
    d_k = jnp.einsum("grst,sgrh->tgh", d_scores, q_rot, preferred_element_type=f32) * factor
    d_q = unrotate(d_q.reshape(seq, kv_heads * 2, HEAD), cosine, sine)
    d_k = unrotate(d_k, cosine, sine)
    d_qkv = jnp.concatenate(
        [
            d_q.reshape(seq, q_cols).astype(bf16),
            d_k.reshape(seq, kv_cols).astype(bf16),
            d_value.reshape(seq, kv_cols).astype(bf16),
        ],
        axis=1,
    )
    d_qkv, g_out = tie(d_qkv, g_out)
    cols_qkv = d_qkv.shape[1]
    g_qkv = mm_tn(h_one, d_qkv).astype(bf16).reshape(chips, 2, rows_z, d_rows, cols_qkv)
    g_qkv = pick(g_qkv, core, 1) + core_swap(pick(g_qkv, 1 - core, 1))
    g_qkv = jnp.transpose(g_qkv, (1, 0, 2, 3)).reshape(1, rows_z, chips * d_rows, cols_qkv)
    folds = width // cols_qkv
    g_out = g_out.reshape(1, rows_z, d_rows, width)
    g_rest = [g_out[..., k * cols_qkv : (k + 1) * cols_qkv] for k in range(folds)]
    g_rest = jnp.concatenate([g_qkv] + g_rest, axis=2)
    d_h_one = mm_nt(d_qkv, w_qkv)
    g_rest, d_h_one = tie(g_rest, d_h_one)
    sums = scatter_window(g_rest, scatter_begin(g_rest), 0)
    d_h_one, result, g_gu, *sums = tie(scatter_chips(d_h_one), result, g_gu, *sums)
    sums = scatter_window(g_rest, sums, 1)
    result, *sums = tie(scatter_chips(result), *sums)
    result = (middle + result).astype(bf16)
    sums = scatter_window(g_rest, sums, 2)
    g_rest = jnp.concatenate(sums, axis=-1).reshape(-1, cols_qkv)
    scale_one = rms_scale(x_own)
    n_one = x_own * scale_one
    gain_one_part = jnp.sum(d_h_one * n_one, axis=0)
    d_input = (d_middle + norm_back(d_h_one * gain_one, n_one, scale_one)).astype(bf16)

    def give_back(a):
        mine, theirs = a[:tok], core_swap(a[tok:])
        first = core == 0
        return jnp.stack([jnp.where(first, mine, theirs), jnp.where(first, theirs, mine)])[:, None]

    def spread(grad, start, cols):
        part = grad[:, :, start : start + cols].astype(f32)
        return jnp.transpose(part, (1, 0, 2)).reshape(d_rows, chips * cols)

    def spread_ff(grad):
        grad = jnp.transpose(grad.astype(f32), (2, 0, 1, 3))
        return grad.reshape(d_rows, 2 * chips * ff_cols)

    g_down = g_down.astype(f32)
    g_gu = g_gu.reshape(chips, 2, d_rows, 2 * ff_cols)
    g_gu = core_pair(pick(g_gu, core, 1), core_swap(pick(g_gu, 1 - core, 1)), 1)
    g_gu = exchange_chips(g_gu)
    g_gate, g_up = spread_ff(g_gu[..., :ff_cols]), spread_ff(g_gu[..., ff_cols:])
    gain_parts = jnp.stack([gain_one_part, gain_two_part])
    gain_parts = sum_z(sum_chips(gain_parts + core_swap(gain_parts)))
    gain_parts = lax.dynamic_slice_in_dim(gain_parts, owner * d_rows, d_rows, 1)
    result, d_input = give_back(result), give_back(d_input)
    g_rest, g_gate, g_up, g_down, gain_parts, result, d_input = tie(
        g_rest, g_gate, g_up, g_down, gain_parts, result, d_input
    )
    g_qkv = exchange_chips(g_rest[: chips * d_rows].reshape(chips, d_rows, cols_qkv))
    g_out = g_rest[chips * d_rows :].reshape(folds, d_rows, cols_qkv)
    g_out = jnp.transpose(g_out, (1, 0, 2)).reshape(d_rows, width).astype(f32)
    return (
        result,
        d_input,
        gain_parts[0],
        spread(g_qkv, 0, q_cols),
        spread(g_qkv, q_cols, kv_cols),
        spread(g_qkv, q_cols + kv_cols, kv_cols),
        g_out,
        gain_parts[1],
        g_gate,
        g_up,
        g_down,
    )


def solution(mesh):
    ctx, fsdp = mesh.shape["ctx"], mesh.shape["fsdp"]
    split = Mesh(mesh.devices.reshape(ctx // 2, 2, fsdp), ("chip", "core", "fsdp"))
    ctx_axes = ("chip", "core")
    all_axes = ("chip", "core", "fsdp")
    tokens = P(None, "fsdp", ctx_axes, None)
    marks = P(None, "fsdp", ctx_axes)
    vector, matrix = P(all_axes), P(all_axes, None)
    return jax.shard_map(
        on_device,
        mesh=split,
        in_specs=(
            tokens, marks, marks, tokens, vector, matrix, matrix, matrix, matrix,
            vector, matrix, matrix, matrix,
        ),
        out_specs=(
            tokens, tokens, vector, matrix, matrix, matrix, matrix, vector,
            matrix, matrix, matrix,
        ),
        check_vma=False,
    )
```

```python
import math

import jax
import jax.numpy as jnp
from jax import lax
from jax.sharding import Mesh, PartitionSpec as P

HEADS = 16
KV_HEADS = 8
HEAD = 96
EPS = 1e-05
THETA = 100000.0
f32 = jnp.float32
bf16 = jnp.bfloat16


def rope_tables(position_ids):
    half = HEAD // 2
    ladder = jnp.arange(half).astype(f32) * (2.0 / HEAD)
    inverse = jnp.exp(-math.log(THETA) * ladder)
    angles = position_ids.astype(f32)[:, None] * inverse[None, :]
    return jnp.cos(angles)[:, None, :], jnp.sin(angles)[:, None, :]


def rotate(vectors, cosine, sine):
    half = HEAD // 2
    a, b = vectors[..., :half], vectors[..., half:]
    return jnp.concatenate([a * cosine - b * sine, b * cosine + a * sine], axis=-1)


def unrotate(grads, cosine, sine):
    half = HEAD // 2
    a, b = grads[..., :half], grads[..., half:]
    return jnp.concatenate([a * cosine + b * sine, b * cosine - a * sine], axis=-1)


def rms_scale(values):
    return lax.rsqrt(jnp.mean(values * values, axis=-1, keepdims=True) + EPS)


def norm_back(grad, normed, scale):
    return scale * (grad - normed * jnp.mean(grad * normed, axis=-1, keepdims=True))


def mm(a, b):
    return jnp.dot(a, b, preferred_element_type=f32)


def mm_tn(a, b):
    return jnp.einsum("td,te->de", a, b, preferred_element_type=f32)


def mm_nt(a, b):
    return jnp.einsum("te,de->td", a, b, preferred_element_type=f32)


def on_device(
    block_input,
    positions,
    segments,
    out_cotangent,
    attn_gain,
    w_query,
    w_key,
    w_value,
    w_out,
    mlp_gain,
    w_gate,
    w_up,
    w_down,
):
    chips = lax.axis_size("chip")
    rows_z = lax.axis_size("fsdp")
    chip = lax.axis_index("chip")
    core = lax.axis_index("core")
    place = lax.axis_index("fsdp")
    tok = block_input.shape[2]
    width = block_input.shape[3]
    d_rows = w_query.shape[0]
    q_cols = w_query.shape[1] // chips
    kv_cols = w_key.shape[1] // chips
    ff_cols = w_gate.shape[1] // (2 * chips)
    kv_heads = KV_HEADS // chips
    factor = HEAD ** (-0.5)

    def core_swap(a):
        return lax.ppermute(a, "core", [(0, 1), (1, 0)])

    def chip_xor(a, j):
        return lax.ppermute(a, "chip", [(i, i ^ j) for i in range(chips)])

    def pick(a, index, axis=0):
        return lax.dynamic_index_in_dim(a, index, axis, keepdims=False)

    def gather_chips(a, axis=0):
        return jnp.concatenate([a] + [chip_xor(a, j) for j in range(1, chips)], axis=axis)

    def scatter_chips(a):
        step = a.shape[0] // chips
        total = a[:step]
        for j in range(1, chips):
            total = total + chip_xor(a[j * step : (j + 1) * step].astype(bf16), j).astype(f32)
        return total

    def by_chip(pieces):
        stacked = jnp.stack(pieces)
        bit = 1
        while bit < chips:
            view = stacked.reshape((chips // (2 * bit), 2, bit) + stacked.shape[1:])
            flipped = jnp.flip(view, axis=1)
            stacked = jnp.where((chip & bit) != 0, flipped, view).reshape(stacked.shape)
            bit *= 2
        return stacked

    def exchange_chips(pack):
        pieces = [pick(pack, chip)]
        for j in range(1, chips):
            pieces.append(chip_xor(pick(pack, chip ^ j), j))
        return by_chip(pieces)

    def core_pair(mine, other, axis):
        first = core == 0
        return jnp.stack([jnp.where(first, mine, other), jnp.where(first, other, mine)], axis)

    def both_cores(a):
        return core_pair(a, core_swap(a), 0)

    def chip_slices(weights, cols):
        return jnp.stack(
            [
                jnp.concatenate([w[:, k * n : (k + 1) * n] for w, n in zip(weights, cols)], axis=1)
                for k in range(chips)
            ]
        )

    def tie(*values):
        return lax.optimization_barrier(values)

    def along_z(a, step):
        return lax.ppermute(a, "fsdp", [(i, (i + step) % rows_z) for i in range(rows_z)])

    def ring_first(a):
        return along_z(a, 1), along_z(a, -1)

    def ring_rest(a, right, left):
        found = [(a, 0, 0), (right, -1, 0), (left, 1, 0)]
        for step in range(2, rows_z // 2 + 1):
            if 2 * step == rows_z:
                half = a.shape[-1] // 2
                found.append((along_z(right[..., :half], 1), -step, 0))
                found.append((along_z(left[..., half:], -1), step, half))
            else:
                right, left = along_z(right, 1), along_z(left, -1)
                found += [(right, -step, 0), (left, step, 0)]
        return found

    windows = [2 + (rows_z - 1) * w // 3 for w in range(4)]

    def part(a, index, start):
        index = lax.rem(index + 2 * rows_z, rows_z)
        size = (a.shape[0], 1, a.shape[2], a.shape[3] // 2)
        return lax.dynamic_slice(a, (0, index, 0, start), size)

    def scatter_begin(a):
        return part(a, place - 1, 0), part(a, place + 1, a.shape[3] // 2)

    def scatter_window(a, sums, window):
        low, high = sums
        for step in range(windows[window], windows[window + 1]):
            low = along_z(low, 1) + part(a, place - step, 0)
            high = along_z(high, -1) + part(a, place + step, a.shape[3] // 2)
        return low, high

    def assemble(found, groups):
        rows, cols = found[0][0].shape
        whole = jnp.zeros((groups, rows_z, rows // groups, cols), bf16)
        for piece, offset, column in found:
            piece = piece.reshape(groups, 1, rows // groups, piece.shape[-1])
            index = lax.rem(place + offset + rows_z, rows_z)
            whole = lax.dynamic_update_slice(whole, piece, (0, index, 0, column))
        return whole

    owner = (chip * 2 + core) * rows_z + place
    spot = chip * 2 + core
    spots = chips * 2
    gains = lax.dynamic_update_slice(
        jnp.zeros((2, width), f32),
        jnp.stack([attn_gain, mlp_gain]).astype(f32),
        (0, owner * d_rows),
    )
    marks = lax.dynamic_update_slice(
        jnp.zeros((4, spots * tok), f32),
        jnp.concatenate([positions[:, 0], segments[:, 0]]).astype(f32),
        (0, spot * tok),
    )
    table = jnp.concatenate([gains.reshape(-1), marks.reshape(-1)]).reshape(-1, 128)

    def sum_chips(a):
        bit = 1
        while bit < chips:
            a = a + chip_xor(a, bit)
            bit *= 2
        return a

    def sum_z(a):
        bit = 1
        while bit < rows_z:
            a = a + lax.ppermute(a, "fsdp", [(i, i ^ bit) for i in range(rows_z)])
            bit *= 2
        return a

    def again(found, pieces):
        return [(piece,) + f[1:] for piece, f in zip(pieces, found)]

    def pieces_of(found):
        return [f[0] for f in found]

    pack_qkv = chip_slices((w_query, w_key, w_value), (q_cols, kv_cols, kv_cols))
    piece_qkv = exchange_chips(pack_qkv).reshape(-1, pack_qkv.shape[-1])
    pair = jnp.stack([block_input[:, 0], out_cotangent[:, 0]], axis=1)
    pair = jnp.concatenate([pick(pair, core), core_swap(pick(pair, 1 - core))], axis=1)
    table = sum_chips(table + core_swap(table))
    gains = sum_z(table.reshape(-1)[: 2 * width].reshape(2, width))
    pack_gu = jnp.stack(
        [
            jnp.concatenate([w[:, n * ff_cols : (n + 1) * ff_cols] for w in (w_gate, w_up)], axis=1)
            for n in range(2 * chips)
        ]
    ).reshape(chips, 2, d_rows, 2 * ff_cols)
    pair, piece_qkv, table, gains, pack_gu = tie(pair, piece_qkv, table, gains, pack_gu)
    x_low, dy_low = pair[0], pair[1]

    qkv_right, qkv_left = ring_first(piece_qkv)
    piece_gu = exchange_chips(pack_gu)
    qkv_right, qkv_left, piece_gu, x_low, w_out = tie(qkv_right, qkv_left, piece_gu, x_low, w_out)

    near = [j for j in range(1, chips) if j & (j - 1) == 0]
    far = [j for j in range(1, chips) if j & (j - 1) != 0]
    x_parts = {0: x_low, **{j: chip_xor(x_low, j) for j in near}}
    found_qkv = ring_rest(piece_qkv, qkv_right, qkv_left)
    piece_gu = core_pair(pick(piece_gu, core, 1), core_swap(pick(piece_gu, 1 - core, 1)), 1)
    piece_gu = piece_gu.reshape(2 * chips * d_rows, 2 * ff_cols)
    order = sorted(x_parts)
    out_right, out_left = ring_first(w_out)
    piece_gu, out_right, out_left, *late = tie(piece_gu, out_right, out_left, *[x_parts[j] for j in order], *pieces_of(found_qkv))
    x_parts = dict(zip(order, late))
    x_parts.update({j: chip_xor(x_parts[0], j) for j in far})
    x_all = jnp.concatenate([x_parts[j] for j in range(chips)])
    found_qkv = again(found_qkv, late[len(order) :])
    gu_right = along_z(piece_gu, 1)
    found_out = ring_rest(w_out, out_right, out_left)
    marks = pick(table.reshape(-1)[2 * width :].reshape(2, 2, spots, tok), core, 1)
    marks = jnp.concatenate(
        [pick(marks, (chip ^ k) * 2 + (core ^ c), 1) for k in range(chips) for c in range(2)],
        axis=1,
    )
    pos_all, seg_all = marks
    allowed = (seg_all[:, None] == seg_all[None, :]) & (pos_all[None, :] <= pos_all[:, None])
    cosine, sine = rope_tables(pos_all)
    w_qkv = assemble(found_qkv, chips)
    w_qkv = core_pair(w_qkv, core_swap(w_qkv), 1).reshape(width, -1)
    w_qkv, x_all, dy_low, cosine, sine, allowed = tie(w_qkv, x_all, dy_low, cosine, sine, allowed)
    gain_one, gain_two = gains
    own = x_low.shape[0]
    seq = x_all.shape[0]

    dy_all = gather_chips(dy_low)
    x_full = x_all.astype(f32)
    h_one = (x_full * rms_scale(x_full) * gain_one).astype(bf16)
    qkv = mm(h_one, w_qkv)
    q_rot = rotate(qkv[:, :q_cols].reshape(seq, kv_heads * 2, HEAD), cosine, sine)
    q_rot = q_rot.astype(bf16).reshape(seq, kv_heads, 2, HEAD)
    k_rot = rotate(
        qkv[:, q_cols : q_cols + kv_cols].reshape(seq, kv_heads, HEAD), cosine, sine
    ).astype(bf16)
    value = qkv[:, q_cols + kv_cols :].astype(bf16).reshape(seq, kv_heads, HEAD)
    q_rot, gu_right, piece_gu, *late = tie(q_rot, gu_right, piece_gu, *pieces_of(found_out))
    found_out = again(found_out, late)
    gu_left = along_z(piece_gu, -1)
    out_w = assemble(found_out, 1).reshape(rows_z * d_rows, width)
    out_w = both_cores(out_w).reshape(-1, width)
    scores = jnp.einsum("sgrh,tgh->grst", q_rot, k_rot, preferred_element_type=f32) * factor
    scores = jnp.where(allowed, scores, -1e30)
    raised = jnp.exp(scores - jnp.max(scores, axis=-1, keepdims=True))
    soft = raised / jnp.sum(raised, axis=-1, keepdims=True)
    soft_low = soft.astype(bf16)
    mixed = jnp.einsum("grst,tgh->sgrh", soft_low, value, preferred_element_type=f32)
    mixed = mixed.astype(bf16).reshape(seq, q_cols)
    mixed, dy_all, out_w, gu_left = tie(mixed, dy_all, out_w, gu_left)
    found_gu = ring_rest(piece_gu, gu_right, gu_left)
    x_own = x_low.astype(f32)
    middle = x_own + scatter_chips(mm(mixed, out_w))

    dy_both = jnp.concatenate([dy_all, core_swap(dy_all)])
    middle, dy_both, w_down, *late = tie(middle, dy_both, w_down, *pieces_of(found_gu))
    found_gu = again(found_gu, late)
    along_down = lax.all_gather(w_down, "fsdp", axis=0, tiled=True)
    w_gu = assemble(found_gu, 2 * chips).reshape(width, 2 * ff_cols)
    scale_two = rms_scale(middle)
    n_two = middle * scale_two
    h_two = gather_chips((n_two * gain_two).astype(bf16))
    h_two, w_gu = tie(h_two, w_gu)
    h_both, along_down = tie(jnp.concatenate([h_two, core_swap(h_two)]), along_down)
    gu = mm(h_both, w_gu)
    gate, up = gu[:, :ff_cols], gu[:, ff_cols:]
    sigma = jax.nn.sigmoid(gate)
    act = (gate * sigma * up).astype(bf16)
    g_down = mm_tn(act, dy_both).astype(bf16)
    g_down, act = tie(g_down, act)
    g_down = lax.psum_scatter(g_down, "fsdp", scatter_dimension=0, tiled=True)
    d_act = mm_nt(dy_both, along_down)
    d_gate = (d_act * up * sigma * (1.0 + gate * (1.0 - sigma))).astype(bf16)
    d_up = (d_act * gate * sigma).astype(bf16)
    d_gu = jnp.concatenate([d_gate, d_up], axis=1)

    def give_partial(rows, weights, product):
        other = core_swap(product(rows[seq:], weights).astype(bf16)).astype(f32)
        return product(rows[:seq], weights) + other

    d_h_two = give_partial(d_gu, w_gu, mm_nt)
    g_gu = mm_tn(h_both, d_gu).astype(bf16).reshape(2 * chips, rows_z, d_rows, 2 * ff_cols)
    g_gu = jnp.transpose(g_gu, (1, 0, 2, 3)).reshape(width, 2 * ff_cols)
    d_h_two, g_gu = tie(scatter_chips(d_h_two), g_gu)
    g_gu = lax.psum_scatter(g_gu, "fsdp", scatter_dimension=0, tiled=True)

    dy_own = dy_low.astype(f32)
    gain_two_part = jnp.sum(d_h_two * n_two, axis=0)
    d_middle = dy_own + norm_back(d_h_two * gain_two, n_two, scale_two)
    branch = gather_chips(d_middle.astype(bf16))
    partial = give_partial(act, along_down, mm)
    branch, partial, g_down = tie(branch, partial, g_down)
    shares = {
        j: partial[j * own : (j + 1) * own].astype(bf16) if j else partial[:own]
        for j in range(chips)
    }
    shares.update({j: chip_xor(shares[j], j) for j in near})

    g_out = mm_tn(mixed, branch).astype(bf16)
    g_out = g_out.reshape(2, g_out.shape[0] // 2, g_out.shape[1])
    g_out = pick(g_out, core) + core_swap(pick(g_out, 1 - core))
    d_mixed = mm_nt(branch, out_w).astype(bf16).reshape(seq, kv_heads, 2, HEAD)
    d_soft = jnp.einsum("sgrh,tgh->grst", d_mixed, value, preferred_element_type=f32)
    d_value = jnp.einsum("grst,sgrh->tgh", soft_low, d_mixed, preferred_element_type=f32)
    inner = jnp.sum(soft * d_soft, axis=-1, keepdims=True)
    d_scores = (soft * (d_soft - inner)).astype(bf16)
    d_scores, *late = tie(d_scores, *[shares[j] for j in range(chips)])
    shares = dict(enumerate(late))
    shares.update({j: chip_xor(shares[j], j) for j in far})
    d_q = jnp.einsum("grst,tgh->sgrh", d_scores, k_rot, preferred_element_type=f32) * factor
    d_k = jnp.einsum("grst,sgrh->tgh", d_scores, q_rot, preferred_element_type=f32) * factor
    d_q = unrotate(d_q.reshape(seq, kv_heads * 2, HEAD), cosine, sine)
    d_k = unrotate(d_k, cosine, sine)
    d_qkv = jnp.concatenate(
        [
            d_q.reshape(seq, q_cols).astype(bf16),
            d_k.reshape(seq, kv_cols).astype(bf16),
            d_value.reshape(seq, kv_cols).astype(bf16),
        ],
        axis=1,
    )
    d_qkv, g_out = tie(d_qkv, g_out)
    cols_qkv = d_qkv.shape[1]
    g_qkv = mm_tn(h_one, d_qkv).astype(bf16).reshape(chips, 2, rows_z, d_rows, cols_qkv)
    g_qkv = pick(g_qkv, core, 1) + core_swap(pick(g_qkv, 1 - core, 1))
    g_qkv = jnp.transpose(g_qkv, (1, 0, 2, 3)).reshape(1, rows_z, chips * d_rows, cols_qkv)
    folds = width // cols_qkv
    g_out = g_out.reshape(1, rows_z, d_rows, width)
    g_rest = [g_out[..., k * cols_qkv : (k + 1) * cols_qkv] for k in range(folds)]
    g_rest = jnp.concatenate([g_qkv] + g_rest, axis=2)
    d_h_one = mm_nt(d_qkv, w_qkv)
    result = middle + shares[0]
    for j in range(1, chips):
        result = result + shares[j].astype(f32)
    g_rest, d_h_one, result = tie(g_rest, d_h_one, result.astype(bf16))
    sums = scatter_window(g_rest, scatter_begin(g_rest), 0)
    d_h_one, *sums = tie(scatter_chips(d_h_one), *sums)
    scale_one = rms_scale(x_own)
    n_one = x_own * scale_one
    gain_one_part = jnp.sum(d_h_one * n_one, axis=0)
    gain_parts = jnp.stack([gain_one_part, gain_two_part])
    gain_parts = sum_chips(gain_parts + core_swap(gain_parts))
    gain_parts, *sums = tie(gain_parts, *scatter_window(g_rest, sums, 1))
    sums = scatter_window(g_rest, sums, 2)
    g_rest = jnp.concatenate(sums, axis=-1).reshape(-1, cols_qkv)
    d_input = (d_middle + norm_back(d_h_one * gain_one, n_one, scale_one)).astype(bf16)

    def give_back(a):
        mine, theirs = a[:tok], core_swap(a[tok:])
        first = core == 0
        return jnp.stack([jnp.where(first, mine, theirs), jnp.where(first, theirs, mine)])[:, None]

    def spread(grad, start, cols):
        part = grad[:, :, start : start + cols].astype(f32)
        return jnp.transpose(part, (1, 0, 2)).reshape(d_rows, chips * cols)

    def spread_ff(grad):
        grad = jnp.transpose(grad.astype(f32), (2, 0, 1, 3))
        return grad.reshape(d_rows, 2 * chips * ff_cols)

    g_down = g_down.astype(f32)
    g_gu = g_gu.reshape(chips, 2, d_rows, 2 * ff_cols)
    g_gu = core_pair(pick(g_gu, core, 1), core_swap(pick(g_gu, 1 - core, 1)), 1)
    g_gu = exchange_chips(g_gu)
    g_gate, g_up = spread_ff(g_gu[..., :ff_cols]), spread_ff(g_gu[..., ff_cols:])
    gain_parts = sum_z(gain_parts)
    gain_parts = lax.dynamic_slice_in_dim(gain_parts, owner * d_rows, d_rows, 1)
    result, d_input = give_back(result), give_back(d_input)
    g_rest, g_gate, g_up, g_down, gain_parts, result, d_input = tie(
        g_rest, g_gate, g_up, g_down, gain_parts, result, d_input
    )
    g_qkv = exchange_chips(g_rest[: chips * d_rows].reshape(chips, d_rows, cols_qkv))
    g_out = g_rest[chips * d_rows :].reshape(folds, d_rows, cols_qkv)
    g_out = jnp.transpose(g_out, (1, 0, 2)).reshape(d_rows, width).astype(f32)
    return (
        result,
        d_input,
        gain_parts[0],
        spread(g_qkv, 0, q_cols),
        spread(g_qkv, q_cols, kv_cols),
        spread(g_qkv, q_cols + kv_cols, kv_cols),
        g_out,
        gain_parts[1],
        g_gate,
        g_up,
        g_down,
    )


def solution(mesh):
    ctx, fsdp = mesh.shape["ctx"], mesh.shape["fsdp"]
    split = Mesh(mesh.devices.reshape(ctx // 2, 2, fsdp), ("chip", "core", "fsdp"))
    ctx_axes = ("chip", "core")
    all_axes = ("chip", "core", "fsdp")
    tokens = P(None, "fsdp", ctx_axes, None)
    marks = P(None, "fsdp", ctx_axes)
    vector, matrix = P(all_axes), P(all_axes, None)
    return jax.shard_map(
        on_device,
        mesh=split,
        in_specs=(
            tokens, marks, marks, tokens, vector, matrix, matrix, matrix, matrix,
            vector, matrix, matrix, matrix,
        ),
        out_specs=(
            tokens, tokens, vector, matrix, matrix, matrix, matrix, vector,
            matrix, matrix, matrix,
        ),
        check_vma=False,
    )
```

```python
import math

import jax
import jax.numpy as jnp
from jax import lax
from jax.sharding import Mesh, PartitionSpec as P

HEADS = 16
KV_HEADS = 8
HEAD = 96
EPS = 1e-05
THETA = 100000.0
f32 = jnp.float32
bf16 = jnp.bfloat16


def rope_tables(position_ids):
    half = HEAD // 2
    ladder = jnp.arange(half).astype(f32) * (2.0 / HEAD)
    inverse = jnp.exp(-math.log(THETA) * ladder)
    angles = position_ids.astype(f32)[:, None] * inverse[None, :]
    return jnp.cos(angles)[:, None, :], jnp.sin(angles)[:, None, :]


def rotate(vectors, cosine, sine):
    half = HEAD // 2
    a, b = vectors[..., :half], vectors[..., half:]
    return jnp.concatenate([a * cosine - b * sine, b * cosine + a * sine], axis=-1)


def unrotate(grads, cosine, sine):
    half = HEAD // 2
    a, b = grads[..., :half], grads[..., half:]
    return jnp.concatenate([a * cosine + b * sine, b * cosine - a * sine], axis=-1)


def rms_scale(values):
    return lax.rsqrt(jnp.mean(values * values, axis=-1, keepdims=True) + EPS)


def norm_back(grad, normed, scale):
    return scale * (grad - normed * jnp.mean(grad * normed, axis=-1, keepdims=True))


def mm(a, b):
    return jnp.dot(a, b, preferred_element_type=f32)


def mm_tn(a, b):
    return jnp.einsum("td,te->de", a, b, preferred_element_type=f32)


def mm_nt(a, b):
    return jnp.einsum("te,de->td", a, b, preferred_element_type=f32)


def on_device(
    block_input,
    positions,
    segments,
    out_cotangent,
    attn_gain,
    w_query,
    w_key,
    w_value,
    w_out,
    mlp_gain,
    w_gate,
    w_up,
    w_down,
):
    chips = lax.axis_size("chip")
    rows_z = lax.axis_size("fsdp")
    chip = lax.axis_index("chip")
    core = lax.axis_index("core")
    place = lax.axis_index("fsdp")
    tok = block_input.shape[2]
    width = block_input.shape[3]
    d_rows = w_query.shape[0]
    q_cols = w_query.shape[1] // chips
    kv_cols = w_key.shape[1] // chips
    ff_cols = w_gate.shape[1] // (2 * chips)
    kv_heads = KV_HEADS // chips
    factor = HEAD ** (-0.5)

    def core_swap(a):
        return lax.ppermute(a, "core", [(0, 1), (1, 0)])

    def chip_xor(a, j):
        return lax.ppermute(a, "chip", [(i, i ^ j) for i in range(chips)])

    def pick(a, index, axis=0):
        return lax.dynamic_index_in_dim(a, index, axis, keepdims=False)

    def gather_chips(a, axis=0):
        return jnp.concatenate([a] + [chip_xor(a, j) for j in range(1, chips)], axis=axis)

    def scatter_chips(a):
        step = a.shape[0] // chips
        total = a[:step]
        for j in range(1, chips):
            total = total + chip_xor(a[j * step : (j + 1) * step].astype(bf16), j).astype(f32)
        return total

    def by_chip(pieces):
        stacked = jnp.stack(pieces)
        bit = 1
        while bit < chips:
            view = stacked.reshape((chips // (2 * bit), 2, bit) + stacked.shape[1:])
            flipped = jnp.flip(view, axis=1)
            stacked = jnp.where((chip & bit) != 0, flipped, view).reshape(stacked.shape)
            bit *= 2
        return stacked

    def exchange_chips(pack):
        pieces = [pick(pack, chip)]
        for j in range(1, chips):
            pieces.append(chip_xor(pick(pack, chip ^ j), j))
        return by_chip(pieces)

    def core_pair(mine, other, axis):
        first = core == 0
        return jnp.stack([jnp.where(first, mine, other), jnp.where(first, other, mine)], axis)

    def both_cores(a):
        return core_pair(a, core_swap(a), 0)

    def chip_slices(weights, cols):
        return jnp.stack(
            [
                jnp.concatenate([w[:, k * n : (k + 1) * n] for w, n in zip(weights, cols)], axis=1)
                for k in range(chips)
            ]
        )

    def tie(*values):
        return lax.optimization_barrier(values)

    def along_z(a, step):
        return lax.ppermute(a, "fsdp", [(i, (i + step) % rows_z) for i in range(rows_z)])

    def ring_first(a):
        return along_z(a, 1), along_z(a, -1)

    def ring_rest(a, right, left):
        found = [(a, 0, 0), (right, -1, 0), (left, 1, 0)]
        for step in range(2, rows_z // 2 + 1):
            if 2 * step == rows_z:
                half = a.shape[-1] // 2
                found.append((along_z(right[..., :half], 1), -step, 0))
                found.append((along_z(left[..., half:], -1), step, half))
            else:
                right, left = along_z(right, 1), along_z(left, -1)
                found += [(right, -step, 0), (left, step, 0)]
        return found

    windows = [2 + (rows_z - 1) * w // 3 for w in range(4)]

    def part(a, index, start):
        index = lax.rem(index + 2 * rows_z, rows_z)
        size = (a.shape[0], 1, a.shape[2], a.shape[3] // 2)
        return lax.dynamic_slice(a, (0, index, 0, start), size)

    def scatter_begin(a):
        return part(a, place - 1, 0), part(a, place + 1, a.shape[3] // 2)

    def scatter_window(a, sums, window):
        low, high = sums
        for step in range(windows[window], windows[window + 1]):
            low = along_z(low, 1) + part(a, place - step, 0)
            high = along_z(high, -1) + part(a, place + step, a.shape[3] // 2)
        return low, high

    def assemble(found, groups):
        rows, cols = found[0][0].shape
        whole = jnp.zeros((groups, rows_z, rows // groups, cols), bf16)
        for piece, offset, column in found:
            piece = piece.reshape(groups, 1, rows // groups, piece.shape[-1])
            index = lax.rem(place + offset + rows_z, rows_z)
            whole = lax.dynamic_update_slice(whole, piece, (0, index, 0, column))
        return whole

    owner = (chip * 2 + core) * rows_z + place
    spot = chip * 2 + core
    spots = chips * 2
    gains = lax.dynamic_update_slice(
        jnp.zeros((2, width), f32),
        jnp.stack([attn_gain, mlp_gain]).astype(f32),
        (0, owner * d_rows),
    )
    marks = lax.dynamic_update_slice(
        jnp.zeros((4, spots * tok), f32),
        jnp.concatenate([positions[:, 0], segments[:, 0]]).astype(f32),
        (0, spot * tok),
    )
    table = jnp.concatenate([gains.reshape(-1), marks.reshape(-1)]).reshape(-1, 128)

    def sum_chips(a):
        bit = 1
        while bit < chips:
            a = a + chip_xor(a, bit)
            bit *= 2
        return a

    def sum_z(a, bit=1, end=rows_z):
        while bit < end:
            a = a + lax.ppermute(a, "fsdp", [(i, i ^ bit) for i in range(rows_z)])
            bit *= 2
        return a

    def again(found, pieces):
        return [(piece,) + f[1:] for piece, f in zip(pieces, found)]

    def pieces_of(found):
        return [f[0] for f in found]

    pack_qkv = chip_slices((w_query, w_key, w_value), (q_cols, kv_cols, kv_cols))
    piece_qkv = exchange_chips(pack_qkv).reshape(-1, pack_qkv.shape[-1])
    pair = jnp.stack([block_input[:, 0], out_cotangent[:, 0]], axis=1)
    pair = jnp.concatenate([pick(pair, core), core_swap(pick(pair, 1 - core))], axis=1)
    table = sum_chips(table + core_swap(table))
    rows = jnp.concatenate([w_out, w_down])
    rows = lax.all_gather(rows, "fsdp", axis=0)
    pack_gu = jnp.stack(
        [
            jnp.concatenate([w[:, n * ff_cols : (n + 1) * ff_cols] for w in (w_gate, w_up)], axis=1)
            for n in range(2 * chips)
        ]
    ).reshape(chips, 2, d_rows, 2 * ff_cols)
    pair, piece_qkv, table, pack_gu = tie(pair, piece_qkv, table, pack_gu)
    x_low, dy_low = pair[0], pair[1]

    qkv_right, qkv_left = ring_first(piece_qkv)
    piece_gu = exchange_chips(pack_gu)
    gains = sum_z(table.reshape(-1)[: 2 * width].reshape(2, width), 1, 2)
    qkv_right, qkv_left, piece_gu, x_low, gains = tie(qkv_right, qkv_left, piece_gu, x_low, gains)
    gains = sum_z(gains, 2, rows_z)

    near = [j for j in range(1, chips) if j & (j - 1) == 0]
    far = [j for j in range(1, chips) if j & (j - 1) != 0]
    x_parts = {0: x_low, **{j: chip_xor(x_low, j) for j in near}}
    found_qkv = ring_rest(piece_qkv, qkv_right, qkv_left)
    piece_gu = core_pair(pick(piece_gu, core, 1), core_swap(pick(piece_gu, 1 - core, 1)), 1)
    piece_gu = piece_gu.reshape(2 * chips * d_rows, 2 * ff_cols)
    order = sorted(x_parts)
    piece_gu, gains, *late = tie(piece_gu, gains, *[x_parts[j] for j in order], *pieces_of(found_qkv))
    x_parts = dict(zip(order, late))
    x_parts.update({j: chip_xor(x_parts[0], j) for j in far})
    x_all = jnp.concatenate([x_parts[j] for j in range(chips)])
    found_qkv = again(found_qkv, late[len(order) :])
    gu_right = along_z(piece_gu, 1)
    marks = pick(table.reshape(-1)[2 * width :].reshape(2, 2, spots, tok), core, 1)
    marks = jnp.concatenate(
        [pick(marks, (chip ^ k) * 2 + (core ^ c), 1) for k in range(chips) for c in range(2)],
        axis=1,
    )
    pos_all, seg_all = marks
    allowed = (seg_all[:, None] == seg_all[None, :]) & (pos_all[None, :] <= pos_all[:, None])
    cosine, sine = rope_tables(pos_all)
    w_qkv = assemble(found_qkv, chips)
    w_qkv = core_pair(w_qkv, core_swap(w_qkv), 1).reshape(width, -1)
    w_qkv, x_all, dy_low, cosine, sine, allowed, gu_right, piece_gu, rows = tie(
        w_qkv, x_all, dy_low, cosine, sine, allowed, gu_right, piece_gu, rows
    )
    along_out = rows[:, : w_out.shape[0]].reshape(-1, width)
    along_down = rows[:, w_out.shape[0] :].reshape(-1, width)
    gu_left = along_z(piece_gu, -1)
    gain_one, gain_two = gains
    own = x_low.shape[0]
    seq = x_all.shape[0]

    dy_all = gather_chips(dy_low)
    x_full = x_all.astype(f32)
    h_one = (x_full * rms_scale(x_full) * gain_one).astype(bf16)
    qkv = mm(h_one, w_qkv)
    q_rot = rotate(qkv[:, :q_cols].reshape(seq, kv_heads * 2, HEAD), cosine, sine)
    q_rot = q_rot.astype(bf16).reshape(seq, kv_heads, 2, HEAD)
    k_rot = rotate(
        qkv[:, q_cols : q_cols + kv_cols].reshape(seq, kv_heads, HEAD), cosine, sine
    ).astype(bf16)
    value = qkv[:, q_cols + kv_cols :].astype(bf16).reshape(seq, kv_heads, HEAD)
    out_w = both_cores(along_out).reshape(-1, width)
    scores = jnp.einsum("sgrh,tgh->grst", q_rot, k_rot, preferred_element_type=f32) * factor
    scores = jnp.where(allowed, scores, -1e30)
    raised = jnp.exp(scores - jnp.max(scores, axis=-1, keepdims=True))
    soft = raised / jnp.sum(raised, axis=-1, keepdims=True)
    soft_low = soft.astype(bf16)
    mixed = jnp.einsum("grst,tgh->sgrh", soft_low, value, preferred_element_type=f32)
    mixed = mixed.astype(bf16).reshape(seq, q_cols)
    mixed, dy_all, out_w, gu_left = tie(mixed, dy_all, out_w, gu_left)
    found_gu = ring_rest(piece_gu, gu_right, gu_left)
    x_own = x_low.astype(f32)
    middle = x_own + scatter_chips(mm(mixed, out_w))

    dy_both = jnp.concatenate([dy_all, core_swap(dy_all)])
    middle, dy_both, *late = tie(middle, dy_both, *pieces_of(found_gu))
    found_gu = again(found_gu, late)
    w_gu = assemble(found_gu, 2 * chips).reshape(width, 2 * ff_cols)
    scale_two = rms_scale(middle)
    n_two = middle * scale_two
    h_two = gather_chips((n_two * gain_two).astype(bf16))
    h_two, w_gu = tie(h_two, w_gu)
    h_both = jnp.concatenate([h_two, core_swap(h_two)])
    gu = mm(h_both, w_gu)
    gate, up = gu[:, :ff_cols], gu[:, ff_cols:]
    sigma = jax.nn.sigmoid(gate)
    act = (gate * sigma * up).astype(bf16)
    g_down = mm_tn(act, dy_both).astype(bf16)
    g_down, act = tie(g_down, act)
    g_down = lax.psum_scatter(g_down, "fsdp", scatter_dimension=0, tiled=True)
    d_act = mm_nt(dy_both, along_down)
    d_gate = (d_act * up * sigma * (1.0 + gate * (1.0 - sigma))).astype(bf16)
    d_up = (d_act * gate * sigma).astype(bf16)
    d_gu = jnp.concatenate([d_gate, d_up], axis=1)

    def give_partial(rows, weights, product):
        other = core_swap(product(rows[seq:], weights).astype(bf16)).astype(f32)
        return product(rows[:seq], weights) + other

    d_h_two = give_partial(d_gu, w_gu, mm_nt)
    g_gu = mm_tn(h_both, d_gu).astype(bf16).reshape(2 * chips, rows_z, d_rows, 2 * ff_cols)
    g_gu = jnp.transpose(g_gu, (1, 0, 2, 3)).reshape(width, 2 * ff_cols)
    d_h_two, g_gu = tie(scatter_chips(d_h_two), g_gu)
    g_gu = lax.psum_scatter(g_gu, "fsdp", scatter_dimension=0, tiled=True)

    dy_own = dy_low.astype(f32)
    gain_two_part = jnp.sum(d_h_two * n_two, axis=0)
    d_middle = dy_own + norm_back(d_h_two * gain_two, n_two, scale_two)
    branch = gather_chips(d_middle.astype(bf16))
    partial = give_partial(act, along_down, mm)
    branch, partial, g_down = tie(branch, partial, g_down)
    shares = {
        j: partial[j * own : (j + 1) * own].astype(bf16) if j else partial[:own]
        for j in range(chips)
    }
    shares.update({j: chip_xor(shares[j], j) for j in near})

    g_out = mm_tn(mixed, branch).astype(bf16)
    g_out = g_out.reshape(2, g_out.shape[0] // 2, g_out.shape[1])
    g_out = pick(g_out, core) + core_swap(pick(g_out, 1 - core))
    d_mixed = mm_nt(branch, out_w).astype(bf16).reshape(seq, kv_heads, 2, HEAD)
    d_soft = jnp.einsum("sgrh,tgh->grst", d_mixed, value, preferred_element_type=f32)
    d_value = jnp.einsum("grst,sgrh->tgh", soft_low, d_mixed, preferred_element_type=f32)
    inner = jnp.sum(soft * d_soft, axis=-1, keepdims=True)
    d_scores = (soft * (d_soft - inner)).astype(bf16)
    d_q = jnp.einsum("grst,tgh->sgrh", d_scores, k_rot, preferred_element_type=f32) * factor
    d_q, *late = tie(d_q, *[shares[j] for j in range(chips)])
    shares = dict(enumerate(late))
    shares.update({j: chip_xor(shares[j], j) for j in far})
    d_k = jnp.einsum("grst,sgrh->tgh", d_scores, q_rot, preferred_element_type=f32) * factor
    d_q = unrotate(d_q.reshape(seq, kv_heads * 2, HEAD), cosine, sine)
    d_k = unrotate(d_k, cosine, sine)
    d_qkv = jnp.concatenate(
        [
            d_q.reshape(seq, q_cols).astype(bf16),
            d_k.reshape(seq, kv_cols).astype(bf16),
            d_value.reshape(seq, kv_cols).astype(bf16),
        ],
        axis=1,
    )
    d_qkv, g_out = tie(d_qkv, g_out)
    cols_qkv = d_qkv.shape[1]
    g_qkv = mm_tn(h_one, d_qkv).astype(bf16).reshape(chips, 2, rows_z, d_rows, cols_qkv)
    g_qkv = pick(g_qkv, core, 1) + core_swap(pick(g_qkv, 1 - core, 1))
    g_qkv = jnp.transpose(g_qkv, (1, 0, 2, 3)).reshape(1, rows_z, chips * d_rows, cols_qkv)
    folds = width // cols_qkv
    g_out = g_out.reshape(1, rows_z, d_rows, width)
    g_rest = [g_out[..., k * cols_qkv : (k + 1) * cols_qkv] for k in range(folds)]
    g_rest = jnp.concatenate([g_qkv] + g_rest, axis=2)
    d_h_one = mm_nt(d_qkv, w_qkv)
    result = middle + shares[0]
    for j in range(1, chips):
        result = result + shares[j].astype(f32)
    g_rest, d_h_one, result = tie(g_rest, d_h_one, result.astype(bf16))
    sums = scatter_window(g_rest, scatter_begin(g_rest), 0)
    d_h_one, *sums = tie(scatter_chips(d_h_one), *sums)
    scale_one = rms_scale(x_own)
    n_one = x_own * scale_one
    gain_one_part = jnp.sum(d_h_one * n_one, axis=0)
    gain_parts = jnp.stack([gain_one_part, gain_two_part])
    gain_parts = sum_chips(gain_parts + core_swap(gain_parts))
    gain_parts, *sums = tie(gain_parts, *scatter_window(g_rest, sums, 1))
    sums = scatter_window(g_rest, sums, 2)
    g_rest = jnp.concatenate(sums, axis=-1).reshape(-1, cols_qkv)
    d_input = (d_middle + norm_back(d_h_one * gain_one, n_one, scale_one)).astype(bf16)

    def give_back(a):
        mine, theirs = a[:tok], core_swap(a[tok:])
        first = core == 0
        return jnp.stack([jnp.where(first, mine, theirs), jnp.where(first, theirs, mine)])[:, None]

    def spread(grad, start, cols):
        part = grad[:, :, start : start + cols].astype(f32)
        return jnp.transpose(part, (1, 0, 2)).reshape(d_rows, chips * cols)

    def spread_ff(grad):
        grad = jnp.transpose(grad.astype(f32), (2, 0, 1, 3))
        return grad.reshape(d_rows, 2 * chips * ff_cols)

    g_down = g_down.astype(f32)
    g_gu = g_gu.reshape(chips, 2, d_rows, 2 * ff_cols)
    g_gu = core_pair(pick(g_gu, core, 1), core_swap(pick(g_gu, 1 - core, 1)), 1)
    g_gu = exchange_chips(g_gu)
    g_gate, g_up = spread_ff(g_gu[..., :ff_cols]), spread_ff(g_gu[..., ff_cols:])
    gain_parts = sum_z(gain_parts)
    gain_parts = lax.dynamic_slice_in_dim(gain_parts, owner * d_rows, d_rows, 1)
    result, d_input = give_back(result), give_back(d_input)
    g_rest, g_gate, g_up, g_down, gain_parts, result, d_input = tie(
        g_rest, g_gate, g_up, g_down, gain_parts, result, d_input
    )
    g_qkv = exchange_chips(g_rest[: chips * d_rows].reshape(chips, d_rows, cols_qkv))
    g_out = g_rest[chips * d_rows :].reshape(folds, d_rows, cols_qkv)
    g_out = jnp.transpose(g_out, (1, 0, 2)).reshape(d_rows, width).astype(f32)
    return (
        result,
        d_input,
        gain_parts[0],
        spread(g_qkv, 0, q_cols),
        spread(g_qkv, q_cols, kv_cols),
        spread(g_qkv, q_cols + kv_cols, kv_cols),
        g_out,
        gain_parts[1],
        g_gate,
        g_up,
        g_down,
    )


def solution(mesh):
    ctx, fsdp = mesh.shape["ctx"], mesh.shape["fsdp"]
    split = Mesh(mesh.devices.reshape(ctx // 2, 2, fsdp), ("chip", "core", "fsdp"))
    ctx_axes = ("chip", "core")
    all_axes = ("chip", "core", "fsdp")
    tokens = P(None, "fsdp", ctx_axes, None)
    marks = P(None, "fsdp", ctx_axes)
    vector, matrix = P(all_axes), P(all_axes, None)
    return jax.shard_map(
        on_device,
        mesh=split,
        in_specs=(
            tokens, marks, marks, tokens, vector, matrix, matrix, matrix, matrix,
            vector, matrix, matrix, matrix,
        ),
        out_specs=(
            tokens, tokens, vector, matrix, matrix, matrix, matrix, vector,
            matrix, matrix, matrix,
        ),
        check_vma=False,
    )
```

```python
import math

import jax
import jax.numpy as jnp
from jax import lax
from jax.sharding import Mesh, PartitionSpec as P

HEADS = 16
KV_HEADS = 8
HEAD = 96
EPS = 1e-05
THETA = 100000.0
f32 = jnp.float32
bf16 = jnp.bfloat16


def rope_tables(position_ids):
    half = HEAD // 2
    ladder = jnp.arange(half).astype(f32) * (2.0 / HEAD)
    inverse = jnp.exp(-math.log(THETA) * ladder)
    angles = position_ids.astype(f32)[:, None] * inverse[None, :]
    return jnp.cos(angles)[:, None, :], jnp.sin(angles)[:, None, :]


def rotate(vectors, cosine, sine):
    half = HEAD // 2
    a, b = vectors[..., :half], vectors[..., half:]
    return jnp.concatenate([a * cosine - b * sine, b * cosine + a * sine], axis=-1)


def unrotate(grads, cosine, sine):
    half = HEAD // 2
    a, b = grads[..., :half], grads[..., half:]
    return jnp.concatenate([a * cosine + b * sine, b * cosine - a * sine], axis=-1)


def rms_scale(values):
    return lax.rsqrt(jnp.mean(values * values, axis=-1, keepdims=True) + EPS)


def norm_back(grad, normed, scale):
    return scale * (grad - normed * jnp.mean(grad * normed, axis=-1, keepdims=True))


def mm(a, b):
    return jnp.dot(a, b, preferred_element_type=f32)


def mm_tn(a, b):
    return jnp.einsum("td,te->de", a, b, preferred_element_type=f32)


def mm_nt(a, b):
    return jnp.einsum("te,de->td", a, b, preferred_element_type=f32)


def on_device(
    block_input,
    positions,
    segments,
    out_cotangent,
    attn_gain,
    w_query,
    w_key,
    w_value,
    w_out,
    mlp_gain,
    w_gate,
    w_up,
    w_down,
):
    chips = lax.axis_size("chip")
    rows_z = lax.axis_size("fsdp")
    chip = lax.axis_index("chip")
    core = lax.axis_index("core")
    place = lax.axis_index("fsdp")
    tok = block_input.shape[2]
    width = block_input.shape[3]
    d_rows = w_query.shape[0]
    q_cols = w_query.shape[1] // chips
    kv_cols = w_key.shape[1] // chips
    ff_cols = w_gate.shape[1] // (2 * chips)
    kv_heads = KV_HEADS // chips
    factor = HEAD ** (-0.5)

    def core_swap(a):
        return lax.ppermute(a, "core", [(0, 1), (1, 0)])

    def chip_xor(a, j):
        return lax.ppermute(a, "chip", [(i, i ^ j) for i in range(chips)])

    def pick(a, index, axis=0):
        return lax.dynamic_index_in_dim(a, index, axis, keepdims=False)

    def gather_chips(a, axis=0):
        return jnp.concatenate([a] + [chip_xor(a, j) for j in range(1, chips)], axis=axis)

    def scatter_chips(a):
        step = a.shape[0] // chips
        total = a[:step]
        for j in range(1, chips):
            total = total + chip_xor(a[j * step : (j + 1) * step].astype(bf16), j).astype(f32)
        return total

    def by_chip(pieces):
        stacked = jnp.stack(pieces)
        bit = 1
        while bit < chips:
            view = stacked.reshape((chips // (2 * bit), 2, bit) + stacked.shape[1:])
            flipped = jnp.flip(view, axis=1)
            stacked = jnp.where((chip & bit) != 0, flipped, view).reshape(stacked.shape)
            bit *= 2
        return stacked

    def exchange_chips(pack):
        pieces = [pick(pack, chip)]
        for j in range(1, chips):
            pieces.append(chip_xor(pick(pack, chip ^ j), j))
        return by_chip(pieces)

    def core_pair(mine, other, axis):
        first = core == 0
        return jnp.stack([jnp.where(first, mine, other), jnp.where(first, other, mine)], axis)

    def both_cores(a):
        return core_pair(a, core_swap(a), 0)

    def chip_slices(weights, cols):
        return jnp.stack(
            [
                jnp.concatenate([w[:, k * n : (k + 1) * n] for w, n in zip(weights, cols)], axis=1)
                for k in range(chips)
            ]
        )

    def tie(*values):
        return lax.optimization_barrier(values)

    def along_z(a, step):
        return lax.ppermute(a, "fsdp", [(i, (i + step) % rows_z) for i in range(rows_z)])

    def ring_first(a):
        return along_z(a, 1), along_z(a, -1)

    def ring_rest(a, right, left):
        found = [(a, 0, 0), (right, -1, 0), (left, 1, 0)]
        for step in range(2, rows_z // 2 + 1):
            if 2 * step == rows_z:
                half = a.shape[-1] // 2
                found.append((along_z(right[..., :half], 1), -step, 0))
                found.append((along_z(left[..., half:], -1), step, half))
            else:
                right, left = along_z(right, 1), along_z(left, -1)
                found += [(right, -step, 0), (left, step, 0)]
        return found

    windows = [2 + (rows_z - 1) * w // 3 for w in range(4)]

    def part(a, index, start):
        index = lax.rem(index + 2 * rows_z, rows_z)
        size = (a.shape[0], 1, a.shape[2], a.shape[3] // 2)
        return lax.dynamic_slice(a, (0, index, 0, start), size)

    def scatter_begin(a):
        return part(a, place - 1, 0), part(a, place + 1, a.shape[3] // 2)

    def scatter_window(a, sums, window):
        low, high = sums
        for step in range(windows[window], windows[window + 1]):
            low = along_z(low, 1) + part(a, place - step, 0)
            high = along_z(high, -1) + part(a, place + step, a.shape[3] // 2)
        return low, high

    def assemble(found, groups):
        rows, cols = found[0][0].shape
        whole = jnp.zeros((groups, rows_z, rows // groups, cols), bf16)
        for piece, offset, column in found:
            piece = piece.reshape(groups, 1, rows // groups, piece.shape[-1])
            index = lax.rem(place + offset + rows_z, rows_z)
            whole = lax.dynamic_update_slice(whole, piece, (0, index, 0, column))
        return whole

    def again(found, pieces):
        return [(piece,) + f[1:] for piece, f in zip(pieces, found)]

    def pieces_of(found):
        return [f[0] for f in found]

    def scaled(gain, *weights):
        return [(w.astype(f32) * gain.astype(f32)[:, None]).astype(bf16) for w in weights]

    pack_qkv = chip_slices(
        scaled(attn_gain, w_query, w_key, w_value), (q_cols, kv_cols, kv_cols)
    )
    piece_qkv = exchange_chips(pack_qkv).reshape(-1, pack_qkv.shape[-1])
    marks = jnp.stack([positions[:, 0] // 32, positions[:, 0] % 32, segments[:, 0]], axis=-1)
    marks = jnp.pad(marks.astype(bf16), ((0, 0), (0, 0), (0, 125)))
    pair = jnp.concatenate([out_cotangent[:, 0], block_input[:, 0], marks], axis=-1)
    pair = jnp.concatenate([pick(pair, core), core_swap(pick(pair, 1 - core))])
    rows = jnp.concatenate([w_out, w_down])
    gate_up = scaled(mlp_gain, w_gate, w_up)
    pack_gu = jnp.stack(
        [
            jnp.concatenate([w[:, n * ff_cols : (n + 1) * ff_cols] for w in gate_up], axis=1)
            for n in range(2 * chips)
        ]
    ).reshape(chips, 2, d_rows, 2 * ff_cols)
    pair, piece_qkv, pack_gu = tie(pair, piece_qkv, pack_gu)
    dy_low, x_low = pair[:, :width], pair[:, width:]

    qkv_right, qkv_left = ring_first(piece_qkv)
    piece_gu = exchange_chips(pack_gu)
    qkv_right, qkv_left, piece_gu, x_low, rows = tie(qkv_right, qkv_left, piece_gu, x_low, rows)
    rows = lax.all_gather(rows, "fsdp", axis=0)

    near = [j for j in range(1, chips) if j & (j - 1) == 0]
    far = [j for j in range(1, chips) if j & (j - 1) != 0]
    x_parts = {0: x_low, **{j: chip_xor(x_low, j) for j in near}}
    found_qkv = ring_rest(piece_qkv, qkv_right, qkv_left)
    piece_gu = core_pair(pick(piece_gu, core, 1), core_swap(pick(piece_gu, 1 - core, 1)), 1)
    piece_gu = piece_gu.reshape(2 * chips * d_rows, 2 * ff_cols)
    order = sorted(x_parts)
    piece_gu, *late = tie(piece_gu, *[x_parts[j] for j in order], *pieces_of(found_qkv))
    x_parts = dict(zip(order, late))
    x_parts.update({j: chip_xor(x_parts[0], j) for j in far})
    x_all = jnp.concatenate([x_parts[j] for j in range(chips)])
    found_qkv = again(found_qkv, late[len(order) :])
    gu_right = along_z(piece_gu, 1)
    marks = x_all[:, width : width + 3].astype(f32).T
    pos_all, seg_all = marks[0] * 32.0 + marks[1], marks[2]
    x_all, x_low = x_all[:, :width], x_low[:, :width]
    allowed = (seg_all[:, None] == seg_all[None, :]) & (pos_all[None, :] <= pos_all[:, None])
    cosine, sine = rope_tables(pos_all)
    w_qkv = assemble(found_qkv, chips)
    w_qkv = core_pair(w_qkv, core_swap(w_qkv), 1).reshape(width, -1)
    w_qkv, x_all, dy_low, cosine, sine, allowed = tie(w_qkv, x_all, dy_low, cosine, sine, allowed)
    own = x_low.shape[0]
    seq = x_all.shape[0]

    dy_all = gather_chips(dy_low)
    x_full = x_all.astype(f32)
    h_one = (x_full * rms_scale(x_full)).astype(bf16)
    qkv = mm(h_one, w_qkv)
    q_rot = rotate(qkv[:, :q_cols].reshape(seq, kv_heads * 2, HEAD), cosine, sine)
    q_rot = q_rot.astype(bf16).reshape(seq, kv_heads, 2, HEAD)
    k_rot = rotate(
        qkv[:, q_cols : q_cols + kv_cols].reshape(seq, kv_heads, HEAD), cosine, sine
    ).astype(bf16)
    value = qkv[:, q_cols + kv_cols :].astype(bf16).reshape(seq, kv_heads, HEAD)
    q_rot, gu_right, piece_gu, rows = tie(q_rot, gu_right, piece_gu, rows)
    gu_left = along_z(piece_gu, -1)
    along_out = rows[:, : w_out.shape[0]].reshape(-1, width)
    along_down = rows[:, w_out.shape[0] :].reshape(-1, width)
    out_w = both_cores(along_out).reshape(-1, width)
    scores = jnp.einsum("sgrh,tgh->grst", q_rot, k_rot, preferred_element_type=f32) * factor
    scores = jnp.where(allowed, scores, -1e30)
    raised = jnp.exp(scores - jnp.max(scores, axis=-1, keepdims=True))
    soft = raised / jnp.sum(raised, axis=-1, keepdims=True)
    soft_low = soft.astype(bf16)
    mixed = jnp.einsum("grst,tgh->sgrh", soft_low, value, preferred_element_type=f32)
    mixed = mixed.astype(bf16).reshape(seq, q_cols)
    mixed, dy_all, out_w, gu_left = tie(mixed, dy_all, out_w, gu_left)
    found_gu = ring_rest(piece_gu, gu_right, gu_left)
    x_own = x_low.astype(f32)
    middle = x_own + scatter_chips(mm(mixed, out_w))

    dy_both = jnp.concatenate([dy_all, core_swap(dy_all)])
    middle, dy_both, *late = tie(middle, dy_both, *pieces_of(found_gu))
    found_gu = again(found_gu, late)
    w_gu = assemble(found_gu, 2 * chips).reshape(width, 2 * ff_cols)
    scale_two = rms_scale(middle)
    n_two = middle * scale_two
    h_two = gather_chips(n_two.astype(bf16))
    h_two, w_gu = tie(h_two, w_gu)
    h_both = jnp.concatenate([h_two, core_swap(h_two)])
    gu = mm(h_both, w_gu)
    gate, up = gu[:, :ff_cols], gu[:, ff_cols:]
    sigma = jax.nn.sigmoid(gate)
    act = (gate * sigma * up).astype(bf16)
    g_down = mm_tn(act, dy_both).astype(bf16)
    g_down, act = tie(g_down, act)
    g_down = lax.psum_scatter(g_down, "fsdp", scatter_dimension=0, tiled=True)
    d_act = mm_nt(dy_both, along_down)
    d_gate = (d_act * up * sigma * (1.0 + gate * (1.0 - sigma))).astype(bf16)
    d_up = (d_act * gate * sigma).astype(bf16)
    d_gu = jnp.concatenate([d_gate, d_up], axis=1)

    def give_partial(rows, weights, product):
        other = core_swap(product(rows[seq:], weights).astype(bf16)).astype(f32)
        return product(rows[:seq], weights) + other

    d_h_two = give_partial(d_gu, w_gu, mm_nt)
    g_gu = mm_tn(h_both, d_gu).astype(bf16).reshape(2 * chips, rows_z, d_rows, 2 * ff_cols)
    g_gu = jnp.transpose(g_gu, (1, 0, 2, 3)).reshape(width, 2 * ff_cols)
    d_h_two, g_gu = tie(scatter_chips(d_h_two), g_gu)
    g_gu = lax.psum_scatter(g_gu, "fsdp", scatter_dimension=0, tiled=True)

    dy_own = dy_low.astype(f32)
    d_middle = dy_own + norm_back(d_h_two, n_two, scale_two)
    branch = gather_chips(d_middle.astype(bf16))
    partial = give_partial(act, along_down, mm)
    branch, partial, g_down = tie(branch, partial, g_down)
    shares = {
        j: partial[j * own : (j + 1) * own].astype(bf16) if j else partial[:own]
        for j in range(chips)
    }
    shares.update({j: chip_xor(shares[j], j) for j in near})

    g_out = mm_tn(mixed, branch).astype(bf16)
    g_out = g_out.reshape(2, g_out.shape[0] // 2, g_out.shape[1])
    g_out = pick(g_out, core) + core_swap(pick(g_out, 1 - core))
    d_mixed = mm_nt(branch, out_w).astype(bf16).reshape(seq, kv_heads, 2, HEAD)
    d_soft = jnp.einsum("sgrh,tgh->grst", d_mixed, value, preferred_element_type=f32)
    d_value = jnp.einsum("grst,sgrh->tgh", soft_low, d_mixed, preferred_element_type=f32)
    inner = jnp.sum(soft * d_soft, axis=-1, keepdims=True)
    d_scores = (soft * (d_soft - inner)).astype(bf16)
    d_q = jnp.einsum("grst,tgh->sgrh", d_scores, k_rot, preferred_element_type=f32) * factor
    d_q, *late = tie(d_q, *[shares[j] for j in range(chips)])
    shares = dict(enumerate(late))
    shares.update({j: chip_xor(shares[j], j) for j in far})
    d_k = jnp.einsum("grst,sgrh->tgh", d_scores, q_rot, preferred_element_type=f32) * factor
    d_q = unrotate(d_q.reshape(seq, kv_heads * 2, HEAD), cosine, sine)
    d_k = unrotate(d_k, cosine, sine)
    d_qkv = jnp.concatenate(
        [
            d_q.reshape(seq, q_cols).astype(bf16),
            d_k.reshape(seq, kv_cols).astype(bf16),
            d_value.reshape(seq, kv_cols).astype(bf16),
        ],
        axis=1,
    )
    d_qkv, g_out = tie(d_qkv, g_out)
    cols_qkv = d_qkv.shape[1]
    g_qkv = mm_tn(h_one, d_qkv).astype(bf16).reshape(chips, 2, rows_z, d_rows, cols_qkv)
    g_qkv = pick(g_qkv, core, 1) + core_swap(pick(g_qkv, 1 - core, 1))
    g_qkv = jnp.transpose(g_qkv, (1, 0, 2, 3)).reshape(1, rows_z, chips * d_rows, cols_qkv)
    folds = width // cols_qkv
    g_out = g_out.reshape(1, rows_z, d_rows, width)
    g_rest = [g_out[..., k * cols_qkv : (k + 1) * cols_qkv] for k in range(folds)]
    g_rest = jnp.concatenate([g_qkv] + g_rest, axis=2)
    d_h_one = mm_nt(d_qkv, w_qkv)
    result = middle + shares[0]
    for j in range(1, chips):
        result = result + shares[j].astype(f32)
    g_rest, d_h_one, result = tie(g_rest, d_h_one, result.astype(bf16))
    sums = scatter_window(g_rest, scatter_begin(g_rest), 0)
    d_h_one, *sums = tie(scatter_chips(d_h_one), *sums)
    scale_one = rms_scale(x_own)
    n_one = x_own * scale_one
    sums = scatter_window(g_rest, sums, 1)
    sums = scatter_window(g_rest, sums, 2)
    g_rest = jnp.concatenate(sums, axis=-1).reshape(-1, cols_qkv)
    d_input = (d_middle + norm_back(d_h_one, n_one, scale_one)).astype(bf16)

    def give_back(a):
        mine, theirs = a[:tok], core_swap(a[tok:])
        first = core == 0
        return jnp.stack([jnp.where(first, mine, theirs), jnp.where(first, theirs, mine)])[:, None]

    def spread(grad, start, cols):
        part = grad[:, :, start : start + cols].astype(f32)
        return jnp.transpose(part, (1, 0, 2)).reshape(d_rows, chips * cols)

    def spread_ff(grad):
        grad = jnp.transpose(grad.astype(f32), (2, 0, 1, 3))
        return grad.reshape(d_rows, 2 * chips * ff_cols)

    g_down = g_down.astype(f32)
    g_gu = g_gu.reshape(chips, 2, d_rows, 2 * ff_cols)
    g_gu = core_pair(pick(g_gu, core, 1), core_swap(pick(g_gu, 1 - core, 1)), 1)
    g_gu = exchange_chips(g_gu)
    g_gate, g_up = spread_ff(g_gu[..., :ff_cols]), spread_ff(g_gu[..., ff_cols:])

    def of_gain(grads, weights):
        return sum(jnp.sum(g * w.astype(f32), axis=1) for g, w in zip(grads, weights))

    def by_gain(gain, grads):
        return [g * gain.astype(f32)[:, None] for g in grads]

    g_mlp_gain = of_gain((g_gate, g_up), (w_gate, w_up))
    g_gate, g_up = by_gain(mlp_gain, (g_gate, g_up))
    result, d_input = give_back(result), give_back(d_input)
    g_rest, g_gate, g_up, g_down, g_mlp_gain, result, d_input = tie(
        g_rest, g_gate, g_up, g_down, g_mlp_gain, result, d_input
    )
    g_qkv = exchange_chips(g_rest[: chips * d_rows].reshape(chips, d_rows, cols_qkv))
    g_out = g_rest[chips * d_rows :].reshape(folds, d_rows, cols_qkv)
    g_out = jnp.transpose(g_out, (1, 0, 2)).reshape(d_rows, width).astype(f32)
    g_query = spread(g_qkv, 0, q_cols)
    g_key = spread(g_qkv, q_cols, kv_cols)
    g_value = spread(g_qkv, q_cols + kv_cols, kv_cols)
    g_attn_gain = of_gain((g_query, g_key, g_value), (w_query, w_key, w_value))
    g_query, g_key, g_value = by_gain(attn_gain, (g_query, g_key, g_value))
    return (
        result,
        d_input,
        g_attn_gain,
        g_query,
        g_key,
        g_value,
        g_out,
        g_mlp_gain,
        g_gate,
        g_up,
        g_down,
    )


def solution(mesh):
    ctx, fsdp = mesh.shape["ctx"], mesh.shape["fsdp"]
    split = Mesh(mesh.devices.reshape(ctx // 2, 2, fsdp), ("chip", "core", "fsdp"))
    ctx_axes = ("chip", "core")
    all_axes = ("chip", "core", "fsdp")
    tokens = P(None, "fsdp", ctx_axes, None)
    marks = P(None, "fsdp", ctx_axes)
    vector, matrix = P(all_axes), P(all_axes, None)
    return jax.shard_map(
        on_device,
        mesh=split,
        in_specs=(
            tokens, marks, marks, tokens, vector, matrix, matrix, matrix, matrix,
            vector, matrix, matrix, matrix,
        ),
        out_specs=(
            tokens, tokens, vector, matrix, matrix, matrix, matrix, vector,
            matrix, matrix, matrix,
        ),
        check_vma=False,
    )
```

```python
import math

import jax
import jax.numpy as jnp
from jax import lax
from jax.sharding import Mesh, PartitionSpec as P

HEADS = 16
KV_HEADS = 8
HEAD = 96
EPS = 1e-05
THETA = 100000.0
f32 = jnp.float32
bf16 = jnp.bfloat16


def rope_tables(position_ids):
    half = HEAD // 2
    ladder = jnp.arange(half).astype(f32) * (2.0 / HEAD)
    inverse = jnp.exp(-math.log(THETA) * ladder)
    angles = position_ids.astype(f32)[:, None] * inverse[None, :]
    return jnp.cos(angles)[:, None, :], jnp.sin(angles)[:, None, :]


def rotate(vectors, cosine, sine):
    half = HEAD // 2
    a, b = vectors[..., :half], vectors[..., half:]
    return jnp.concatenate([a * cosine - b * sine, b * cosine + a * sine], axis=-1)


def unrotate(grads, cosine, sine):
    half = HEAD // 2
    a, b = grads[..., :half], grads[..., half:]
    return jnp.concatenate([a * cosine + b * sine, b * cosine - a * sine], axis=-1)


def rms_scale(values):
    return lax.rsqrt(jnp.mean(values * values, axis=-1, keepdims=True) + EPS)


def norm_back(grad, normed, scale):
    return scale * (grad - normed * jnp.mean(grad * normed, axis=-1, keepdims=True))


def mm(a, b):
    return jnp.dot(a, b, preferred_element_type=f32)


def mm_tn(a, b):
    return jnp.einsum("td,te->de", a, b, preferred_element_type=f32)


def mm_nt(a, b):
    return jnp.einsum("te,de->td", a, b, preferred_element_type=f32)


def on_device(
    block_input,
    positions,
    segments,
    out_cotangent,
    attn_gain,
    w_query,
    w_key,
    w_value,
    w_out,
    mlp_gain,
    w_gate,
    w_up,
    w_down,
):
    chips = lax.axis_size("chip")
    rows_z = lax.axis_size("fsdp")
    chip = lax.axis_index("chip")
    core = lax.axis_index("core")
    place = lax.axis_index("fsdp")
    tok = block_input.shape[2]
    width = block_input.shape[3]
    d_rows = w_query.shape[0]
    q_cols = w_query.shape[1] // chips
    kv_cols = w_key.shape[1] // chips
    ff_cols = w_gate.shape[1] // (2 * chips)
    kv_heads = KV_HEADS // chips
    factor = HEAD ** (-0.5)

    def core_swap(a):
        return lax.ppermute(a, "core", [(0, 1), (1, 0)])

    def chip_xor(a, j):
        return lax.ppermute(a, "chip", [(i, i ^ j) for i in range(chips)])

    def pick(a, index, axis=0):
        return lax.dynamic_index_in_dim(a, index, axis, keepdims=False)

    def gather_chips(a, axis=0):
        return jnp.concatenate([a] + [chip_xor(a, j) for j in range(1, chips)], axis=axis)

    def scatter_chips(a):
        step = a.shape[0] // chips
        total = a[:step]
        for j in range(1, chips):
            total = total + chip_xor(a[j * step : (j + 1) * step].astype(bf16), j).astype(f32)
        return total

    def by_chip(pieces):
        stacked = jnp.stack(pieces)
        bit = 1
        while bit < chips:
            view = stacked.reshape((chips // (2 * bit), 2, bit) + stacked.shape[1:])
            flipped = jnp.flip(view, axis=1)
            stacked = jnp.where((chip & bit) != 0, flipped, view).reshape(stacked.shape)
            bit *= 2
        return stacked

    def exchange_chips(pack):
        pieces = [pick(pack, chip)]
        for j in range(1, chips):
            pieces.append(chip_xor(pick(pack, chip ^ j), j))
        return by_chip(pieces)

    def core_pair(mine, other, axis):
        first = core == 0
        return jnp.stack([jnp.where(first, mine, other), jnp.where(first, other, mine)], axis)

    def both_cores(a):
        return core_pair(a, core_swap(a), 0)

    def chip_slices(weights, cols):
        return jnp.stack(
            [
                jnp.concatenate([w[:, k * n : (k + 1) * n] for w, n in zip(weights, cols)], axis=1)
                for k in range(chips)
            ]
        )

    def tie(*values):
        return lax.optimization_barrier(values)

    def along_z(a, step):
        return lax.ppermute(a, "fsdp", [(i, (i + step) % rows_z) for i in range(rows_z)])

    def ring_first(a):
        return along_z(a, 1), along_z(a, -1)

    def ring_rest(a, right, left):
        found = [(a, 0, 0), (right, -1, 0), (left, 1, 0)]
        for step in range(2, rows_z // 2 + 1):
            if 2 * step == rows_z:
                half = a.shape[-1] // 2
                found.append((along_z(right[..., :half], 1), -step, 0))
                found.append((along_z(left[..., half:], -1), step, half))
            else:
                right, left = along_z(right, 1), along_z(left, -1)
                found += [(right, -step, 0), (left, step, 0)]
        return found

    windows = [2 + (rows_z - 1) * w // 3 for w in range(4)]

    def part(a, index, start):
        index = lax.rem(index + 2 * rows_z, rows_z)
        size = (a.shape[0], 1, a.shape[2], a.shape[3] // 2)
        return lax.dynamic_slice(a, (0, index, 0, start), size)

    def scatter_begin(a):
        return part(a, place - 1, 0), part(a, place + 1, a.shape[3] // 2)

    def scatter_window(a, sums, window):
        low, high = sums
        for step in range(windows[window], windows[window + 1]):
            low = along_z(low, 1) + part(a, place - step, 0)
            high = along_z(high, -1) + part(a, place + step, a.shape[3] // 2)
        return low, high

    def assemble(found, groups):
        rows, cols = found[0][0].shape
        whole = jnp.zeros((groups, rows_z, rows // groups, cols), bf16)
        for piece, offset, column in found:
            piece = piece.reshape(groups, 1, rows // groups, piece.shape[-1])
            index = lax.rem(place + offset + rows_z, rows_z)
            whole = lax.dynamic_update_slice(whole, piece, (0, index, 0, column))
        return whole

    def again(found, pieces):
        return [(piece,) + f[1:] for piece, f in zip(pieces, found)]

    def pieces_of(found):
        return [f[0] for f in found]

    def scaled(gain, *weights):
        return [(w.astype(f32) * gain.astype(f32)[:, None]).astype(bf16) for w in weights]

    pack_qkv = chip_slices(
        scaled(attn_gain, w_query, w_key, w_value), (q_cols, kv_cols, kv_cols)
    )
    piece_qkv = exchange_chips(pack_qkv).reshape(-1, pack_qkv.shape[-1])
    marks = jnp.stack([positions[:, 0] // 32, positions[:, 0] % 32, segments[:, 0]], axis=-1)
    marks = jnp.pad(marks.astype(bf16), ((0, 0), (0, 0), (0, 125)))
    pair = jnp.concatenate([out_cotangent[:, 0], block_input[:, 0], marks], axis=-1)
    pair = jnp.concatenate([pick(pair, core), core_swap(pick(pair, 1 - core))])
    rows = jnp.concatenate([w_out, w_down])
    gate_up = scaled(mlp_gain, w_gate, w_up)
    pack_gu = jnp.stack(
        [
            jnp.concatenate([w[:, n * ff_cols : (n + 1) * ff_cols] for w in gate_up], axis=1)
            for n in range(2 * chips)
        ]
    ).reshape(chips, 2, d_rows, 2 * ff_cols)
    pair, piece_qkv, pack_gu = tie(pair, piece_qkv, pack_gu)
    dy_low, x_low = pair[:, :width], pair[:, width:]

    qkv_right, qkv_left = ring_first(piece_qkv)
    piece_gu = exchange_chips(pack_gu)
    qkv_right, qkv_left, piece_gu, x_low, rows = tie(qkv_right, qkv_left, piece_gu, x_low, rows)
    rows = lax.all_gather(rows, "fsdp", axis=0)

    near = [j for j in range(1, chips) if j & (j - 1) == 0]
    far = [j for j in range(1, chips) if j & (j - 1) != 0]
    x_parts = {0: x_low, **{j: chip_xor(x_low, j) for j in near}}
    found_qkv = ring_rest(piece_qkv, qkv_right, qkv_left)
    piece_gu = core_pair(pick(piece_gu, core, 1), core_swap(pick(piece_gu, 1 - core, 1)), 1)
    piece_gu = piece_gu.reshape(2 * chips * d_rows, 2 * ff_cols)
    order = sorted(x_parts)
    piece_gu, *late = tie(piece_gu, *[x_parts[j] for j in order], *pieces_of(found_qkv))
    x_parts = dict(zip(order, late))
    x_parts.update({j: chip_xor(x_low, j) for j in far})
    x_all = jnp.concatenate([x_parts[j] for j in range(chips)])
    found_qkv = again(found_qkv, late[len(order) :])
    marks = x_all[:, width : width + 3].astype(f32).T
    pos_all, seg_all = marks[0] * 32.0 + marks[1], marks[2]
    x_all, x_low = x_all[:, :width], x_low[:, :width]
    allowed = (seg_all[:, None] == seg_all[None, :]) & (pos_all[None, :] <= pos_all[:, None])
    cosine, sine = rope_tables(pos_all)
    w_qkv = assemble(found_qkv, chips)
    w_qkv = core_pair(w_qkv, core_swap(w_qkv), 1).reshape(width, -1)
    w_qkv, x_all, dy_low, cosine, sine, allowed = tie(w_qkv, x_all, dy_low, cosine, sine, allowed)
    own = x_low.shape[0]
    seq = x_all.shape[0]

    dy_all = gather_chips(dy_low)
    x_full = x_all.astype(f32)
    h_one = (x_full * rms_scale(x_full)).astype(bf16)
    qkv = mm(h_one, w_qkv)
    q_rot = rotate(qkv[:, :q_cols].reshape(seq, kv_heads * 2, HEAD), cosine, sine)
    q_rot = q_rot.astype(bf16).reshape(seq, kv_heads, 2, HEAD)
    k_rot = rotate(
        qkv[:, q_cols : q_cols + kv_cols].reshape(seq, kv_heads, HEAD), cosine, sine
    ).astype(bf16)
    value = qkv[:, q_cols + kv_cols :].astype(bf16).reshape(seq, kv_heads, HEAD)
    scores = jnp.einsum("sgrh,tgh->grst", q_rot, k_rot, preferred_element_type=f32) * factor
    scores = jnp.where(allowed, scores, -1e30)
    raised = jnp.exp(scores - jnp.max(scores, axis=-1, keepdims=True))
    soft = raised / jnp.sum(raised, axis=-1, keepdims=True)
    soft_low, rows = tie(soft.astype(bf16), rows)
    along_out = rows[:, : w_out.shape[0]].reshape(-1, width)
    along_down = rows[:, w_out.shape[0] :].reshape(-1, width)
    out_w = both_cores(along_out).reshape(-1, width)
    mixed = jnp.einsum("grst,tgh->sgrh", soft_low, value, preferred_element_type=f32)
    mixed = mixed.astype(bf16).reshape(seq, q_cols)
    mixed, dy_all, out_w = tie(mixed, dy_all, out_w)
    x_own = x_low.astype(f32)
    middle = x_own + scatter_chips(mm(mixed, out_w))

    dy_both = jnp.concatenate([dy_all, core_swap(dy_all)])
    along_gu = lax.all_gather(piece_gu, "fsdp", axis=0, tiled=True)
    middle, dy_both = tie(middle, dy_both)
    scale_two = rms_scale(middle)
    n_two = middle * scale_two
    h_two = gather_chips(n_two.astype(bf16))
    h_both, along_gu = tie(jnp.concatenate([h_two, core_swap(h_two)]), along_gu)
    w_gu = along_gu.reshape(rows_z, 2 * chips, d_rows, 2 * ff_cols)
    w_gu = jnp.transpose(w_gu, (1, 0, 2, 3)).reshape(width, 2 * ff_cols)
    gu = mm(h_both, w_gu)
    gate, up = gu[:, :ff_cols], gu[:, ff_cols:]
    sigma = jax.nn.sigmoid(gate)
    act = (gate * sigma * up).astype(bf16)
    d_act = mm_nt(dy_both, along_down)
    d_gate = (d_act * up * sigma * (1.0 + gate * (1.0 - sigma))).astype(bf16)
    d_up = (d_act * gate * sigma).astype(bf16)
    d_gu = jnp.concatenate([d_gate, d_up], axis=1)
    g_down = mm_tn(act, dy_both).astype(bf16)
    g_down, d_gu = tie(g_down, d_gu)
    g_down = lax.psum_scatter(g_down, "fsdp", scatter_dimension=0, tiled=True)

    def give_partial(rows, weights, product):
        other = core_swap(product(rows[seq:], weights).astype(bf16)).astype(f32)
        return product(rows[:seq], weights) + other

    d_h_two = give_partial(d_gu, w_gu, mm_nt)
    g_gu = mm_tn(h_both, d_gu).astype(bf16).reshape(2 * chips, rows_z, d_rows, 2 * ff_cols)
    g_gu = jnp.transpose(g_gu, (1, 0, 2, 3)).reshape(width, 2 * ff_cols)
    d_h_two, g_gu, act = tie(scatter_chips(d_h_two), g_gu, act)
    g_gu = lax.psum_scatter(g_gu, "fsdp", scatter_dimension=0, tiled=True)

    dy_own = dy_low.astype(f32)
    d_middle = dy_own + norm_back(d_h_two, n_two, scale_two)
    branch = gather_chips(d_middle.astype(bf16))
    partial = give_partial(act, along_down, mm)
    kept, given = partial[:own], partial[own:].astype(bf16)
    branch, kept, given, g_down = tie(branch, kept, given, g_down)
    shares = {j: given[(j - 1) * own : j * own] if j else kept for j in range(chips)}
    shares.update({j: chip_xor(shares[j], j) for j in near})

    g_out = mm_tn(mixed, branch).astype(bf16)
    g_out = g_out.reshape(2, g_out.shape[0] // 2, g_out.shape[1])
    g_out = pick(g_out, core) + core_swap(pick(g_out, 1 - core))
    d_mixed = mm_nt(branch, out_w).astype(bf16).reshape(seq, kv_heads, 2, HEAD)
    d_soft = jnp.einsum("sgrh,tgh->grst", d_mixed, value, preferred_element_type=f32)
    d_value = jnp.einsum("grst,sgrh->tgh", soft_low, d_mixed, preferred_element_type=f32)
    inner = jnp.sum(soft * d_soft, axis=-1, keepdims=True)
    d_scores = (soft * (d_soft - inner)).astype(bf16)
    d_q = jnp.einsum("grst,tgh->sgrh", d_scores, k_rot, preferred_element_type=f32) * factor
    d_q, *late = tie(d_q, *[shares[j] for j in range(chips)])
    shares = dict(enumerate(late))
    shares.update({j: chip_xor(shares[j], j) for j in far})
    d_k = jnp.einsum("grst,sgrh->tgh", d_scores, q_rot, preferred_element_type=f32) * factor
    d_q = unrotate(d_q.reshape(seq, kv_heads * 2, HEAD), cosine, sine)
    d_k = unrotate(d_k, cosine, sine)
    d_qkv = jnp.concatenate(
        [
            d_q.reshape(seq, q_cols).astype(bf16),
            d_k.reshape(seq, kv_cols).astype(bf16),
            d_value.reshape(seq, kv_cols).astype(bf16),
        ],
        axis=1,
    )
    d_qkv, g_out = tie(d_qkv, g_out)
    cols_qkv = d_qkv.shape[1]
    g_qkv = mm_tn(h_one, d_qkv).astype(bf16).reshape(chips, 2, rows_z, d_rows, cols_qkv)
    g_qkv = pick(g_qkv, core, 1) + core_swap(pick(g_qkv, 1 - core, 1))
    g_qkv = jnp.transpose(g_qkv, (1, 0, 2, 3)).reshape(1, rows_z, chips * d_rows, cols_qkv)
    folds = width // cols_qkv
    g_out = g_out.reshape(1, rows_z, d_rows, width)
    g_rest = [g_out[..., k * cols_qkv : (k + 1) * cols_qkv] for k in range(folds)]
    g_rest = jnp.concatenate([g_qkv] + g_rest, axis=2)
    d_h_one = mm_nt(d_qkv, w_qkv)
    result = middle + shares[0]
    for j in range(1, chips):
        result = result + shares[j].astype(f32)
    g_rest, d_h_one, result = tie(g_rest, d_h_one, result.astype(bf16))
    sums = scatter_window(g_rest, scatter_begin(g_rest), 0)
    d_h_one, *sums = tie(scatter_chips(d_h_one), *sums)
    scale_one = rms_scale(x_own)
    n_one = x_own * scale_one
    sums = scatter_window(g_rest, sums, 1)
    sums = scatter_window(g_rest, sums, 2)
    g_rest = jnp.concatenate(sums, axis=-1).reshape(-1, cols_qkv)
    d_input = (d_middle + norm_back(d_h_one, n_one, scale_one)).astype(bf16)

    def give_back(a):
        mine, theirs = a[:tok], core_swap(a[tok:])
        first = core == 0
        return jnp.stack([jnp.where(first, mine, theirs), jnp.where(first, theirs, mine)])[:, None]

    def spread(grad, start, cols):
        part = grad[:, :, start : start + cols].astype(f32)
        return jnp.transpose(part, (1, 0, 2)).reshape(d_rows, chips * cols)

    def spread_ff(grad):
        grad = jnp.transpose(grad.astype(f32), (2, 0, 1, 3))
        return grad.reshape(d_rows, 2 * chips * ff_cols)

    g_down = g_down.astype(f32)
    g_gu = g_gu.reshape(chips, 2, d_rows, 2 * ff_cols)
    g_gu = core_pair(pick(g_gu, core, 1), core_swap(pick(g_gu, 1 - core, 1)), 1)
    g_gu = exchange_chips(g_gu)
    g_gate, g_up = spread_ff(g_gu[..., :ff_cols]), spread_ff(g_gu[..., ff_cols:])

    def of_gain(grads, weights):
        return sum(jnp.sum(g * w.astype(f32), axis=1) for g, w in zip(grads, weights))

    def by_gain(gain, grads):
        return [g * gain.astype(f32)[:, None] for g in grads]

    g_mlp_gain = of_gain((g_gate, g_up), (w_gate, w_up))
    g_gate, g_up = by_gain(mlp_gain, (g_gate, g_up))
    result, d_input = give_back(result), give_back(d_input)
    g_rest, g_gate, g_up, g_down, g_mlp_gain, result, d_input = tie(
        g_rest, g_gate, g_up, g_down, g_mlp_gain, result, d_input
    )
    g_qkv = exchange_chips(g_rest[: chips * d_rows].reshape(chips, d_rows, cols_qkv))
    g_out = g_rest[chips * d_rows :].reshape(folds, d_rows, cols_qkv)
    g_out = jnp.transpose(g_out, (1, 0, 2)).reshape(d_rows, width).astype(f32)
    g_query = spread(g_qkv, 0, q_cols)
    g_key = spread(g_qkv, q_cols, kv_cols)
    g_value = spread(g_qkv, q_cols + kv_cols, kv_cols)
    g_attn_gain = of_gain((g_query, g_key, g_value), (w_query, w_key, w_value))
    g_query, g_key, g_value = by_gain(attn_gain, (g_query, g_key, g_value))
    return (
        result,
        d_input,
        g_attn_gain,
        g_query,
        g_key,
        g_value,
        g_out,
        g_mlp_gain,
        g_gate,
        g_up,
        g_down,
    )


def solution(mesh):
    ctx, fsdp = mesh.shape["ctx"], mesh.shape["fsdp"]
    split = Mesh(mesh.devices.reshape(ctx // 2, 2, fsdp), ("chip", "core", "fsdp"))
    ctx_axes = ("chip", "core")
    all_axes = ("chip", "core", "fsdp")
    tokens = P(None, "fsdp", ctx_axes, None)
    marks = P(None, "fsdp", ctx_axes)
    vector, matrix = P(all_axes), P(all_axes, None)
    return jax.shard_map(
        on_device,
        mesh=split,
        in_specs=(
            tokens, marks, marks, tokens, vector, matrix, matrix, matrix, matrix,
            vector, matrix, matrix, matrix,
        ),
        out_specs=(
            tokens, tokens, vector, matrix, matrix, matrix, matrix, vector,
            matrix, matrix, matrix,
        ),
        check_vma=False,
    )
```

```python
import math

import jax
import jax.numpy as jnp
from jax import lax
from jax.sharding import Mesh, PartitionSpec as P

HEADS = 16
KV_HEADS = 8
HEAD = 96
EPS = 1e-05
THETA = 100000.0
f32 = jnp.float32
bf16 = jnp.bfloat16


def rope_tables(position_ids):
    half = HEAD // 2
    ladder = jnp.arange(half).astype(f32) * (2.0 / HEAD)
    inverse = jnp.exp(-math.log(THETA) * ladder)
    angles = position_ids.astype(f32)[:, None] * inverse[None, :]
    return jnp.cos(angles)[:, None, :], jnp.sin(angles)[:, None, :]


def rotate(vectors, cosine, sine):
    half = HEAD // 2
    a, b = vectors[..., :half], vectors[..., half:]
    return jnp.concatenate([a * cosine - b * sine, b * cosine + a * sine], axis=-1)


def unrotate(grads, cosine, sine):
    half = HEAD // 2
    a, b = grads[..., :half], grads[..., half:]
    return jnp.concatenate([a * cosine + b * sine, b * cosine - a * sine], axis=-1)


def rms_scale(values):
    return lax.rsqrt(jnp.mean(values * values, axis=-1, keepdims=True) + EPS)


def norm_back(grad, normed, scale):
    return scale * (grad - normed * jnp.mean(grad * normed, axis=-1, keepdims=True))


def mm(a, b):
    return jnp.dot(a, b, preferred_element_type=f32)


def mm_tn(a, b):
    return jnp.einsum("td,te->de", a, b, preferred_element_type=f32)


def mm_nt(a, b):
    return jnp.einsum("te,de->td", a, b, preferred_element_type=f32)


def on_device(
    block_input,
    positions,
    segments,
    out_cotangent,
    attn_gain,
    w_query,
    w_key,
    w_value,
    w_out,
    mlp_gain,
    w_gate,
    w_up,
    w_down,
):
    chips = lax.axis_size("chip")
    rows_z = lax.axis_size("fsdp")
    chip = lax.axis_index("chip")
    core = lax.axis_index("core")
    place = lax.axis_index("fsdp")
    tok = block_input.shape[2]
    width = block_input.shape[3]
    d_rows = w_query.shape[0]
    q_cols = w_query.shape[1] // chips
    kv_cols = w_key.shape[1] // chips
    ff_cols = w_gate.shape[1] // (2 * chips)
    kv_heads = KV_HEADS // chips
    factor = HEAD ** (-0.5)

    def core_swap(a):
        return lax.ppermute(a, "core", [(0, 1), (1, 0)])

    def chip_xor(a, j):
        return lax.ppermute(a, "chip", [(i, i ^ j) for i in range(chips)])

    def pick(a, index, axis=0):
        return lax.dynamic_index_in_dim(a, index, axis, keepdims=False)

    def gather_chips(a, axis=0):
        return jnp.concatenate([a] + [chip_xor(a, j) for j in range(1, chips)], axis=axis)

    def scatter_chips(a):
        step = a.shape[0] // chips
        total = a[:step]
        for j in range(1, chips):
            total = total + chip_xor(a[j * step : (j + 1) * step].astype(bf16), j).astype(f32)
        return total

    def by_chip(pieces):
        stacked = jnp.stack(pieces)
        bit = 1
        while bit < chips:
            view = stacked.reshape((chips // (2 * bit), 2, bit) + stacked.shape[1:])
            flipped = jnp.flip(view, axis=1)
            stacked = jnp.where((chip & bit) != 0, flipped, view).reshape(stacked.shape)
            bit *= 2
        return stacked

    def exchange_chips(pack):
        pieces = [pick(pack, chip)]
        for j in range(1, chips):
            pieces.append(chip_xor(pick(pack, chip ^ j), j))
        return by_chip(pieces)

    def core_pair(mine, other, axis):
        first = core == 0
        return jnp.stack([jnp.where(first, mine, other), jnp.where(first, other, mine)], axis)

    def both_cores(a):
        return core_pair(a, core_swap(a), 0)

    def chip_slices(weights, cols):
        return jnp.stack(
            [
                jnp.concatenate([w[:, k * n : (k + 1) * n] for w, n in zip(weights, cols)], axis=1)
                for k in range(chips)
            ]
        )

    def tie(*values):
        return lax.optimization_barrier(values)

    def along_z(a, step):
        return lax.ppermute(a, "fsdp", [(i, (i + step) % rows_z) for i in range(rows_z)])

    def ring_first(a):
        return along_z(a, 1), along_z(a, -1)

    def ring_rest(a, right, left):
        found = [(a, 0, 0), (right, -1, 0), (left, 1, 0)]
        for step in range(2, rows_z // 2 + 1):
            if 2 * step == rows_z:
                half = a.shape[-1] // 2
                found.append((along_z(right[..., :half], 1), -step, 0))
                found.append((along_z(left[..., half:], -1), step, half))
            else:
                right, left = along_z(right, 1), along_z(left, -1)
                found += [(right, -step, 0), (left, step, 0)]
        return found

    def assemble(found, groups):
        rows, cols = found[0][0].shape
        whole = jnp.zeros((groups, rows_z, rows // groups, cols), bf16)
        for piece, offset, column in found:
            piece = piece.reshape(groups, 1, rows // groups, piece.shape[-1])
            index = lax.rem(place + offset + rows_z, rows_z)
            whole = lax.dynamic_update_slice(whole, piece, (0, index, 0, column))
        return whole

    def again(found, pieces):
        return [(piece,) + f[1:] for piece, f in zip(pieces, found)]

    def pieces_of(found):
        return [f[0] for f in found]

    def scaled(gain, *weights):
        return [(w.astype(f32) * gain.astype(f32)[:, None]).astype(bf16) for w in weights]

    pack_qkv = chip_slices(
        scaled(attn_gain, w_query, w_key, w_value), (q_cols, kv_cols, kv_cols)
    )
    piece_qkv = exchange_chips(pack_qkv).reshape(-1, pack_qkv.shape[-1])
    marks = jnp.stack([positions[:, 0] // 32, positions[:, 0] % 32, segments[:, 0]], axis=-1)
    marks = jnp.pad(marks.astype(bf16), ((0, 0), (0, 0), (0, 125)))
    pair = jnp.concatenate([out_cotangent[:, 0], block_input[:, 0], marks], axis=-1)
    pair = jnp.concatenate([pick(pair, core), core_swap(pick(pair, 1 - core))])
    rows = jnp.concatenate([w_out, w_down])
    gate_up = scaled(mlp_gain, w_gate, w_up)
    pack_gu = jnp.stack(
        [
            jnp.concatenate([w[:, n * ff_cols : (n + 1) * ff_cols] for w in gate_up], axis=1)
            for n in range(2 * chips)
        ]
    ).reshape(chips, 2, d_rows, 2 * ff_cols)
    pair, piece_qkv, pack_gu = tie(pair, piece_qkv, pack_gu)
    dy_low, x_low = pair[:, :width], pair[:, width:]

    qkv_right, qkv_left = ring_first(piece_qkv)
    piece_gu = exchange_chips(pack_gu)
    qkv_right, qkv_left, piece_gu, x_low, rows = tie(qkv_right, qkv_left, piece_gu, x_low, rows)
    rows = lax.all_gather(rows, "fsdp", axis=0)

    near = [j for j in range(1, chips) if j & (j - 1) == 0]
    far = [j for j in range(1, chips) if j & (j - 1) != 0]
    x_parts = {0: x_low, **{j: chip_xor(x_low, j) for j in near}}
    found_qkv = ring_rest(piece_qkv, qkv_right, qkv_left)
    piece_gu = core_pair(pick(piece_gu, core, 1), core_swap(pick(piece_gu, 1 - core, 1)), 1)
    piece_gu = piece_gu.reshape(2 * chips * d_rows, 2 * ff_cols)
    order = sorted(x_parts)
    piece_gu, *late = tie(piece_gu, *[x_parts[j] for j in order], *pieces_of(found_qkv))
    x_parts = dict(zip(order, late))
    x_parts.update({j: chip_xor(x_low, j) for j in far})
    x_all = jnp.concatenate([x_parts[j] for j in range(chips)])
    found_qkv = again(found_qkv, late[len(order) :])
    marks = x_all[:, width : width + 3].astype(f32).T
    pos_all, seg_all = marks[0] * 32.0 + marks[1], marks[2]
    x_all, x_low = x_all[:, :width], x_low[:, :width]
    allowed = (seg_all[:, None] == seg_all[None, :]) & (pos_all[None, :] <= pos_all[:, None])
    cosine, sine = rope_tables(pos_all)
    w_qkv = assemble(found_qkv, chips)
    w_qkv = core_pair(w_qkv, core_swap(w_qkv), 1).reshape(width, -1)
    w_qkv, x_all, dy_low, cosine, sine, allowed = tie(w_qkv, x_all, dy_low, cosine, sine, allowed)
    own = x_low.shape[0]
    seq = x_all.shape[0]

    dy_all = gather_chips(dy_low)
    x_full = x_all.astype(f32)
    h_one = (x_full * rms_scale(x_full)).astype(bf16)
    qkv = mm(h_one, w_qkv)
    q_rot = rotate(qkv[:, :q_cols].reshape(seq, kv_heads * 2, HEAD), cosine, sine)
    q_rot = q_rot.astype(bf16).reshape(seq, kv_heads, 2, HEAD)
    k_rot = rotate(
        qkv[:, q_cols : q_cols + kv_cols].reshape(seq, kv_heads, HEAD), cosine, sine
    ).astype(bf16)
    value = qkv[:, q_cols + kv_cols :].astype(bf16).reshape(seq, kv_heads, HEAD)
    scores = jnp.einsum("sgrh,tgh->grst", q_rot, k_rot, preferred_element_type=f32) * factor
    scores = jnp.where(allowed, scores, -1e30)
    raised = jnp.exp(scores - jnp.max(scores, axis=-1, keepdims=True))
    soft = raised / jnp.sum(raised, axis=-1, keepdims=True)
    soft_low, rows = tie(soft.astype(bf16), rows)
    along_out = rows[:, : w_out.shape[0]].reshape(-1, width)
    along_down = rows[:, w_out.shape[0] :].reshape(-1, width)
    out_w = both_cores(along_out).reshape(-1, width)
    mixed = jnp.einsum("grst,tgh->sgrh", soft_low, value, preferred_element_type=f32)
    mixed = mixed.astype(bf16).reshape(seq, q_cols)
    mixed, dy_all, out_w = tie(mixed, dy_all, out_w)
    x_own = x_low.astype(f32)
    middle = x_own + scatter_chips(mm(mixed, out_w))

    dy_both = jnp.concatenate([dy_all, core_swap(dy_all)])
    along_gu = lax.all_gather(piece_gu, "fsdp", axis=0, tiled=True)
    middle, dy_both = tie(middle, dy_both)
    scale_two = rms_scale(middle)
    n_two = middle * scale_two
    h_two = gather_chips(n_two.astype(bf16))
    h_both, along_gu = tie(jnp.concatenate([h_two, core_swap(h_two)]), along_gu)
    w_gu = along_gu.reshape(rows_z, 2 * chips, d_rows, 2 * ff_cols)
    w_gu = jnp.transpose(w_gu, (1, 0, 2, 3)).reshape(width, 2 * ff_cols)
    gu = mm(h_both, w_gu)
    gate, up = gu[:, :ff_cols], gu[:, ff_cols:]
    sigma = jax.nn.sigmoid(gate)
    act = (gate * sigma * up).astype(bf16)
    d_act = mm_nt(dy_both, along_down)
    d_gate = (d_act * up * sigma * (1.0 + gate * (1.0 - sigma))).astype(bf16)
    d_up = (d_act * gate * sigma).astype(bf16)
    d_gu = jnp.concatenate([d_gate, d_up], axis=1)
    g_down = mm_tn(act, dy_both).astype(bf16)
    g_down, d_gu = tie(g_down, d_gu)
    g_down = lax.psum_scatter(g_down, "fsdp", scatter_dimension=0, tiled=True)

    def give_partial(rows, weights, product):
        other = core_swap(product(rows[seq:], weights).astype(bf16)).astype(f32)
        return product(rows[:seq], weights) + other

    d_h_two, act = tie(give_partial(d_gu, w_gu, mm_nt), act)
    g_gu = mm_tn(h_both, d_gu).astype(bf16).reshape(2 * chips, rows_z, d_rows, 2 * ff_cols)
    g_gu = jnp.transpose(g_gu, (1, 0, 2, 3)).reshape(width, 2 * ff_cols)
    d_h_two, g_gu = tie(scatter_chips(d_h_two), g_gu)
    g_gu = lax.psum_scatter(g_gu, "fsdp", scatter_dimension=0, tiled=True)

    dy_own = dy_low.astype(f32)
    d_middle = dy_own + norm_back(d_h_two, n_two, scale_two)
    branch = gather_chips(d_middle.astype(bf16))
    partial = give_partial(act, along_down, mm)
    kept, given = partial[:own], partial[own:].astype(bf16)
    branch, kept, given, g_down = tie(branch, kept, given, g_down)

    g_out = mm_tn(mixed, branch).astype(bf16)
    g_out = g_out.reshape(2, g_out.shape[0] // 2, g_out.shape[1])
    g_out = pick(g_out, core) + core_swap(pick(g_out, 1 - core))
    d_mixed = mm_nt(branch, out_w).astype(bf16).reshape(seq, kv_heads, 2, HEAD)
    d_soft = jnp.einsum("sgrh,tgh->grst", d_mixed, value, preferred_element_type=f32)
    d_value = jnp.einsum("grst,sgrh->tgh", soft_low, d_mixed, preferred_element_type=f32)
    inner = jnp.sum(soft * d_soft, axis=-1, keepdims=True)
    d_scores = (soft * (d_soft - inner)).astype(bf16)
    d_q = jnp.einsum("grst,tgh->sgrh", d_scores, k_rot, preferred_element_type=f32) * factor
    d_k = jnp.einsum("grst,sgrh->tgh", d_scores, q_rot, preferred_element_type=f32) * factor
    d_q = unrotate(d_q.reshape(seq, kv_heads * 2, HEAD), cosine, sine)
    d_k = unrotate(d_k, cosine, sine)
    d_qkv = jnp.concatenate(
        [
            d_q.reshape(seq, q_cols).astype(bf16),
            d_k.reshape(seq, kv_cols).astype(bf16),
            d_value.reshape(seq, kv_cols).astype(bf16),
        ],
        axis=1,
    )
    d_qkv, g_out = tie(d_qkv, g_out)
    cols_qkv = d_qkv.shape[1]
    g_qkv = mm_tn(h_one, d_qkv).astype(bf16).reshape(chips, 2, rows_z, d_rows, cols_qkv)
    g_qkv = pick(g_qkv, core, 1) + core_swap(pick(g_qkv, 1 - core, 1))
    g_qkv = jnp.transpose(g_qkv, (1, 0, 2, 3)).reshape(1, rows_z, chips * d_rows, cols_qkv)
    folds = width // cols_qkv
    g_out = g_out.reshape(1, rows_z, d_rows, width)
    g_rest = [g_out[..., k * cols_qkv : (k + 1) * cols_qkv] for k in range(folds)]
    g_rest = jnp.concatenate([g_qkv] + g_rest, axis=2)
    d_h_one = mm_nt(d_qkv, w_qkv)
    g_rest, d_h_one = tie(g_rest.reshape(-1, cols_qkv), d_h_one)
    g_rest = lax.psum_scatter(g_rest, "fsdp", scatter_dimension=0, tiled=True)
    d_h_one, given = tie(scatter_chips(d_h_one), given)
    result = middle + kept
    for j in range(1, chips):
        result = result + chip_xor(given[(j - 1) * own : j * own], j).astype(f32)
    g_gu = g_gu.reshape(chips, 2, d_rows, 2 * ff_cols)
    g_gu = core_pair(pick(g_gu, core, 1), core_swap(pick(g_gu, 1 - core, 1)), 1)
    g_gu = exchange_chips(g_gu)
    result, g_rest, g_gu = tie(result.astype(bf16), g_rest, g_gu)
    scale_one = rms_scale(x_own)
    n_one = x_own * scale_one
    d_input = (d_middle + norm_back(d_h_one, n_one, scale_one)).astype(bf16)

    def give_back(a):
        mine, theirs = a[:tok], core_swap(a[tok:])
        first = core == 0
        return jnp.stack([jnp.where(first, mine, theirs), jnp.where(first, theirs, mine)])[:, None]

    def spread(grad, start, cols):
        part = grad[:, :, start : start + cols].astype(f32)
        return jnp.transpose(part, (1, 0, 2)).reshape(d_rows, chips * cols)

    def spread_ff(grad):
        grad = jnp.transpose(grad.astype(f32), (2, 0, 1, 3))
        return grad.reshape(d_rows, 2 * chips * ff_cols)

    g_down = g_down.astype(f32)
    g_gate, g_up = spread_ff(g_gu[..., :ff_cols]), spread_ff(g_gu[..., ff_cols:])

    def of_gain(grads, weights):
        return sum(jnp.sum(g * w.astype(f32), axis=1) for g, w in zip(grads, weights))

    def by_gain(gain, grads):
        return [g * gain.astype(f32)[:, None] for g in grads]

    g_mlp_gain = of_gain((g_gate, g_up), (w_gate, w_up))
    g_gate, g_up = by_gain(mlp_gain, (g_gate, g_up))
    result, d_input = give_back(result), give_back(d_input)
    g_rest, g_gate, g_up, g_down, g_mlp_gain, result, d_input = tie(
        g_rest, g_gate, g_up, g_down, g_mlp_gain, result, d_input
    )
    g_qkv = exchange_chips(g_rest[: chips * d_rows].reshape(chips, d_rows, cols_qkv))
    g_out = g_rest[chips * d_rows :].reshape(folds, d_rows, cols_qkv)
    g_out = jnp.transpose(g_out, (1, 0, 2)).reshape(d_rows, width).astype(f32)
    g_query = spread(g_qkv, 0, q_cols)
    g_key = spread(g_qkv, q_cols, kv_cols)
    g_value = spread(g_qkv, q_cols + kv_cols, kv_cols)
    g_attn_gain = of_gain((g_query, g_key, g_value), (w_query, w_key, w_value))
    g_query, g_key, g_value = by_gain(attn_gain, (g_query, g_key, g_value))
    return (
        result,
        d_input,
        g_attn_gain,
        g_query,
        g_key,
        g_value,
        g_out,
        g_mlp_gain,
        g_gate,
        g_up,
        g_down,
    )


def solution(mesh):
    ctx, fsdp = mesh.shape["ctx"], mesh.shape["fsdp"]
    split = Mesh(mesh.devices.reshape(ctx // 2, 2, fsdp), ("chip", "core", "fsdp"))
    ctx_axes = ("chip", "core")
    all_axes = ("chip", "core", "fsdp")
    tokens = P(None, "fsdp", ctx_axes, None)
    marks = P(None, "fsdp", ctx_axes)
    vector, matrix = P(all_axes), P(all_axes, None)
    return jax.shard_map(
        on_device,
        mesh=split,
        in_specs=(
            tokens, marks, marks, tokens, vector, matrix, matrix, matrix, matrix,
            vector, matrix, matrix, matrix,
        ),
        out_specs=(
            tokens, tokens, vector, matrix, matrix, matrix, matrix, vector,
            matrix, matrix, matrix,
        ),
        check_vma=False,
    )
```

```python
import math

import jax
import jax.numpy as jnp
from jax import lax
from jax.sharding import Mesh, PartitionSpec as P

HEADS = 16
KV_HEADS = 8
HEAD = 96
EPS = 1e-05
THETA = 100000.0
f32 = jnp.float32
bf16 = jnp.bfloat16


def rope_tables(position_ids):
    half = HEAD // 2
    ladder = jnp.arange(half).astype(f32) * (2.0 / HEAD)
    inverse = jnp.exp(-math.log(THETA) * ladder)
    angles = position_ids.astype(f32)[:, None] * inverse[None, :]
    return jnp.cos(angles)[:, None, :], jnp.sin(angles)[:, None, :]


def rotate(vectors, cosine, sine):
    half = HEAD // 2
    a, b = vectors[..., :half], vectors[..., half:]
    return jnp.concatenate([a * cosine - b * sine, b * cosine + a * sine], axis=-1)


def unrotate(grads, cosine, sine):
    half = HEAD // 2
    a, b = grads[..., :half], grads[..., half:]
    return jnp.concatenate([a * cosine + b * sine, b * cosine - a * sine], axis=-1)


def rms_scale(values):
    return lax.rsqrt(jnp.mean(values * values, axis=-1, keepdims=True) + EPS)


def norm_back(grad, normed, scale):
    return scale * (grad - normed * jnp.mean(grad * normed, axis=-1, keepdims=True))


def mm(a, b):
    return jnp.dot(a, b, preferred_element_type=f32)


def mm_tn(a, b):
    return jnp.einsum("td,te->de", a, b, preferred_element_type=f32)


def mm_nt(a, b):
    return jnp.einsum("te,de->td", a, b, preferred_element_type=f32)


def on_device(
    block_input,
    positions,
    segments,
    out_cotangent,
    attn_gain,
    w_query,
    w_key,
    w_value,
    w_out,
    mlp_gain,
    w_gate,
    w_up,
    w_down,
):
    chips = lax.axis_size("chip")
    rows_z = lax.axis_size("fsdp")
    chip = lax.axis_index("chip")
    core = lax.axis_index("core")
    place = lax.axis_index("fsdp")
    tok = block_input.shape[2]
    width = block_input.shape[3]
    d_rows = w_query.shape[0]
    q_cols = w_query.shape[1] // chips
    kv_cols = w_key.shape[1] // chips
    ff_cols = w_gate.shape[1] // (2 * chips)
    kv_heads = KV_HEADS // chips
    factor = HEAD ** (-0.5)

    def core_swap(a):
        return lax.ppermute(a, "core", [(0, 1), (1, 0)])

    def chip_xor(a, j):
        return lax.ppermute(a, "chip", [(i, i ^ j) for i in range(chips)])

    def pick(a, index, axis=0):
        return lax.dynamic_index_in_dim(a, index, axis, keepdims=False)

    def gather_chips(a, axis=0):
        return jnp.concatenate([a] + [chip_xor(a, j) for j in range(1, chips)], axis=axis)

    def scatter_chips(a):
        step = a.shape[0] // chips
        total = a[:step]
        for j in range(1, chips):
            total = total + chip_xor(a[j * step : (j + 1) * step].astype(bf16), j).astype(f32)
        return total

    def by_chip(pieces):
        stacked = jnp.stack(pieces)
        bit = 1
        while bit < chips:
            view = stacked.reshape((chips // (2 * bit), 2, bit) + stacked.shape[1:])
            flipped = jnp.flip(view, axis=1)
            stacked = jnp.where((chip & bit) != 0, flipped, view).reshape(stacked.shape)
            bit *= 2
        return stacked

    def exchange_chips(pack):
        pieces = [pick(pack, chip)]
        for j in range(1, chips):
            pieces.append(chip_xor(pick(pack, chip ^ j), j))
        return by_chip(pieces)

    def core_pair(mine, other, axis):
        first = core == 0
        return jnp.stack([jnp.where(first, mine, other), jnp.where(first, other, mine)], axis)

    def both_cores(a):
        return core_pair(a, core_swap(a), 0)

    def chip_slices(weights, cols):
        return jnp.stack(
            [
                jnp.concatenate([w[:, k * n : (k + 1) * n] for w, n in zip(weights, cols)], axis=1)
                for k in range(chips)
            ]
        )

    def tie(*values):
        return lax.optimization_barrier(values)

    def along_z(a, step):
        return lax.ppermute(a, "fsdp", [(i, (i + step) % rows_z) for i in range(rows_z)])

    def ring_first(a):
        return along_z(a, 1), along_z(a, -1)

    def ring_rest(a, right, left):
        found = [(a, 0, 0), (right, -1, 0), (left, 1, 0)]
        for step in range(2, rows_z // 2 + 1):
            if 2 * step == rows_z:
                half = a.shape[-1] // 2
                found.append((along_z(right[..., :half], 1), -step, 0))
                found.append((along_z(left[..., half:], -1), step, half))
            else:
                right, left = along_z(right, 1), along_z(left, -1)
                found += [(right, -step, 0), (left, step, 0)]
        return found

    def assemble(found, groups):
        rows, cols = found[0][0].shape
        whole = jnp.zeros((groups, rows_z, rows // groups, cols), bf16)
        for piece, offset, column in found:
            piece = piece.reshape(groups, 1, rows // groups, piece.shape[-1])
            index = lax.rem(place + offset + rows_z, rows_z)
            whole = lax.dynamic_update_slice(whole, piece, (0, index, 0, column))
        return whole

    def again(found, pieces):
        return [(piece,) + f[1:] for piece, f in zip(pieces, found)]

    def pieces_of(found):
        return [f[0] for f in found]

    def scaled(gain, *weights):
        return [(w.astype(f32) * gain.astype(f32)[:, None]).astype(bf16) for w in weights]

    pack_qkv = chip_slices(
        scaled(attn_gain, w_query, w_key, w_value), (q_cols, kv_cols, kv_cols)
    )
    piece_qkv = exchange_chips(pack_qkv).reshape(-1, pack_qkv.shape[-1])
    marks = jnp.stack([positions[:, 0] // 32, positions[:, 0] % 32, segments[:, 0]], axis=-1)
    marks = jnp.pad(marks.astype(bf16), ((0, 0), (0, 0), (0, 125)))
    pair = jnp.concatenate([out_cotangent[:, 0], block_input[:, 0], marks], axis=-1)
    pair = jnp.concatenate([pick(pair, core), core_swap(pick(pair, 1 - core))])
    lower, upper = w_down[: w_down.shape[0] // 2], w_down[w_down.shape[0] // 2 :]
    rows = jnp.concatenate([w_out, lower])
    gate_up = scaled(mlp_gain, w_gate, w_up)
    pack_gu = jnp.stack(
        [
            jnp.concatenate([w[:, n * ff_cols : (n + 1) * ff_cols] for w in gate_up], axis=1)
            for n in range(2 * chips)
        ]
    ).reshape(chips, 2, d_rows, 2 * ff_cols)
    pair, piece_qkv, pack_gu = tie(pair, piece_qkv, pack_gu)
    dy_low, x_low = pair[:, :width], pair[:, width:]

    qkv_right, qkv_left = ring_first(piece_qkv)
    piece_gu = exchange_chips(pack_gu)
    qkv_right, qkv_left, piece_gu, x_low, rows = tie(qkv_right, qkv_left, piece_gu, x_low, rows)
    rows = lax.all_gather(rows, "fsdp", axis=0)

    near = [j for j in range(1, chips) if j & (j - 1) == 0]
    far = [j for j in range(1, chips) if j & (j - 1) != 0]
    x_parts = {0: x_low, **{j: chip_xor(x_low, j) for j in near}}
    found_qkv = ring_rest(piece_qkv, qkv_right, qkv_left)
    piece_gu = core_pair(pick(piece_gu, core, 1), core_swap(pick(piece_gu, 1 - core, 1)), 1)
    piece_gu = piece_gu.reshape(2 * chips * d_rows, 2 * ff_cols)
    order = sorted(x_parts)
    piece_gu, *late = tie(piece_gu, *[x_parts[j] for j in order], *pieces_of(found_qkv))
    x_parts = dict(zip(order, late))
    x_parts.update({j: chip_xor(x_low, j) for j in far})
    x_all = jnp.concatenate([x_parts[j] for j in range(chips)])
    found_qkv = again(found_qkv, late[len(order) :])
    marks = x_all[:, width : width + 3].astype(f32).T
    pos_all, seg_all = marks[0] * 32.0 + marks[1], marks[2]
    x_all, x_low = x_all[:, :width], x_low[:, :width]
    allowed = (seg_all[:, None] == seg_all[None, :]) & (pos_all[None, :] <= pos_all[:, None])
    cosine, sine = rope_tables(pos_all)
    w_qkv = assemble(found_qkv, chips)
    w_qkv = core_pair(w_qkv, core_swap(w_qkv), 1).reshape(width, -1)
    w_qkv, x_all, dy_low, cosine, sine, allowed = tie(w_qkv, x_all, dy_low, cosine, sine, allowed)
    own = x_low.shape[0]
    seq = x_all.shape[0]

    dy_all = gather_chips(dy_low)
    x_full = x_all.astype(f32)
    h_one = (x_full * rms_scale(x_full)).astype(bf16)
    qkv = mm(h_one, w_qkv)
    q_rot = rotate(qkv[:, :q_cols].reshape(seq, kv_heads * 2, HEAD), cosine, sine)
    q_rot = q_rot.astype(bf16).reshape(seq, kv_heads, 2, HEAD)
    k_rot = rotate(
        qkv[:, q_cols : q_cols + kv_cols].reshape(seq, kv_heads, HEAD), cosine, sine
    ).astype(bf16)
    value = qkv[:, q_cols + kv_cols :].astype(bf16).reshape(seq, kv_heads, HEAD)
    scores = jnp.einsum("sgrh,tgh->grst", q_rot, k_rot, preferred_element_type=f32) * factor
    scores = jnp.where(allowed, scores, -1e30)
    raised = jnp.exp(scores - jnp.max(scores, axis=-1, keepdims=True))
    soft = raised / jnp.sum(raised, axis=-1, keepdims=True)
    soft_low, rows = tie(soft.astype(bf16), rows)
    along_out = rows[:, : w_out.shape[0]].reshape(-1, width)
    out_w = both_cores(along_out).reshape(-1, width)
    mixed = jnp.einsum("grst,tgh->sgrh", soft_low, value, preferred_element_type=f32)
    mixed = mixed.astype(bf16).reshape(seq, q_cols)
    mixed, dy_all, out_w = tie(mixed, dy_all, out_w)
    x_own = x_low.astype(f32)
    middle = x_own + scatter_chips(mm(mixed, out_w))

    dy_both = jnp.concatenate([dy_all, core_swap(dy_all)])
    along_gu = lax.all_gather(piece_gu, "fsdp", axis=0, tiled=True)
    middle, dy_both, upper = tie(middle, dy_both, upper)
    upper_right, upper_left = ring_first(upper)
    scale_two = rms_scale(middle)
    n_two = middle * scale_two
    h_two = gather_chips(n_two.astype(bf16))
    h_two, upper_right, upper_left = tie(h_two, upper_right, upper_left)
    along_upper = assemble(ring_rest(upper, upper_right, upper_left), 1)[0]
    along_down = jnp.concatenate([rows[:, w_out.shape[0] :], along_upper], axis=1)
    along_down = along_down.reshape(-1, width)
    h_both, along_gu, along_down = tie(
        jnp.concatenate([h_two, core_swap(h_two)]), along_gu, along_down
    )
    w_gu = along_gu.reshape(rows_z, 2 * chips, d_rows, 2 * ff_cols)
    w_gu = jnp.transpose(w_gu, (1, 0, 2, 3)).reshape(width, 2 * ff_cols)
    gu = mm(h_both, w_gu)
    gate, up = gu[:, :ff_cols], gu[:, ff_cols:]
    sigma = jax.nn.sigmoid(gate)
    act = (gate * sigma * up).astype(bf16)
    d_act = mm_nt(dy_both, along_down)
    d_gate = (d_act * up * sigma * (1.0 + gate * (1.0 - sigma))).astype(bf16)
    d_up = (d_act * gate * sigma).astype(bf16)
    d_gu = jnp.concatenate([d_gate, d_up], axis=1)
    g_down = mm_tn(act, dy_both).astype(bf16)
    g_down, d_gu = tie(g_down, d_gu)
    g_down = lax.psum_scatter(g_down, "fsdp", scatter_dimension=0, tiled=True)

    def give_partial(rows, weights, product):
        other = core_swap(product(rows[seq:], weights).astype(bf16)).astype(f32)
        return product(rows[:seq], weights) + other

    d_h_two, act = tie(give_partial(d_gu, w_gu, mm_nt), act)
    g_gu = mm_tn(h_both, d_gu).astype(bf16).reshape(2 * chips, rows_z, d_rows, 2 * ff_cols)
    g_gu = jnp.transpose(g_gu, (1, 0, 2, 3)).reshape(width, 2 * ff_cols)
    d_h_two, g_gu = tie(scatter_chips(d_h_two), g_gu)
    g_gu = lax.psum_scatter(g_gu, "fsdp", scatter_dimension=0, tiled=True)

    dy_own = dy_low.astype(f32)
    d_middle = dy_own + norm_back(d_h_two, n_two, scale_two)
    branch = gather_chips(d_middle.astype(bf16))
    partial = give_partial(act, along_down, mm)
    kept, given = partial[:own], partial[own:].astype(bf16)
    branch, kept, given, g_down = tie(branch, kept, given, g_down)

    g_out = mm_tn(mixed, branch).astype(bf16)
    g_out = g_out.reshape(2, g_out.shape[0] // 2, g_out.shape[1])
    g_out = pick(g_out, core) + core_swap(pick(g_out, 1 - core))
    d_mixed = mm_nt(branch, out_w).astype(bf16).reshape(seq, kv_heads, 2, HEAD)
    d_soft = jnp.einsum("sgrh,tgh->grst", d_mixed, value, preferred_element_type=f32)
    d_value = jnp.einsum("grst,sgrh->tgh", soft_low, d_mixed, preferred_element_type=f32)
    inner = jnp.sum(soft * d_soft, axis=-1, keepdims=True)
    d_scores = (soft * (d_soft - inner)).astype(bf16)
    d_q = jnp.einsum("grst,tgh->sgrh", d_scores, k_rot, preferred_element_type=f32) * factor
    d_k = jnp.einsum("grst,sgrh->tgh", d_scores, q_rot, preferred_element_type=f32) * factor
    d_q = unrotate(d_q.reshape(seq, kv_heads * 2, HEAD), cosine, sine)
    d_k = unrotate(d_k, cosine, sine)
    d_qkv = jnp.concatenate(
        [
            d_q.reshape(seq, q_cols).astype(bf16),
            d_k.reshape(seq, kv_cols).astype(bf16),
            d_value.reshape(seq, kv_cols).astype(bf16),
        ],
        axis=1,
    )
    d_qkv, g_out = tie(d_qkv, g_out)
    cols_qkv = d_qkv.shape[1]
    g_qkv = mm_tn(h_one, d_qkv).astype(bf16).reshape(chips, 2, rows_z, d_rows, cols_qkv)
    g_qkv = pick(g_qkv, core, 1) + core_swap(pick(g_qkv, 1 - core, 1))
    g_qkv = jnp.transpose(g_qkv, (1, 0, 2, 3)).reshape(1, rows_z, chips * d_rows, cols_qkv)
    folds = width // cols_qkv
    g_out = g_out.reshape(1, rows_z, d_rows, width)
    g_rest = [g_out[..., k * cols_qkv : (k + 1) * cols_qkv] for k in range(folds)]
    g_rest = jnp.concatenate([g_qkv] + g_rest, axis=2)
    d_h_one = mm_nt(d_qkv, w_qkv)
    g_rest, d_h_one = tie(g_rest.reshape(-1, cols_qkv), d_h_one)
    g_rest = lax.psum_scatter(g_rest, "fsdp", scatter_dimension=0, tiled=True)
    d_h_one, given, g_gu = tie(scatter_chips(d_h_one), given, g_gu)
    result = middle + kept
    for j in range(1, chips):
        result = result + chip_xor(given[(j - 1) * own : j * own], j).astype(f32)
    g_gu = g_gu.reshape(chips, 2, d_rows, 2 * ff_cols)
    g_gu = core_pair(pick(g_gu, core, 1), core_swap(pick(g_gu, 1 - core, 1)), 1)
    g_gu = exchange_chips(g_gu)
    result, g_rest, g_gu = tie(result.astype(bf16), g_rest, g_gu)
    scale_one = rms_scale(x_own)
    n_one = x_own * scale_one
    d_input = (d_middle + norm_back(d_h_one, n_one, scale_one)).astype(bf16)

    def give_back(a):
        mine, theirs = a[:tok], core_swap(a[tok:])
        first = core == 0
        return jnp.stack([jnp.where(first, mine, theirs), jnp.where(first, theirs, mine)])[:, None]

    def spread(grad, start, cols):
        part = grad[:, :, start : start + cols].astype(f32)
        return jnp.transpose(part, (1, 0, 2)).reshape(d_rows, chips * cols)

    def spread_ff(grad):
        grad = jnp.transpose(grad.astype(f32), (2, 0, 1, 3))
        return grad.reshape(d_rows, 2 * chips * ff_cols)

    g_down = g_down.astype(f32)
    g_gate, g_up = spread_ff(g_gu[..., :ff_cols]), spread_ff(g_gu[..., ff_cols:])

    def of_gain(grads, weights):
        return sum(jnp.sum(g * w.astype(f32), axis=1) for g, w in zip(grads, weights))

    def by_gain(gain, grads):
        return [g * gain.astype(f32)[:, None] for g in grads]

    g_mlp_gain = of_gain((g_gate, g_up), (w_gate, w_up))
    g_gate, g_up = by_gain(mlp_gain, (g_gate, g_up))
    result, d_input = give_back(result), give_back(d_input)
    g_rest, g_gate, g_up, g_down, g_mlp_gain, result, d_input = tie(
        g_rest, g_gate, g_up, g_down, g_mlp_gain, result, d_input
    )
    g_qkv = exchange_chips(g_rest[: chips * d_rows].reshape(chips, d_rows, cols_qkv))
    g_out = g_rest[chips * d_rows :].reshape(folds, d_rows, cols_qkv)
    g_out = jnp.transpose(g_out, (1, 0, 2)).reshape(d_rows, width).astype(f32)
    g_query = spread(g_qkv, 0, q_cols)
    g_key = spread(g_qkv, q_cols, kv_cols)
    g_value = spread(g_qkv, q_cols + kv_cols, kv_cols)
    g_attn_gain = of_gain((g_query, g_key, g_value), (w_query, w_key, w_value))
    g_query, g_key, g_value = by_gain(attn_gain, (g_query, g_key, g_value))
    return (
        result,
        d_input,
        g_attn_gain,
        g_query,
        g_key,
        g_value,
        g_out,
        g_mlp_gain,
        g_gate,
        g_up,
        g_down,
    )


def solution(mesh):
    ctx, fsdp = mesh.shape["ctx"], mesh.shape["fsdp"]
    split = Mesh(mesh.devices.reshape(ctx // 2, 2, fsdp), ("chip", "core", "fsdp"))
    ctx_axes = ("chip", "core")
    all_axes = ("chip", "core", "fsdp")
    tokens = P(None, "fsdp", ctx_axes, None)
    marks = P(None, "fsdp", ctx_axes)
    vector, matrix = P(all_axes), P(all_axes, None)
    return jax.shard_map(
        on_device,
        mesh=split,
        in_specs=(
            tokens, marks, marks, tokens, vector, matrix, matrix, matrix, matrix,
            vector, matrix, matrix, matrix,
        ),
        out_specs=(
            tokens, tokens, vector, matrix, matrix, matrix, matrix, vector,
            matrix, matrix, matrix,
        ),
        check_vma=False,
    )
```

```python
import math

import jax
import jax.numpy as jnp
from jax import lax
from jax.sharding import Mesh, PartitionSpec as P

HEADS = 16
KV_HEADS = 8
HEAD = 96
EPS = 1e-05
THETA = 100000.0
f32 = jnp.float32
bf16 = jnp.bfloat16


def rope_tables(position_ids):
    half = HEAD // 2
    ladder = jnp.arange(half).astype(f32) * (2.0 / HEAD)
    inverse = jnp.exp(-math.log(THETA) * ladder)
    angles = position_ids.astype(f32)[:, None] * inverse[None, :]
    return jnp.cos(angles)[:, None, :], jnp.sin(angles)[:, None, :]


def rotate(vectors, cosine, sine):
    half = HEAD // 2
    a, b = vectors[..., :half], vectors[..., half:]
    return jnp.concatenate([a * cosine - b * sine, b * cosine + a * sine], axis=-1)


def unrotate(grads, cosine, sine):
    half = HEAD // 2
    a, b = grads[..., :half], grads[..., half:]
    return jnp.concatenate([a * cosine + b * sine, b * cosine - a * sine], axis=-1)


def rms_scale(values):
    return lax.rsqrt(jnp.mean(values * values, axis=-1, keepdims=True) + EPS)


def norm_back(grad, normed, scale):
    return scale * (grad - normed * jnp.mean(grad * normed, axis=-1, keepdims=True))


def mm(a, b):
    return jnp.dot(a, b, preferred_element_type=f32)


def mm_tn(a, b):
    return jnp.einsum("td,te->de", a, b, preferred_element_type=f32)


def mm_nt(a, b):
    return jnp.einsum("te,de->td", a, b, preferred_element_type=f32)


def on_device(
    block_input,
    positions,
    segments,
    out_cotangent,
    attn_gain,
    w_query,
    w_key,
    w_value,
    w_out,
    mlp_gain,
    w_gate,
    w_up,
    w_down,
):
    chips = lax.axis_size("chip")
    rows_z = lax.axis_size("fsdp")
    chip = lax.axis_index("chip")
    core = lax.axis_index("core")
    place = lax.axis_index("fsdp")
    tok = block_input.shape[2]
    width = block_input.shape[3]
    d_rows = w_query.shape[0]
    q_cols = w_query.shape[1] // chips
    kv_cols = w_key.shape[1] // chips
    ff_cols = w_gate.shape[1] // (2 * chips)
    kv_heads = KV_HEADS // chips
    factor = HEAD ** (-0.5)

    def core_swap(a):
        return lax.ppermute(a, "core", [(0, 1), (1, 0)])

    def chip_xor(a, j):
        return lax.ppermute(a, "chip", [(i, i ^ j) for i in range(chips)])

    def pick(a, index, axis=0):
        return lax.dynamic_index_in_dim(a, index, axis, keepdims=False)

    def gather_chips(a, axis=0):
        return jnp.concatenate([a] + [chip_xor(a, j) for j in range(1, chips)], axis=axis)

    def scatter_chips(a):
        step = a.shape[0] // chips
        total = a[:step]
        for j in range(1, chips):
            total = total + chip_xor(a[j * step : (j + 1) * step].astype(bf16), j).astype(f32)
        return total

    def by_chip(pieces):
        stacked = jnp.stack(pieces)
        bit = 1
        while bit < chips:
            view = stacked.reshape((chips // (2 * bit), 2, bit) + stacked.shape[1:])
            flipped = jnp.flip(view, axis=1)
            stacked = jnp.where((chip & bit) != 0, flipped, view).reshape(stacked.shape)
            bit *= 2
        return stacked

    def exchange_chips(pack):
        pieces = [pick(pack, chip)]
        for j in range(1, chips):
            pieces.append(chip_xor(pick(pack, chip ^ j), j))
        return by_chip(pieces)

    def core_pair(mine, other, axis):
        first = core == 0
        return jnp.stack([jnp.where(first, mine, other), jnp.where(first, other, mine)], axis)

    def both_cores(a):
        return core_pair(a, core_swap(a), 0)

    def chip_slices(weights, cols):
        return jnp.stack(
            [
                jnp.concatenate([w[:, k * n : (k + 1) * n] for w, n in zip(weights, cols)], axis=1)
                for k in range(chips)
            ]
        )

    def tie(*values):
        return lax.optimization_barrier(values)

    def along_z(a, step):
        return lax.ppermute(a, "fsdp", [(i, (i + step) % rows_z) for i in range(rows_z)])

    def ring_first(a):
        return along_z(a, 1), along_z(a, -1)

    def ring_rest(a, right, left):
        found = [(a, 0, 0), (right, -1, 0), (left, 1, 0)]
        for step in range(2, rows_z // 2 + 1):
            if 2 * step == rows_z:
                half = a.shape[-1] // 2
                found.append((along_z(right[..., :half], 1), -step, 0))
                found.append((along_z(left[..., half:], -1), step, half))
            else:
                right, left = along_z(right, 1), along_z(left, -1)
                found += [(right, -step, 0), (left, step, 0)]
        return found

    def assemble(found, groups):
        rows, cols = found[0][0].shape
        whole = jnp.zeros((groups, rows_z, rows // groups, cols), bf16)
        for piece, offset, column in found:
            piece = piece.reshape(groups, 1, rows // groups, piece.shape[-1])
            index = lax.rem(place + offset + rows_z, rows_z)
            whole = lax.dynamic_update_slice(whole, piece, (0, index, 0, column))
        return whole

    def again(found, pieces):
        return [(piece,) + f[1:] for piece, f in zip(pieces, found)]

    def pieces_of(found):
        return [f[0] for f in found]

    def scaled(gain, *weights):
        return [(w.astype(f32) * gain.astype(f32)[:, None]).astype(bf16) for w in weights]

    pack_qkv = chip_slices(
        scaled(attn_gain, w_query, w_key, w_value), (q_cols, kv_cols, kv_cols)
    )
    piece_qkv = exchange_chips(pack_qkv).reshape(-1, pack_qkv.shape[-1])
    marks = jnp.stack([positions[:, 0] // 32, positions[:, 0] % 32, segments[:, 0]], axis=-1)
    marks = jnp.pad(marks.astype(bf16), ((0, 0), (0, 0), (0, 125)))
    pair = jnp.concatenate([out_cotangent[:, 0], block_input[:, 0], marks], axis=-1)
    pair = jnp.concatenate([pick(pair, core), core_swap(pick(pair, 1 - core))])
    lower, upper = w_down[: w_down.shape[0] // 2], w_down[w_down.shape[0] // 2 :]
    rows = jnp.concatenate([w_out, lower])
    gate_up = scaled(mlp_gain, w_gate, w_up)
    pack_gu = jnp.stack(
        [
            jnp.concatenate([w[:, n * ff_cols : (n + 1) * ff_cols] for w in gate_up], axis=1)
            for n in range(2 * chips)
        ]
    ).reshape(chips, 2, d_rows, 2 * ff_cols)
    pair, piece_qkv, pack_gu = tie(pair, piece_qkv, pack_gu)
    dy_low, x_low = pair[:, :width], pair[:, width:]

    qkv_right, qkv_left = ring_first(piece_qkv)
    piece_gu = exchange_chips(pack_gu)
    qkv_right, qkv_left, piece_gu, x_low, rows = tie(qkv_right, qkv_left, piece_gu, x_low, rows)
    rows = lax.all_gather(rows, "fsdp", axis=0)

    near = [j for j in range(1, chips) if j & (j - 1) == 0]
    far = [j for j in range(1, chips) if j & (j - 1) != 0]
    x_parts = {0: x_low, **{j: chip_xor(x_low, j) for j in near}}
    found_qkv = ring_rest(piece_qkv, qkv_right, qkv_left)
    piece_gu = core_pair(pick(piece_gu, core, 1), core_swap(pick(piece_gu, 1 - core, 1)), 1)
    piece_gu = piece_gu.reshape(2 * chips * d_rows, 2 * ff_cols)
    order = sorted(x_parts)
    piece_gu, *late = tie(piece_gu, *[x_parts[j] for j in order], *pieces_of(found_qkv))
    x_parts = dict(zip(order, late))
    x_parts.update({j: chip_xor(x_low, j) for j in far})
    x_all = jnp.concatenate([x_parts[j] for j in range(chips)])
    found_qkv = again(found_qkv, late[len(order) :])
    marks = x_all[:, width : width + 3].astype(f32).T
    pos_all, seg_all = marks[0] * 32.0 + marks[1], marks[2]
    x_all, x_low = x_all[:, :width], x_low[:, :width]
    allowed = (seg_all[:, None] == seg_all[None, :]) & (pos_all[None, :] <= pos_all[:, None])
    cosine, sine = rope_tables(pos_all)
    w_qkv = assemble(found_qkv, chips)
    w_qkv = core_pair(w_qkv, core_swap(w_qkv), 1).reshape(width, -1)
    w_qkv, x_all, dy_low, cosine, sine, allowed = tie(w_qkv, x_all, dy_low, cosine, sine, allowed)
    own = x_low.shape[0]
    seq = x_all.shape[0]

    dy_all = gather_chips(dy_low)
    x_full = x_all.astype(f32)
    h_one = (x_full * rms_scale(x_full)).astype(bf16)
    qkv = mm(h_one, w_qkv)
    q_rot = rotate(qkv[:, :q_cols].reshape(seq, kv_heads * 2, HEAD), cosine, sine)
    q_rot = q_rot.astype(bf16).reshape(seq, kv_heads, 2, HEAD)
    k_rot = rotate(
        qkv[:, q_cols : q_cols + kv_cols].reshape(seq, kv_heads, HEAD), cosine, sine
    ).astype(bf16)
    value = qkv[:, q_cols + kv_cols :].astype(bf16).reshape(seq, kv_heads, HEAD)
    q_rot, rows = tie(q_rot, rows)
    along_out = rows[:, : w_out.shape[0]].reshape(-1, width)
    out_w = both_cores(along_out).reshape(-1, width)
    scores = jnp.einsum("sgrh,tgh->grst", q_rot, k_rot, preferred_element_type=f32) * factor
    scores = jnp.where(allowed, scores, -1e30)
    raised = jnp.exp(scores - jnp.max(scores, axis=-1, keepdims=True))
    soft = raised / jnp.sum(raised, axis=-1, keepdims=True)
    soft_low = soft.astype(bf16)
    mixed = jnp.einsum("grst,tgh->sgrh", soft_low, value, preferred_element_type=f32)
    mixed = mixed.astype(bf16).reshape(seq, q_cols)
    mixed, dy_all, out_w = tie(mixed, dy_all, out_w)
    x_own = x_low.astype(f32)
    middle = x_own + scatter_chips(mm(mixed, out_w))

    dy_both = jnp.concatenate([dy_all, core_swap(dy_all)])
    along_gu = lax.all_gather(piece_gu, "fsdp", axis=0, tiled=True)
    middle, dy_both = tie(middle, dy_both)
    scale_two = rms_scale(middle)
    n_two = middle * scale_two
    h_two = gather_chips(n_two.astype(bf16))
    h_two, upper = tie(h_two, upper)
    upper_right, upper_left = ring_first(upper)
    h_both, along_gu, upper_right, upper_left = tie(
        jnp.concatenate([h_two, core_swap(h_two)]), along_gu, upper_right, upper_left
    )
    along_upper = assemble(ring_rest(upper, upper_right, upper_left), 1)[0]
    along_down = jnp.concatenate([rows[:, w_out.shape[0] :], along_upper], axis=1)
    along_down = along_down.reshape(-1, width)
    w_gu = along_gu.reshape(rows_z, 2 * chips, d_rows, 2 * ff_cols)
    w_gu = jnp.transpose(w_gu, (1, 0, 2, 3)).reshape(width, 2 * ff_cols)
    gu = mm(h_both, w_gu)
    gate, up = gu[:, :ff_cols], gu[:, ff_cols:]
    sigma = jax.nn.sigmoid(gate)
    act = (gate * sigma * up).astype(bf16)
    d_act = mm_nt(dy_both, along_down)
    d_gate = (d_act * up * sigma * (1.0 + gate * (1.0 - sigma))).astype(bf16)
    d_up = (d_act * gate * sigma).astype(bf16)
    d_gu = jnp.concatenate([d_gate, d_up], axis=1)
    g_down = mm_tn(act, dy_both).astype(bf16)
    g_down, d_gu = tie(g_down, d_gu)
    g_down = lax.psum_scatter(g_down, "fsdp", scatter_dimension=0, tiled=True)

    def give_partial(rows, weights, product):
        other = core_swap(product(rows[seq:], weights).astype(bf16)).astype(f32)
        return product(rows[:seq], weights) + other

    d_h_two, act = tie(give_partial(d_gu, w_gu, mm_nt), act)
    g_gu = mm_tn(h_both, d_gu).astype(bf16).reshape(2 * chips, rows_z, d_rows, 2 * ff_cols)
    g_gu = jnp.transpose(g_gu, (1, 0, 2, 3)).reshape(width, 2 * ff_cols)
    d_h_two, g_gu = tie(scatter_chips(d_h_two), g_gu)
    g_gu = lax.psum_scatter(g_gu, "fsdp", scatter_dimension=0, tiled=True)

    dy_own = dy_low.astype(f32)
    d_middle = dy_own + norm_back(d_h_two, n_two, scale_two)
    branch = gather_chips(d_middle.astype(bf16))
    partial = give_partial(act, along_down, mm)
    kept, given = partial[:own], partial[own:].astype(bf16)
    branch, kept, given, g_down = tie(branch, kept, given, g_down)

    g_out = mm_tn(mixed, branch).astype(bf16)
    g_out = g_out.reshape(2, g_out.shape[0] // 2, g_out.shape[1])
    g_out = pick(g_out, core) + core_swap(pick(g_out, 1 - core))
    d_mixed = mm_nt(branch, out_w).astype(bf16).reshape(seq, kv_heads, 2, HEAD)
    d_soft = jnp.einsum("sgrh,tgh->grst", d_mixed, value, preferred_element_type=f32)
    d_value = jnp.einsum("grst,sgrh->tgh", soft_low, d_mixed, preferred_element_type=f32)
    inner = jnp.sum(soft * d_soft, axis=-1, keepdims=True)
    d_scores = (soft * (d_soft - inner)).astype(bf16)
    d_q = jnp.einsum("grst,tgh->sgrh", d_scores, k_rot, preferred_element_type=f32) * factor
    d_k = jnp.einsum("grst,sgrh->tgh", d_scores, q_rot, preferred_element_type=f32) * factor
    d_q = unrotate(d_q.reshape(seq, kv_heads * 2, HEAD), cosine, sine)
    d_k = unrotate(d_k, cosine, sine)
    d_qkv = jnp.concatenate(
        [
            d_q.reshape(seq, q_cols).astype(bf16),
            d_k.reshape(seq, kv_cols).astype(bf16),
            d_value.reshape(seq, kv_cols).astype(bf16),
        ],
        axis=1,
    )
    d_qkv, g_out = tie(d_qkv, g_out)
    cols_qkv = d_qkv.shape[1]
    g_qkv = mm_tn(h_one, d_qkv).astype(bf16).reshape(chips, 2, rows_z, d_rows, cols_qkv)
    g_qkv = pick(g_qkv, core, 1) + core_swap(pick(g_qkv, 1 - core, 1))
    g_qkv = jnp.transpose(g_qkv, (1, 0, 2, 3)).reshape(1, rows_z, chips * d_rows, cols_qkv)
    folds = width // cols_qkv
    g_out = g_out.reshape(1, rows_z, d_rows, width)
    g_rest = [g_out[..., k * cols_qkv : (k + 1) * cols_qkv] for k in range(folds)]
    g_rest = jnp.concatenate([g_qkv] + g_rest, axis=2)
    d_h_one = mm_nt(d_qkv, w_qkv)
    g_rest, d_h_one = tie(g_rest.reshape(-1, cols_qkv), d_h_one)
    g_rest = lax.psum_scatter(g_rest, "fsdp", scatter_dimension=0, tiled=True)
    d_h_one, given, g_gu = tie(scatter_chips(d_h_one), given, g_gu)
    result = middle + kept
    for j in range(1, chips):
        result = result + chip_xor(given[(j - 1) * own : j * own], j).astype(f32)
    g_gu = g_gu.reshape(chips, 2, d_rows, 2 * ff_cols)
    g_gu = core_pair(pick(g_gu, core, 1), core_swap(pick(g_gu, 1 - core, 1)), 1)
    g_gu = exchange_chips(g_gu)
    def spread_ff(grad):
        grad = jnp.transpose(grad.astype(f32), (2, 0, 1, 3))
        return grad.reshape(d_rows, 2 * chips * ff_cols)

    g_gate, g_up = spread_ff(g_gu[..., :ff_cols]), spread_ff(g_gu[..., ff_cols:])

    def of_gain(grads, weights):
        return sum(jnp.sum(g * w.astype(f32), axis=1) for g, w in zip(grads, weights))

    def by_gain(gain, grads):
        return [g * gain.astype(f32)[:, None] for g in grads]

    g_mlp_gain = of_gain((g_gate, g_up), (w_gate, w_up))
    g_gate, g_up = by_gain(mlp_gain, (g_gate, g_up))
    result, g_rest, g_gate, g_up, g_mlp_gain = tie(
        result.astype(bf16), g_rest, g_gate, g_up, g_mlp_gain
    )
    scale_one = rms_scale(x_own)
    n_one = x_own * scale_one
    d_input = (d_middle + norm_back(d_h_one, n_one, scale_one)).astype(bf16)

    def give_back(a):
        mine, theirs = a[:tok], core_swap(a[tok:])
        first = core == 0
        return jnp.stack([jnp.where(first, mine, theirs), jnp.where(first, theirs, mine)])[:, None]

    def spread(grad, start, cols):
        part = grad[:, :, start : start + cols].astype(f32)
        return jnp.transpose(part, (1, 0, 2)).reshape(d_rows, chips * cols)

    g_down = g_down.astype(f32)
    result, d_input = give_back(result), give_back(d_input)
    g_rest, g_gate, g_up, g_down, g_mlp_gain, result, d_input = tie(
        g_rest, g_gate, g_up, g_down, g_mlp_gain, result, d_input
    )
    g_qkv = exchange_chips(g_rest[: chips * d_rows].reshape(chips, d_rows, cols_qkv))
    g_out = g_rest[chips * d_rows :].reshape(folds, d_rows, cols_qkv)
    g_out = jnp.transpose(g_out, (1, 0, 2)).reshape(d_rows, width).astype(f32)
    g_query = spread(g_qkv, 0, q_cols)
    g_key = spread(g_qkv, q_cols, kv_cols)
    g_value = spread(g_qkv, q_cols + kv_cols, kv_cols)
    g_attn_gain = of_gain((g_query, g_key, g_value), (w_query, w_key, w_value))
    g_query, g_key, g_value = by_gain(attn_gain, (g_query, g_key, g_value))
    return (
        result,
        d_input,
        g_attn_gain,
        g_query,
        g_key,
        g_value,
        g_out,
        g_mlp_gain,
        g_gate,
        g_up,
        g_down,
    )


def solution(mesh):
    ctx, fsdp = mesh.shape["ctx"], mesh.shape["fsdp"]
    split = Mesh(mesh.devices.reshape(ctx // 2, 2, fsdp), ("chip", "core", "fsdp"))
    ctx_axes = ("chip", "core")
    all_axes = ("chip", "core", "fsdp")
    tokens = P(None, "fsdp", ctx_axes, None)
    marks = P(None, "fsdp", ctx_axes)
    vector, matrix = P(all_axes), P(all_axes, None)
    return jax.shard_map(
        on_device,
        mesh=split,
        in_specs=(
            tokens, marks, marks, tokens, vector, matrix, matrix, matrix, matrix,
            vector, matrix, matrix, matrix,
        ),
        out_specs=(
            tokens, tokens, vector, matrix, matrix, matrix, matrix, vector,
            matrix, matrix, matrix,
        ),
        check_vma=False,
    )
```

```python
import math

import jax
import jax.numpy as jnp
from jax import lax
from jax.sharding import Mesh, PartitionSpec as P

HEADS = 16
KV_HEADS = 8
HEAD = 96
EPS = 1e-05
THETA = 100000.0
f32 = jnp.float32
bf16 = jnp.bfloat16


def rope_tables(position_ids):
    half = HEAD // 2
    ladder = jnp.arange(half).astype(f32) * (2.0 / HEAD)
    inverse = jnp.exp(-math.log(THETA) * ladder)
    angles = position_ids.astype(f32)[:, None] * inverse[None, :]
    return jnp.cos(angles)[:, None, :], jnp.sin(angles)[:, None, :]


def rotate(vectors, cosine, sine):
    half = HEAD // 2
    a, b = vectors[..., :half], vectors[..., half:]
    return jnp.concatenate([a * cosine - b * sine, b * cosine + a * sine], axis=-1)


def unrotate(grads, cosine, sine):
    half = HEAD // 2
    a, b = grads[..., :half], grads[..., half:]
    return jnp.concatenate([a * cosine + b * sine, b * cosine - a * sine], axis=-1)


def rms_scale(values):
    return lax.rsqrt(jnp.mean(values * values, axis=-1, keepdims=True) + EPS)


def norm_back(grad, normed, scale):
    return scale * (grad - normed * jnp.mean(grad * normed, axis=-1, keepdims=True))


def mm(a, b):
    return jnp.dot(a, b, preferred_element_type=f32)


def mm_tn(a, b):
    return jnp.einsum("td,te->de", a, b, preferred_element_type=f32)


def mm_nt(a, b):
    return jnp.einsum("te,de->td", a, b, preferred_element_type=f32)


def on_device(
    block_input,
    positions,
    segments,
    out_cotangent,
    attn_gain,
    w_query,
    w_key,
    w_value,
    w_out,
    mlp_gain,
    w_gate,
    w_up,
    w_down,
):
    chips = lax.axis_size("chip")
    rows_z = lax.axis_size("fsdp")
    chip = lax.axis_index("chip")
    core = lax.axis_index("core")
    place = lax.axis_index("fsdp")
    tok = block_input.shape[2]
    width = block_input.shape[3]
    d_rows = w_query.shape[0]
    q_cols = w_query.shape[1] // chips
    kv_cols = w_key.shape[1] // chips
    ff_cols = w_gate.shape[1] // (2 * chips)
    kv_heads = KV_HEADS // chips
    factor = HEAD ** (-0.5)

    def core_swap(a):
        return lax.ppermute(a, "core", [(0, 1), (1, 0)])

    def chip_xor(a, j):
        return lax.ppermute(a, "chip", [(i, i ^ j) for i in range(chips)])

    def pick(a, index, axis=0):
        return lax.dynamic_index_in_dim(a, index, axis, keepdims=False)

    def gather_chips(a, axis=0):
        return jnp.concatenate([a] + [chip_xor(a, j) for j in range(1, chips)], axis=axis)

    def scatter_chips(a):
        step = a.shape[0] // chips
        total = a[:step]
        for j in range(1, chips):
            total = total + chip_xor(a[j * step : (j + 1) * step].astype(bf16), j).astype(f32)
        return total

    def by_chip(pieces):
        stacked = jnp.stack(pieces)
        bit = 1
        while bit < chips:
            view = stacked.reshape((chips // (2 * bit), 2, bit) + stacked.shape[1:])
            flipped = jnp.flip(view, axis=1)
            stacked = jnp.where((chip & bit) != 0, flipped, view).reshape(stacked.shape)
            bit *= 2
        return stacked

    def exchange_chips(pack):
        pieces = [pick(pack, chip)]
        for j in range(1, chips):
            pieces.append(chip_xor(pick(pack, chip ^ j), j))
        return by_chip(pieces)

    def core_pair(mine, other, axis):
        first = core == 0
        return jnp.stack([jnp.where(first, mine, other), jnp.where(first, other, mine)], axis)

    def both_cores(a):
        return core_pair(a, core_swap(a), 0)

    def chip_slices(weights, cols):
        return jnp.stack(
            [
                jnp.concatenate([w[:, k * n : (k + 1) * n] for w, n in zip(weights, cols)], axis=1)
                for k in range(chips)
            ]
        )

    def tie(*values):
        return lax.optimization_barrier(values)

    def along_z(a, step):
        return lax.ppermute(a, "fsdp", [(i, (i + step) % rows_z) for i in range(rows_z)])

    def ring_first(a):
        return along_z(a, 1), along_z(a, -1)

    def ring_rest(a, right, left):
        found = [(a, 0, 0), (right, -1, 0), (left, 1, 0)]
        for step in range(2, rows_z // 2 + 1):
            if 2 * step == rows_z:
                half = a.shape[-1] // 2
                found.append((along_z(right[..., :half], 1), -step, 0))
                found.append((along_z(left[..., half:], -1), step, half))
            else:
                right, left = along_z(right, 1), along_z(left, -1)
                found += [(right, -step, 0), (left, step, 0)]
        return found

    def assemble(found, groups):
        rows, cols = found[0][0].shape
        whole = jnp.zeros((groups, rows_z, rows // groups, cols), bf16)
        for piece, offset, column in found:
            piece = piece.reshape(groups, 1, rows // groups, piece.shape[-1])
            index = lax.rem(place + offset + rows_z, rows_z)
            whole = lax.dynamic_update_slice(whole, piece, (0, index, 0, column))
        return whole

    def again(found, pieces):
        return [(piece,) + f[1:] for piece, f in zip(pieces, found)]

    def pieces_of(found):
        return [f[0] for f in found]

    def scaled(gain, *weights):
        return [(w.astype(f32) * gain.astype(f32)[:, None]).astype(bf16) for w in weights]

    pack_qkv = chip_slices(
        scaled(attn_gain, w_query, w_key, w_value), (q_cols, kv_cols, kv_cols)
    )
    piece_qkv = exchange_chips(pack_qkv).reshape(-1, pack_qkv.shape[-1])
    marks = jnp.stack([positions[:, 0] // 32, positions[:, 0] % 32, segments[:, 0]], axis=-1)
    marks = jnp.pad(marks.astype(bf16), ((0, 0), (0, 0), (0, 125)))
    pair = jnp.concatenate([out_cotangent[:, 0], block_input[:, 0], marks], axis=-1)
    pair = jnp.concatenate([pick(pair, core), core_swap(pick(pair, 1 - core))])
    lower, upper = w_down[: w_down.shape[0] // 2], w_down[w_down.shape[0] // 2 :]
    rows = jnp.concatenate([w_out, lower])
    gate_up = scaled(mlp_gain, w_gate, w_up)
    pack_gu = jnp.stack(
        [
            jnp.concatenate([w[:, n * ff_cols : (n + 1) * ff_cols] for w in gate_up], axis=1)
            for n in range(2 * chips)
        ]
    ).reshape(chips, 2, d_rows, 2 * ff_cols)
    pair, piece_qkv, pack_gu = tie(pair, piece_qkv, pack_gu)
    dy_low, x_low = pair[:, :width], pair[:, width:]

    qkv_right, qkv_left = ring_first(piece_qkv)
    piece_gu = exchange_chips(pack_gu)
    qkv_right, qkv_left, piece_gu, x_low, rows = tie(qkv_right, qkv_left, piece_gu, x_low, rows)
    rows = lax.all_gather(rows, "fsdp", axis=0)

    near = [j for j in range(1, chips) if j & (j - 1) == 0]
    far = [j for j in range(1, chips) if j & (j - 1) != 0]
    x_parts = {0: x_low, **{j: chip_xor(x_low, j) for j in near}}
    found_qkv = ring_rest(piece_qkv, qkv_right, qkv_left)
    piece_gu = core_pair(pick(piece_gu, core, 1), core_swap(pick(piece_gu, 1 - core, 1)), 1)
    piece_gu = piece_gu.reshape(2 * chips * d_rows, 2 * ff_cols)
    order = sorted(x_parts)
    piece_gu, *late = tie(piece_gu, *[x_parts[j] for j in order], *pieces_of(found_qkv))
    x_parts = dict(zip(order, late))
    x_parts.update({j: chip_xor(x_low, j) for j in far})
    x_all = jnp.concatenate([x_parts[j] for j in range(chips)])
    found_qkv = again(found_qkv, late[len(order) :])
    marks = x_all[:, width : width + 3].astype(f32).T
    pos_all, seg_all = marks[0] * 32.0 + marks[1], marks[2]
    x_all, x_low = x_all[:, :width], x_low[:, :width]
    allowed = (seg_all[:, None] == seg_all[None, :]) & (pos_all[None, :] <= pos_all[:, None])
    cosine, sine = rope_tables(pos_all)
    w_qkv = assemble(found_qkv, chips)
    w_qkv = core_pair(w_qkv, core_swap(w_qkv), 1).reshape(width, -1)
    w_qkv, x_all, dy_low, cosine, sine, allowed = tie(w_qkv, x_all, dy_low, cosine, sine, allowed)
    own = x_low.shape[0]
    seq = x_all.shape[0]

    x_full = x_all.astype(f32)
    h_one = (x_full * rms_scale(x_full)).astype(bf16)
    qkv = mm(h_one, w_qkv)
    q_rot = rotate(qkv[:, :q_cols].reshape(seq, kv_heads * 2, HEAD), cosine, sine)
    q_rot = q_rot.astype(bf16).reshape(seq, kv_heads, 2, HEAD)
    k_rot = rotate(
        qkv[:, q_cols : q_cols + kv_cols].reshape(seq, kv_heads, HEAD), cosine, sine
    ).astype(bf16)
    value = qkv[:, q_cols + kv_cols :].astype(bf16).reshape(seq, kv_heads, HEAD)
    q_rot, rows, dy_low = tie(q_rot, rows, dy_low)
    dy_all = gather_chips(dy_low)
    along_out = rows[:, : w_out.shape[0]].reshape(-1, width)
    out_w = both_cores(along_out).reshape(-1, width)
    scores = jnp.einsum("sgrh,tgh->grst", q_rot, k_rot, preferred_element_type=f32) * factor
    scores = jnp.where(allowed, scores, -1e30)
    raised = jnp.exp(scores - jnp.max(scores, axis=-1, keepdims=True))
    soft = raised / jnp.sum(raised, axis=-1, keepdims=True)
    soft_low = soft.astype(bf16)
    mixed = jnp.einsum("grst,tgh->sgrh", soft_low, value, preferred_element_type=f32)
    mixed = mixed.astype(bf16).reshape(seq, q_cols)
    mixed, dy_all, out_w = tie(mixed, dy_all, out_w)
    x_own = x_low.astype(f32)
    middle = x_own + scatter_chips(mm(mixed, out_w))

    dy_both = jnp.concatenate([dy_all, core_swap(dy_all)])
    along_gu = lax.all_gather(piece_gu, "fsdp", axis=0, tiled=True)
    middle, dy_both = tie(middle, dy_both)
    scale_two = rms_scale(middle)
    n_two = middle * scale_two
    h_two = gather_chips(n_two.astype(bf16))
    h_two, upper = tie(h_two, upper)
    upper_right, upper_left = ring_first(upper)
    h_both, along_gu, upper_right, upper_left = tie(
        jnp.concatenate([h_two, core_swap(h_two)]), along_gu, upper_right, upper_left
    )
    along_upper = assemble(ring_rest(upper, upper_right, upper_left), 1)[0]
    along_down = jnp.concatenate([rows[:, w_out.shape[0] :], along_upper], axis=1)
    along_down = along_down.reshape(-1, width)
    w_gu = along_gu.reshape(rows_z, 2 * chips, d_rows, 2 * ff_cols)
    w_gu = jnp.transpose(w_gu, (1, 0, 2, 3)).reshape(width, 2 * ff_cols)
    gu = mm(h_both, w_gu)
    gate, up = gu[:, :ff_cols], gu[:, ff_cols:]
    sigma = jax.nn.sigmoid(gate)
    act = (gate * sigma * up).astype(bf16)
    d_act = mm_nt(dy_both, along_down)
    d_gate = (d_act * up * sigma * (1.0 + gate * (1.0 - sigma))).astype(bf16)
    d_up = (d_act * gate * sigma).astype(bf16)
    d_gu = jnp.concatenate([d_gate, d_up], axis=1)
    g_down = mm_tn(act, dy_both).astype(bf16)
    g_down, d_gu = tie(g_down, d_gu)
    g_down = lax.psum_scatter(g_down, "fsdp", scatter_dimension=0, tiled=True)

    def give_partial(rows, weights, product):
        other = core_swap(product(rows[seq:], weights).astype(bf16)).astype(f32)
        return product(rows[:seq], weights) + other

    d_h_two, act = tie(give_partial(d_gu, w_gu, mm_nt), act)
    g_gu = mm_tn(h_both, d_gu).astype(bf16).reshape(2 * chips, rows_z, d_rows, 2 * ff_cols)
    g_gu = jnp.transpose(g_gu, (1, 0, 2, 3)).reshape(width, 2 * ff_cols)
    d_h_two, g_gu = tie(scatter_chips(d_h_two), g_gu)
    g_gu = lax.psum_scatter(g_gu, "fsdp", scatter_dimension=0, tiled=True)

    dy_own = dy_low.astype(f32)
    d_middle = dy_own + norm_back(d_h_two, n_two, scale_two)
    branch = gather_chips(d_middle.astype(bf16))
    partial = give_partial(act, along_down, mm)
    kept, given = partial[:own], partial[own:].astype(bf16)
    branch, kept, given, g_down = tie(branch, kept, given, g_down)

    g_out = mm_tn(mixed, branch).astype(bf16)
    g_out = g_out.reshape(2, g_out.shape[0] // 2, g_out.shape[1])
    g_out = pick(g_out, core) + core_swap(pick(g_out, 1 - core))
    d_mixed = mm_nt(branch, out_w).astype(bf16).reshape(seq, kv_heads, 2, HEAD)
    d_soft = jnp.einsum("sgrh,tgh->grst", d_mixed, value, preferred_element_type=f32)
    d_value = jnp.einsum("grst,sgrh->tgh", soft_low, d_mixed, preferred_element_type=f32)
    inner = jnp.sum(soft * d_soft, axis=-1, keepdims=True)
    d_scores = (soft * (d_soft - inner)).astype(bf16)
    d_q = jnp.einsum("grst,tgh->sgrh", d_scores, k_rot, preferred_element_type=f32) * factor
    d_k = jnp.einsum("grst,sgrh->tgh", d_scores, q_rot, preferred_element_type=f32) * factor
    d_q = unrotate(d_q.reshape(seq, kv_heads * 2, HEAD), cosine, sine)
    d_k = unrotate(d_k, cosine, sine)
    d_qkv = jnp.concatenate(
        [
            d_q.reshape(seq, q_cols).astype(bf16),
            d_k.reshape(seq, kv_cols).astype(bf16),
            d_value.reshape(seq, kv_cols).astype(bf16),
        ],
        axis=1,
    )
    d_qkv, g_out = tie(d_qkv, g_out)
    cols_qkv = d_qkv.shape[1]
    g_qkv = mm_tn(h_one, d_qkv).astype(bf16).reshape(chips, 2, rows_z, d_rows, cols_qkv)
    g_qkv = pick(g_qkv, core, 1) + core_swap(pick(g_qkv, 1 - core, 1))
    g_qkv = jnp.transpose(g_qkv, (1, 0, 2, 3)).reshape(1, rows_z, chips * d_rows, cols_qkv)
    folds = width // cols_qkv
    g_out = g_out.reshape(1, rows_z, d_rows, width)
    g_rest = [g_out[..., k * cols_qkv : (k + 1) * cols_qkv] for k in range(folds)]
    g_rest = jnp.concatenate([g_qkv] + g_rest, axis=2)
    d_h_one = mm_nt(d_qkv, w_qkv)
    g_rest, d_h_one = tie(g_rest.reshape(-1, cols_qkv), d_h_one)
    g_rest = lax.psum_scatter(g_rest, "fsdp", scatter_dimension=0, tiled=True)
    d_h_one, given, g_gu = tie(scatter_chips(d_h_one), given, g_gu)
    result = middle + kept
    for j in range(1, chips):
        result = result + chip_xor(given[(j - 1) * own : j * own], j).astype(f32)
    g_gu = g_gu.reshape(chips, 2, d_rows, 2 * ff_cols)
    g_gu = core_pair(pick(g_gu, core, 1), core_swap(pick(g_gu, 1 - core, 1)), 1)
    g_gu = exchange_chips(g_gu)
    def spread_ff(grad):
        grad = jnp.transpose(grad.astype(f32), (2, 0, 1, 3))
        return grad.reshape(d_rows, 2 * chips * ff_cols)

    g_gate, g_up = spread_ff(g_gu[..., :ff_cols]), spread_ff(g_gu[..., ff_cols:])

    def of_gain(grads, weights):
        return sum(jnp.sum(g * w.astype(f32), axis=1) for g, w in zip(grads, weights))

    def by_gain(gain, grads):
        return [g * gain.astype(f32)[:, None] for g in grads]

    g_mlp_gain = of_gain((g_gate, g_up), (w_gate, w_up))
    g_gate, g_up = by_gain(mlp_gain, (g_gate, g_up))
    result, g_rest, g_gate, g_up, g_mlp_gain = tie(
        result.astype(bf16), g_rest, g_gate, g_up, g_mlp_gain
    )
    scale_one = rms_scale(x_own)
    n_one = x_own * scale_one
    d_input = (d_middle + norm_back(d_h_one, n_one, scale_one)).astype(bf16)

    def give_back(a):
        mine, theirs = a[:tok], core_swap(a[tok:])
        first = core == 0
        return jnp.stack([jnp.where(first, mine, theirs), jnp.where(first, theirs, mine)])[:, None]

    def spread(grad, start, cols):
        part = grad[:, :, start : start + cols].astype(f32)
        return jnp.transpose(part, (1, 0, 2)).reshape(d_rows, chips * cols)

    g_down = g_down.astype(f32)
    result, d_input = give_back(result), give_back(d_input)
    g_rest, g_gate, g_up, g_down, g_mlp_gain, result, d_input = tie(
        g_rest, g_gate, g_up, g_down, g_mlp_gain, result, d_input
    )
    g_qkv = exchange_chips(g_rest[: chips * d_rows].reshape(chips, d_rows, cols_qkv))
    g_out = g_rest[chips * d_rows :].reshape(folds, d_rows, cols_qkv)
    g_out = jnp.transpose(g_out, (1, 0, 2)).reshape(d_rows, width).astype(f32)
    g_query = spread(g_qkv, 0, q_cols)
    g_key = spread(g_qkv, q_cols, kv_cols)
    g_value = spread(g_qkv, q_cols + kv_cols, kv_cols)
    g_attn_gain = of_gain((g_query, g_key, g_value), (w_query, w_key, w_value))
    g_query, g_key, g_value = by_gain(attn_gain, (g_query, g_key, g_value))
    return (
        result,
        d_input,
        g_attn_gain,
        g_query,
        g_key,
        g_value,
        g_out,
        g_mlp_gain,
        g_gate,
        g_up,
        g_down,
    )


def solution(mesh):
    ctx, fsdp = mesh.shape["ctx"], mesh.shape["fsdp"]
    split = Mesh(mesh.devices.reshape(ctx // 2, 2, fsdp), ("chip", "core", "fsdp"))
    ctx_axes = ("chip", "core")
    all_axes = ("chip", "core", "fsdp")
    tokens = P(None, "fsdp", ctx_axes, None)
    marks = P(None, "fsdp", ctx_axes)
    vector, matrix = P(all_axes), P(all_axes, None)
    return jax.shard_map(
        on_device,
        mesh=split,
        in_specs=(
            tokens, marks, marks, tokens, vector, matrix, matrix, matrix, matrix,
            vector, matrix, matrix, matrix,
        ),
        out_specs=(
            tokens, tokens, vector, matrix, matrix, matrix, matrix, vector,
            matrix, matrix, matrix,
        ),
        check_vma=False,
    )
```

```python
import math

import jax
import jax.numpy as jnp
from jax import lax
from jax.sharding import Mesh, PartitionSpec as P

HEADS = 16
KV_HEADS = 8
HEAD = 96
EPS = 1e-05
THETA = 100000.0
f32 = jnp.float32
bf16 = jnp.bfloat16


def rope_tables(position_ids):
    half = HEAD // 2
    ladder = jnp.arange(half).astype(f32) * (2.0 / HEAD)
    inverse = jnp.exp(-math.log(THETA) * ladder)
    angles = position_ids.astype(f32)[:, None] * inverse[None, :]
    return jnp.cos(angles)[:, None, :], jnp.sin(angles)[:, None, :]


def rotate(vectors, cosine, sine):
    half = HEAD // 2
    a, b = vectors[..., :half], vectors[..., half:]
    return jnp.concatenate([a * cosine - b * sine, b * cosine + a * sine], axis=-1)


def unrotate(grads, cosine, sine):
    half = HEAD // 2
    a, b = grads[..., :half], grads[..., half:]
    return jnp.concatenate([a * cosine + b * sine, b * cosine - a * sine], axis=-1)


def rms_scale(values):
    return lax.rsqrt(jnp.mean(values * values, axis=-1, keepdims=True) + EPS)


def norm_back(grad, normed, scale):
    return scale * (grad - normed * jnp.mean(grad * normed, axis=-1, keepdims=True))


def mm(a, b):
    return jnp.dot(a, b, preferred_element_type=f32)


def mm_tn(a, b):
    return jnp.einsum("td,te->de", a, b, preferred_element_type=f32)


def mm_nt(a, b):
    return jnp.einsum("te,de->td", a, b, preferred_element_type=f32)


def on_device(
    block_input,
    positions,
    segments,
    out_cotangent,
    attn_gain,
    w_query,
    w_key,
    w_value,
    w_out,
    mlp_gain,
    w_gate,
    w_up,
    w_down,
):
    chips = lax.axis_size("chip")
    rows_z = lax.axis_size("fsdp")
    chip = lax.axis_index("chip")
    core = lax.axis_index("core")
    place = lax.axis_index("fsdp")
    tok = block_input.shape[2]
    width = block_input.shape[3]
    d_rows = w_query.shape[0]
    q_cols = w_query.shape[1] // chips
    kv_cols = w_key.shape[1] // chips
    ff_cols = w_gate.shape[1] // (2 * chips)
    kv_heads = KV_HEADS // chips
    factor = HEAD ** (-0.5)

    def core_swap(a):
        return lax.ppermute(a, "core", [(0, 1), (1, 0)])

    def chip_xor(a, j):
        return lax.ppermute(a, "chip", [(i, i ^ j) for i in range(chips)])

    def pick(a, index, axis=0):
        return lax.dynamic_index_in_dim(a, index, axis, keepdims=False)

    def gather_chips(a, axis=0):
        return jnp.concatenate([a] + [chip_xor(a, j) for j in range(1, chips)], axis=axis)

    def scatter_chips(a):
        step = a.shape[0] // chips
        total = a[:step]
        for j in range(1, chips):
            total = total + chip_xor(a[j * step : (j + 1) * step].astype(bf16), j).astype(f32)
        return total

    def by_chip(pieces):
        stacked = jnp.stack(pieces)
        bit = 1
        while bit < chips:
            view = stacked.reshape((chips // (2 * bit), 2, bit) + stacked.shape[1:])
            flipped = jnp.flip(view, axis=1)
            stacked = jnp.where((chip & bit) != 0, flipped, view).reshape(stacked.shape)
            bit *= 2
        return stacked

    def exchange_chips(pack):
        pieces = [pick(pack, chip)]
        for j in range(1, chips):
            pieces.append(chip_xor(pick(pack, chip ^ j), j))
        return by_chip(pieces)

    def core_pair(mine, other, axis):
        first = core == 0
        return jnp.stack([jnp.where(first, mine, other), jnp.where(first, other, mine)], axis)

    def both_cores(a):
        return core_pair(a, core_swap(a), 0)

    def chip_slices(weights, cols):
        return jnp.stack(
            [
                jnp.concatenate([w[:, k * n : (k + 1) * n] for w, n in zip(weights, cols)], axis=1)
                for k in range(chips)
            ]
        )

    def tie(*values):
        return lax.optimization_barrier(values)

    def along_z(a, step):
        return lax.ppermute(a, "fsdp", [(i, (i + step) % rows_z) for i in range(rows_z)])

    def ring_first(a):
        return along_z(a, 1), along_z(a, -1)

    def ring_rest(a, right, left):
        found = [(a, 0, 0), (right, -1, 0), (left, 1, 0)]
        for step in range(2, rows_z // 2 + 1):
            if 2 * step == rows_z:
                half = a.shape[-1] // 2
                found.append((along_z(right[..., :half], 1), -step, 0))
                found.append((along_z(left[..., half:], -1), step, half))
            else:
                right, left = along_z(right, 1), along_z(left, -1)
                found += [(right, -step, 0), (left, step, 0)]
        return found

    def assemble(found, groups):
        rows, cols = found[0][0].shape
        whole = jnp.zeros((groups, rows_z, rows // groups, cols), bf16)
        for piece, offset, column in found:
            piece = piece.reshape(groups, 1, rows // groups, piece.shape[-1])
            index = lax.rem(place + offset + rows_z, rows_z)
            whole = lax.dynamic_update_slice(whole, piece, (0, index, 0, column))
        return whole

    def again(found, pieces):
        return [(piece,) + f[1:] for piece, f in zip(pieces, found)]

    def pieces_of(found):
        return [f[0] for f in found]

    def scaled(gain, *weights):
        return [(w.astype(f32) * gain.astype(f32)[:, None]).astype(bf16) for w in weights]

    pack_qkv = chip_slices(
        scaled(attn_gain, w_query, w_key, w_value), (q_cols, kv_cols, kv_cols)
    )
    piece_qkv = exchange_chips(pack_qkv).reshape(-1, pack_qkv.shape[-1])
    marks = jnp.stack([positions[:, 0] // 32, positions[:, 0] % 32, segments[:, 0]], axis=-1)
    marks = jnp.pad(marks.astype(bf16), ((0, 0), (0, 0), (0, 125)))
    pair = jnp.concatenate([out_cotangent[:, 0], block_input[:, 0], marks], axis=-1)
    pair = jnp.concatenate([pick(pair, core), core_swap(pick(pair, 1 - core))])
    lower, upper = w_down[: w_down.shape[0] // 2], w_down[w_down.shape[0] // 2 :]
    rows = jnp.concatenate([w_out, lower])
    gate_up = scaled(mlp_gain, w_gate, w_up)
    pack_gu = jnp.stack(
        [
            jnp.concatenate([w[:, n * ff_cols : (n + 1) * ff_cols] for w in gate_up], axis=1)
            for n in range(2 * chips)
        ]
    ).reshape(chips, 2, d_rows, 2 * ff_cols)
    pair, piece_qkv, pack_gu = tie(pair, piece_qkv, pack_gu)
    dy_low, x_low = pair[:, :width], pair[:, width:]

    qkv_right, qkv_left = ring_first(piece_qkv)
    piece_gu = exchange_chips(pack_gu)
    qkv_right, qkv_left, piece_gu, x_low, rows = tie(qkv_right, qkv_left, piece_gu, x_low, rows)
    rows = lax.all_gather(rows, "fsdp", axis=0)

    near = [j for j in range(1, chips) if j & (j - 1) == 0]
    far = [j for j in range(1, chips) if j & (j - 1) != 0]
    x_parts = {0: x_low, **{j: chip_xor(x_low, j) for j in near}}
    found_qkv = ring_rest(piece_qkv, qkv_right, qkv_left)
    piece_gu = core_pair(pick(piece_gu, core, 1), core_swap(pick(piece_gu, 1 - core, 1)), 1)
    piece_gu = piece_gu.reshape(2 * chips * d_rows, 2 * ff_cols)
    order = sorted(x_parts)
    piece_gu, *late = tie(piece_gu, *[x_parts[j] for j in order], *pieces_of(found_qkv))
    x_parts = dict(zip(order, late))
    x_parts.update({j: chip_xor(x_low, j) for j in far})
    x_all = jnp.concatenate([x_parts[j] for j in range(chips)])
    found_qkv = again(found_qkv, late[len(order) :])
    marks = x_all[:, width : width + 3].astype(f32).T
    pos_all, seg_all = marks[0] * 32.0 + marks[1], marks[2]
    x_all, x_low = x_all[:, :width], x_low[:, :width]
    allowed = (seg_all[:, None] == seg_all[None, :]) & (pos_all[None, :] <= pos_all[:, None])
    cosine, sine = rope_tables(pos_all)
    w_qkv = assemble(found_qkv, chips)
    w_qkv = core_pair(w_qkv, core_swap(w_qkv), 1).reshape(width, -1)
    w_qkv, x_all, dy_low, cosine, sine, allowed = tie(w_qkv, x_all, dy_low, cosine, sine, allowed)
    own = x_low.shape[0]
    seq = x_all.shape[0]

    dy_all = gather_chips(dy_low)
    x_full = x_all.astype(f32)
    h_one = (x_full * rms_scale(x_full)).astype(bf16)
    qkv = mm(h_one, w_qkv)
    q_rot = rotate(qkv[:, :q_cols].reshape(seq, kv_heads * 2, HEAD), cosine, sine)
    q_rot = q_rot.astype(bf16).reshape(seq, kv_heads, 2, HEAD)
    k_rot = rotate(
        qkv[:, q_cols : q_cols + kv_cols].reshape(seq, kv_heads, HEAD), cosine, sine
    ).astype(bf16)
    value = qkv[:, q_cols + kv_cols :].astype(bf16).reshape(seq, kv_heads, HEAD)
    scores = jnp.einsum("sgrh,tgh->grst", q_rot, k_rot, preferred_element_type=f32) * factor
    scores = jnp.where(allowed, scores, -1e30)
    raised = jnp.exp(scores - jnp.max(scores, axis=-1, keepdims=True))
    soft = raised / jnp.sum(raised, axis=-1, keepdims=True)
    soft_low, rows = tie(soft.astype(bf16), rows)
    along_out = rows[:, : w_out.shape[0]].reshape(-1, width)
    out_w = both_cores(along_out).reshape(-1, width)
    mixed = jnp.einsum("grst,tgh->sgrh", soft_low, value, preferred_element_type=f32)
    mixed = mixed.astype(bf16).reshape(seq, q_cols)
    mixed, dy_all, out_w = tie(mixed, dy_all, out_w)
    x_own = x_low.astype(f32)
    middle = x_own + scatter_chips(mm(mixed, out_w))

    dy_both = jnp.concatenate([dy_all, core_swap(dy_all)])
    along_gu = lax.all_gather(piece_gu, "fsdp", axis=0, tiled=True)
    middle, dy_both = tie(middle, dy_both)
    scale_two = rms_scale(middle)
    n_two = middle * scale_two
    h_two = gather_chips(n_two.astype(bf16))
    h_two, upper = tie(h_two, upper)
    upper_right, upper_left = ring_first(upper)
    h_both, along_gu, upper_right, upper_left = tie(
        jnp.concatenate([h_two, core_swap(h_two)]), along_gu, upper_right, upper_left
    )
    along_upper = assemble(ring_rest(upper, upper_right, upper_left), 1)[0]
    along_down = jnp.concatenate([rows[:, w_out.shape[0] :], along_upper], axis=1)
    along_down = along_down.reshape(-1, width)
    w_gu = along_gu.reshape(rows_z, 2 * chips, d_rows, 2 * ff_cols)
    w_gu = jnp.transpose(w_gu, (1, 0, 2, 3)).reshape(width, 2 * ff_cols)
    gu = mm(h_both, w_gu)
    gate, up = gu[:, :ff_cols], gu[:, ff_cols:]
    sigma = jax.nn.sigmoid(gate)
    act = (gate * sigma * up).astype(bf16)
    d_act = mm_nt(dy_both, along_down)
    d_gate = (d_act * up * sigma * (1.0 + gate * (1.0 - sigma))).astype(bf16)
    d_up = (d_act * gate * sigma).astype(bf16)
    d_gu = jnp.concatenate([d_gate, d_up], axis=1)
    g_down = mm_tn(act, dy_both).astype(bf16)
    g_down, d_gu = tie(g_down, d_gu)
    g_down = lax.psum_scatter(g_down, "fsdp", scatter_dimension=0, tiled=True)

    def give_partial(rows, weights, product):
        other = core_swap(product(rows[seq:], weights).astype(bf16)).astype(f32)
        return product(rows[:seq], weights) + other

    d_h_two, act = tie(give_partial(d_gu, w_gu, mm_nt), act)
    g_gu = mm_tn(h_both, d_gu).astype(bf16).reshape(2 * chips, rows_z, d_rows, 2 * ff_cols)
    g_gu = jnp.transpose(g_gu, (1, 0, 2, 3)).reshape(width, 2 * ff_cols)
    d_h_two, g_gu = tie(scatter_chips(d_h_two), g_gu)
    g_gu = lax.psum_scatter(g_gu, "fsdp", scatter_dimension=0, tiled=True)

    dy_own = dy_low.astype(f32)
    d_middle = dy_own + norm_back(d_h_two, n_two, scale_two)
    branch = gather_chips(d_middle.astype(bf16))
    partial = give_partial(act, along_down, mm)
    kept, given = partial[:own], partial[own:].astype(bf16)
    branch, kept, given, g_down = tie(branch, kept, given, g_down)

    g_out = mm_tn(mixed, branch).astype(bf16)
    g_out = g_out.reshape(2, g_out.shape[0] // 2, g_out.shape[1])
    g_out = pick(g_out, core) + core_swap(pick(g_out, 1 - core))
    d_mixed = mm_nt(branch, out_w).astype(bf16).reshape(seq, kv_heads, 2, HEAD)
    d_soft = jnp.einsum("sgrh,tgh->grst", d_mixed, value, preferred_element_type=f32)
    d_value = jnp.einsum("grst,sgrh->tgh", soft_low, d_mixed, preferred_element_type=f32)
    inner = jnp.sum(soft * d_soft, axis=-1, keepdims=True)
    d_scores = (soft * (d_soft - inner)).astype(bf16)
    d_q = jnp.einsum("grst,tgh->sgrh", d_scores, k_rot, preferred_element_type=f32) * factor
    d_k = jnp.einsum("grst,sgrh->tgh", d_scores, q_rot, preferred_element_type=f32) * factor
    d_q = unrotate(d_q.reshape(seq, kv_heads * 2, HEAD), cosine, sine)
    d_k = unrotate(d_k, cosine, sine)
    d_qkv = jnp.concatenate(
        [
            d_q.reshape(seq, q_cols).astype(bf16),
            d_k.reshape(seq, kv_cols).astype(bf16),
            d_value.reshape(seq, kv_cols).astype(bf16),
        ],
        axis=1,
    )
    d_qkv, g_out = tie(d_qkv, g_out)
    cols_qkv = d_qkv.shape[1]
    g_qkv = mm_tn(h_one, d_qkv).astype(bf16).reshape(chips, 2, rows_z, d_rows, cols_qkv)
    g_qkv = pick(g_qkv, core, 1) + core_swap(pick(g_qkv, 1 - core, 1))
    g_qkv = jnp.transpose(g_qkv, (1, 0, 2, 3)).reshape(1, rows_z, chips * d_rows, cols_qkv)
    folds = width // cols_qkv
    g_out = g_out.reshape(1, rows_z, d_rows, width)
    g_rest = [g_out[..., k * cols_qkv : (k + 1) * cols_qkv] for k in range(folds)]
    g_rest = jnp.concatenate([g_qkv] + g_rest, axis=2)
    d_h_one = mm_nt(d_qkv, w_qkv)
    g_rest, d_h_one = tie(g_rest.reshape(-1, cols_qkv), d_h_one)
    g_rest = lax.psum_scatter(g_rest, "fsdp", scatter_dimension=0, tiled=True)
    d_h_one, given, g_gu = tie(scatter_chips(d_h_one), given, g_gu)
    result = middle + kept
    for j in range(1, chips):
        result = result + chip_xor(given[(j - 1) * own : j * own], j).astype(f32)
    g_gu = g_gu.reshape(chips, 2, d_rows, 2 * ff_cols)
    g_gu = core_pair(pick(g_gu, core, 1), core_swap(pick(g_gu, 1 - core, 1)), 1)
    g_gu = exchange_chips(g_gu)
    def spread_ff(grad):
        grad = jnp.transpose(grad.astype(f32), (2, 0, 1, 3))
        return grad.reshape(d_rows, 2 * chips * ff_cols)

    g_gate, g_up = spread_ff(g_gu[..., :ff_cols]), spread_ff(g_gu[..., ff_cols:])

    def of_gain(grads, weights):
        return sum(jnp.sum(g * w.astype(f32), axis=1) for g, w in zip(grads, weights))

    def by_gain(gain, grads):
        return [g * gain.astype(f32)[:, None] for g in grads]

    g_mlp_gain = of_gain((g_gate, g_up), (w_gate, w_up))
    g_gate, g_up = by_gain(mlp_gain, (g_gate, g_up))
    result, g_rest, g_gate, g_up, g_mlp_gain = tie(
        result.astype(bf16), g_rest, g_gate, g_up, g_mlp_gain
    )
    scale_one = rms_scale(x_own)
    n_one = x_own * scale_one
    d_input = (d_middle + norm_back(d_h_one, n_one, scale_one)).astype(bf16)

    def give_back(a):
        mine, theirs = a[:tok], core_swap(a[tok:])
        first = core == 0
        return jnp.stack([jnp.where(first, mine, theirs), jnp.where(first, theirs, mine)])[:, None]

    def spread(grad, start, cols):
        part = grad[:, :, start : start + cols].astype(f32)
        return jnp.transpose(part, (1, 0, 2)).reshape(d_rows, chips * cols)

    g_down = g_down.astype(f32)
    result, d_input = give_back(result), give_back(d_input)
    g_rest, g_gate, g_up, g_down, g_mlp_gain, result, d_input = tie(
        g_rest, g_gate, g_up, g_down, g_mlp_gain, result, d_input
    )
    g_qkv = exchange_chips(g_rest[: chips * d_rows].reshape(chips, d_rows, cols_qkv))
    g_out = g_rest[chips * d_rows :].reshape(folds, d_rows, cols_qkv)
    g_out = jnp.transpose(g_out, (1, 0, 2)).reshape(d_rows, width).astype(f32)
    g_query = spread(g_qkv, 0, q_cols)
    g_key = spread(g_qkv, q_cols, kv_cols)
    g_value = spread(g_qkv, q_cols + kv_cols, kv_cols)
    g_attn_gain = of_gain((g_query, g_key, g_value), (w_query, w_key, w_value))
    g_query, g_key, g_value = by_gain(attn_gain, (g_query, g_key, g_value))
    return (
        result,
        d_input,
        g_attn_gain,
        g_query,
        g_key,
        g_value,
        g_out,
        g_mlp_gain,
        g_gate,
        g_up,
        g_down,
    )


def solution(mesh):
    ctx, fsdp = mesh.shape["ctx"], mesh.shape["fsdp"]
    split = Mesh(mesh.devices.reshape(ctx // 2, 2, fsdp), ("chip", "core", "fsdp"))
    ctx_axes = ("chip", "core")
    all_axes = ("chip", "core", "fsdp")
    tokens = P(None, "fsdp", ctx_axes, None)
    marks = P(None, "fsdp", ctx_axes)
    vector, matrix = P(all_axes), P(all_axes, None)
    return jax.shard_map(
        on_device,
        mesh=split,
        in_specs=(
            tokens, marks, marks, tokens, vector, matrix, matrix, matrix, matrix,
            vector, matrix, matrix, matrix,
        ),
        out_specs=(
            tokens, tokens, vector, matrix, matrix, matrix, matrix, vector,
            matrix, matrix, matrix,
        ),
        check_vma=False,
    )
```

```python
import math

import jax
import jax.numpy as jnp
from jax import lax
from jax.sharding import Mesh, PartitionSpec as P

HEADS = 16
KV_HEADS = 8
HEAD = 96
EPS = 1e-05
THETA = 100000.0
f32 = jnp.float32
bf16 = jnp.bfloat16


def rope_tables(position_ids):
    half = HEAD // 2
    ladder = jnp.arange(half).astype(f32) * (2.0 / HEAD)
    inverse = jnp.exp(-math.log(THETA) * ladder)
    angles = position_ids.astype(f32)[:, None] * inverse[None, :]
    return jnp.cos(angles)[:, None, :], jnp.sin(angles)[:, None, :]


def rotate(vectors, cosine, sine):
    half = HEAD // 2
    a, b = vectors[..., :half], vectors[..., half:]
    return jnp.concatenate([a * cosine - b * sine, b * cosine + a * sine], axis=-1)


def unrotate(grads, cosine, sine):
    half = HEAD // 2
    a, b = grads[..., :half], grads[..., half:]
    return jnp.concatenate([a * cosine + b * sine, b * cosine - a * sine], axis=-1)


def rms_scale(values):
    return lax.rsqrt(jnp.mean(values * values, axis=-1, keepdims=True) + EPS)


def norm_back(grad, normed, scale):
    return scale * (grad - normed * jnp.mean(grad * normed, axis=-1, keepdims=True))


def mm(a, b):
    return jnp.dot(a, b, preferred_element_type=f32)


def mm_tn(a, b):
    return jnp.einsum("td,te->de", a, b, preferred_element_type=f32)


def mm_nt(a, b):
    return jnp.einsum("te,de->td", a, b, preferred_element_type=f32)


def on_device(
    block_input,
    positions,
    segments,
    out_cotangent,
    attn_gain,
    w_query,
    w_key,
    w_value,
    w_out,
    mlp_gain,
    w_gate,
    w_up,
    w_down,
):
    chips = lax.axis_size("chip")
    rows_z = lax.axis_size("fsdp")
    chip = lax.axis_index("chip")
    core = lax.axis_index("core")
    place = lax.axis_index("fsdp")
    tok = block_input.shape[2]
    width = block_input.shape[3]
    d_rows = w_query.shape[0]
    q_cols = w_query.shape[1] // chips
    kv_cols = w_key.shape[1] // chips
    ff_cols = w_gate.shape[1] // (2 * chips)
    kv_heads = KV_HEADS // chips
    factor = HEAD ** (-0.5)

    def core_swap(a):
        return lax.ppermute(a, "core", [(0, 1), (1, 0)])

    def chip_xor(a, j):
        return lax.ppermute(a, "chip", [(i, i ^ j) for i in range(chips)])

    def pick(a, index, axis=0):
        return lax.dynamic_index_in_dim(a, index, axis, keepdims=False)

    def gather_chips(a, axis=0):
        return jnp.concatenate([a] + [chip_xor(a, j) for j in range(1, chips)], axis=axis)

    def scatter_chips(a):
        step = a.shape[0] // chips
        total = a[:step]
        for j in range(1, chips):
            total = total + chip_xor(a[j * step : (j + 1) * step].astype(bf16), j).astype(f32)
        return total

    def by_chip(pieces):
        stacked = jnp.stack(pieces)
        bit = 1
        while bit < chips:
            view = stacked.reshape((chips // (2 * bit), 2, bit) + stacked.shape[1:])
            flipped = jnp.flip(view, axis=1)
            stacked = jnp.where((chip & bit) != 0, flipped, view).reshape(stacked.shape)
            bit *= 2
        return stacked

    def exchange_chips(pack):
        pieces = [pick(pack, chip)]
        for j in range(1, chips):
            pieces.append(chip_xor(pick(pack, chip ^ j), j))
        return by_chip(pieces)

    def core_pair(mine, other, axis):
        first = core == 0
        return jnp.stack([jnp.where(first, mine, other), jnp.where(first, other, mine)], axis)

    def both_cores(a):
        return core_pair(a, core_swap(a), 0)

    def chip_slices(weights, cols):
        return jnp.stack(
            [
                jnp.concatenate([w[:, k * n : (k + 1) * n] for w, n in zip(weights, cols)], axis=1)
                for k in range(chips)
            ]
        )

    def tie(*values):
        return lax.optimization_barrier(values)

    def along_z(a, step):
        return lax.ppermute(a, "fsdp", [(i, (i + step) % rows_z) for i in range(rows_z)])

    def ring_first(a):
        return along_z(a, 1), along_z(a, -1)

    def ring_rest(a, right, left):
        found = [(a, 0, 0), (right, -1, 0), (left, 1, 0)]
        for step in range(2, rows_z // 2 + 1):
            if 2 * step == rows_z:
                half = a.shape[-1] // 2
                found.append((along_z(right[..., :half], 1), -step, 0))
                found.append((along_z(left[..., half:], -1), step, half))
            else:
                right, left = along_z(right, 1), along_z(left, -1)
                found += [(right, -step, 0), (left, step, 0)]
        return found

    def assemble(found, groups):
        rows, cols = found[0][0].shape
        whole = jnp.zeros((groups, rows_z, rows // groups, cols), bf16)
        for piece, offset, column in found:
            piece = piece.reshape(groups, 1, rows // groups, piece.shape[-1])
            index = lax.rem(place + offset + rows_z, rows_z)
            whole = lax.dynamic_update_slice(whole, piece, (0, index, 0, column))
        return whole

    def again(found, pieces):
        return [(piece,) + f[1:] for piece, f in zip(pieces, found)]

    def pieces_of(found):
        return [f[0] for f in found]

    def scaled(gain, *weights):
        return [(w.astype(f32) * gain.astype(f32)[:, None]).astype(bf16) for w in weights]

    pack_qkv = chip_slices(
        scaled(attn_gain, w_query, w_key, w_value), (q_cols, kv_cols, kv_cols)
    )
    piece_qkv = exchange_chips(pack_qkv).reshape(-1, pack_qkv.shape[-1])
    marks = jnp.stack([positions[:, 0] // 32, positions[:, 0] % 32, segments[:, 0]], axis=-1)
    marks = jnp.pad(marks.astype(bf16), ((0, 0), (0, 0), (0, 125)))
    pair = jnp.concatenate([out_cotangent[:, 0], block_input[:, 0], marks], axis=-1)
    pair = jnp.concatenate([pick(pair, core), core_swap(pick(pair, 1 - core))])
    lower, upper = w_down[: w_down.shape[0] // 2], w_down[w_down.shape[0] // 2 :]
    rows = jnp.concatenate([w_out, lower])
    gate_up = scaled(mlp_gain, w_gate, w_up)
    pack_gu = jnp.stack(
        [
            jnp.concatenate([w[:, n * ff_cols : (n + 1) * ff_cols] for w in gate_up], axis=1)
            for n in range(2 * chips)
        ]
    ).reshape(chips, 2, d_rows, 2 * ff_cols)
    pair, piece_qkv, pack_gu = tie(pair, piece_qkv, pack_gu)
    dy_low, x_low = pair[:, :width], pair[:, width:]

    qkv_right, qkv_left = ring_first(piece_qkv)
    piece_gu = exchange_chips(pack_gu)
    qkv_right, qkv_left, piece_gu, x_low, rows = tie(qkv_right, qkv_left, piece_gu, x_low, rows)
    rows = lax.all_gather(rows, "fsdp", axis=0)

    near = [j for j in range(1, chips) if j & (j - 1) == 0]
    far = [j for j in range(1, chips) if j & (j - 1) != 0]
    x_parts = {0: x_low, **{j: chip_xor(x_low, j) for j in near}}
    found_qkv = ring_rest(piece_qkv, qkv_right, qkv_left)
    piece_gu = core_pair(pick(piece_gu, core, 1), core_swap(pick(piece_gu, 1 - core, 1)), 1)
    piece_gu = piece_gu.reshape(2 * chips * d_rows, 2 * ff_cols)
    order = sorted(x_parts)
    piece_gu, *late = tie(piece_gu, *[x_parts[j] for j in order], *pieces_of(found_qkv))
    x_parts = dict(zip(order, late))
    x_parts.update({j: chip_xor(x_low, j) for j in far})
    x_all = jnp.concatenate([x_parts[j] for j in range(chips)])
    found_qkv = again(found_qkv, late[len(order) :])
    marks = x_all[:, width : width + 3].astype(f32).T
    pos_all, seg_all = marks[0] * 32.0 + marks[1], marks[2]
    x_all, x_low = x_all[:, :width], x_low[:, :width]
    allowed = (seg_all[:, None] == seg_all[None, :]) & (pos_all[None, :] <= pos_all[:, None])
    cosine, sine = rope_tables(pos_all)
    w_qkv = assemble(found_qkv, chips)
    w_qkv = core_pair(w_qkv, core_swap(w_qkv), 1).reshape(width, -1)
    w_qkv, x_all, dy_low, cosine, sine, allowed = tie(w_qkv, x_all, dy_low, cosine, sine, allowed)
    own = x_low.shape[0]
    seq = x_all.shape[0]

    x_full = x_all.astype(f32)
    h_one = (x_full * rms_scale(x_full)).astype(bf16)
    qkv = mm(h_one, w_qkv)
    q_rot = rotate(qkv[:, :q_cols].reshape(seq, kv_heads * 2, HEAD), cosine, sine)
    q_rot = q_rot.astype(bf16).reshape(seq, kv_heads, 2, HEAD)
    k_rot = rotate(
        qkv[:, q_cols : q_cols + kv_cols].reshape(seq, kv_heads, HEAD), cosine, sine
    ).astype(bf16)
    value = qkv[:, q_cols + kv_cols :].astype(bf16).reshape(seq, kv_heads, HEAD)
    q_rot, rows, dy_low = tie(q_rot, rows, dy_low)
    dy_all = gather_chips(dy_low)
    along_out = rows[:, : w_out.shape[0]].reshape(-1, width)
    out_w = both_cores(along_out).reshape(-1, width)
    scores = jnp.einsum("sgrh,tgh->grst", q_rot, k_rot, preferred_element_type=f32) * factor
    scores = jnp.where(allowed, scores, -1e30)
    raised = jnp.exp(scores - jnp.max(scores, axis=-1, keepdims=True))
    soft = raised / jnp.sum(raised, axis=-1, keepdims=True)
    soft_low = soft.astype(bf16)
    mixed = jnp.einsum("grst,tgh->sgrh", soft_low, value, preferred_element_type=f32)
    mixed = mixed.astype(bf16).reshape(seq, q_cols)
    mixed, out_w = tie(mixed, out_w)
    x_own = x_low.astype(f32)
    middle = x_own + scatter_chips(mm(mixed, out_w))

    dy_both = jnp.concatenate([dy_all, core_swap(dy_all)])
    along_gu = lax.all_gather(piece_gu, "fsdp", axis=0, tiled=True)
    middle, dy_both, upper = tie(middle, dy_both, upper)
    upper_right, upper_left = ring_first(upper)
    scale_two = rms_scale(middle)
    n_two = middle * scale_two
    h_two = gather_chips(n_two.astype(bf16))
    h_two, upper_right, upper_left = tie(h_two, upper_right, upper_left)
    h_both, along_gu = tie(jnp.concatenate([h_two, core_swap(h_two)]), along_gu)
    along_upper = assemble(ring_rest(upper, upper_right, upper_left), 1)[0]
    along_down = jnp.concatenate([rows[:, w_out.shape[0] :], along_upper], axis=1)
    along_down = along_down.reshape(-1, width)
    w_gu = along_gu.reshape(rows_z, 2 * chips, d_rows, 2 * ff_cols)
    w_gu = jnp.transpose(w_gu, (1, 0, 2, 3)).reshape(width, 2 * ff_cols)
    gu = mm(h_both, w_gu)
    gate, up = gu[:, :ff_cols], gu[:, ff_cols:]
    sigma = jax.nn.sigmoid(gate)
    act = (gate * sigma * up).astype(bf16)
    d_act = mm_nt(dy_both, along_down)
    d_gate = (d_act * up * sigma * (1.0 + gate * (1.0 - sigma))).astype(bf16)
    d_up = (d_act * gate * sigma).astype(bf16)
    d_gu = jnp.concatenate([d_gate, d_up], axis=1)
    g_down = mm_tn(act, dy_both).astype(bf16)
    g_down, d_gu = tie(g_down, d_gu)
    g_down = lax.psum_scatter(g_down, "fsdp", scatter_dimension=0, tiled=True)

    def give_partial(rows, weights, product):
        other = core_swap(product(rows[seq:], weights).astype(bf16)).astype(f32)
        return product(rows[:seq], weights) + other

    d_h_two, act = tie(give_partial(d_gu, w_gu, mm_nt), act)
    g_gu = mm_tn(h_both, d_gu).astype(bf16).reshape(2 * chips, rows_z, d_rows, 2 * ff_cols)
    g_gu = jnp.transpose(g_gu, (1, 0, 2, 3)).reshape(width, 2 * ff_cols)
    d_h_two, g_gu = tie(scatter_chips(d_h_two), g_gu)
    g_gu = lax.psum_scatter(g_gu, "fsdp", scatter_dimension=0, tiled=True)

    dy_own = dy_low.astype(f32)
    d_middle = dy_own + norm_back(d_h_two, n_two, scale_two)
    branch = gather_chips(d_middle.astype(bf16))
    partial = give_partial(act, along_down, mm)
    kept, given = partial[:own], partial[own:].astype(bf16)
    branch, kept, given, g_down = tie(branch, kept, given, g_down)

    g_out = mm_tn(mixed, branch).astype(bf16)
    g_out = g_out.reshape(2, g_out.shape[0] // 2, g_out.shape[1])
    g_out = pick(g_out, core) + core_swap(pick(g_out, 1 - core))
    d_mixed = mm_nt(branch, out_w).astype(bf16).reshape(seq, kv_heads, 2, HEAD)
    d_soft = jnp.einsum("sgrh,tgh->grst", d_mixed, value, preferred_element_type=f32)
    d_value = jnp.einsum("grst,sgrh->tgh", soft_low, d_mixed, preferred_element_type=f32)
    inner = jnp.sum(soft * d_soft, axis=-1, keepdims=True)
    d_scores = (soft * (d_soft - inner)).astype(bf16)
    d_q = jnp.einsum("grst,tgh->sgrh", d_scores, k_rot, preferred_element_type=f32) * factor
    d_k = jnp.einsum("grst,sgrh->tgh", d_scores, q_rot, preferred_element_type=f32) * factor
    d_q = unrotate(d_q.reshape(seq, kv_heads * 2, HEAD), cosine, sine)
    d_k = unrotate(d_k, cosine, sine)
    d_qkv = jnp.concatenate(
        [
            d_q.reshape(seq, q_cols).astype(bf16),
            d_k.reshape(seq, kv_cols).astype(bf16),
            d_value.reshape(seq, kv_cols).astype(bf16),
        ],
        axis=1,
    )
    d_qkv, g_out = tie(d_qkv, g_out)
    cols_qkv = d_qkv.shape[1]
    g_qkv = mm_tn(h_one, d_qkv).astype(bf16).reshape(chips, 2, rows_z, d_rows, cols_qkv)
    g_qkv = pick(g_qkv, core, 1) + core_swap(pick(g_qkv, 1 - core, 1))
    g_qkv = jnp.transpose(g_qkv, (1, 0, 2, 3)).reshape(1, rows_z, chips * d_rows, cols_qkv)
    folds = width // cols_qkv
    g_out = g_out.reshape(1, rows_z, d_rows, width)
    g_rest = [g_out[..., k * cols_qkv : (k + 1) * cols_qkv] for k in range(folds)]
    g_rest = jnp.concatenate([g_qkv] + g_rest, axis=2)
    d_h_one = mm_nt(d_qkv, w_qkv)
    g_rest, d_h_one = tie(g_rest.reshape(-1, cols_qkv), d_h_one)
    g_rest = lax.psum_scatter(g_rest, "fsdp", scatter_dimension=0, tiled=True)
    d_h_one, given, g_gu = tie(scatter_chips(d_h_one), given, g_gu)
    result = middle + kept
    for j in range(1, chips):
        result = result + chip_xor(given[(j - 1) * own : j * own], j).astype(f32)
    g_gu = g_gu.reshape(chips, 2, d_rows, 2 * ff_cols)
    g_gu = core_pair(pick(g_gu, core, 1), core_swap(pick(g_gu, 1 - core, 1)), 1)
    g_gu = exchange_chips(g_gu)
    def spread_ff(grad):
        grad = jnp.transpose(grad.astype(f32), (2, 0, 1, 3))
        return grad.reshape(d_rows, 2 * chips * ff_cols)

    g_gate, g_up = spread_ff(g_gu[..., :ff_cols]), spread_ff(g_gu[..., ff_cols:])

    def of_gain(grads, weights):
        return sum(jnp.sum(g * w.astype(f32), axis=1) for g, w in zip(grads, weights))

    def by_gain(gain, grads):
        return [g * gain.astype(f32)[:, None] for g in grads]

    g_mlp_gain = of_gain((g_gate, g_up), (w_gate, w_up))
    g_gate, g_up = by_gain(mlp_gain, (g_gate, g_up))
    result, g_rest, g_gate, g_up, g_mlp_gain = tie(
        result.astype(bf16), g_rest, g_gate, g_up, g_mlp_gain
    )
    scale_one = rms_scale(x_own)
    n_one = x_own * scale_one
    d_input = (d_middle + norm_back(d_h_one, n_one, scale_one)).astype(bf16)

    def give_back(a):
        mine, theirs = a[:tok], core_swap(a[tok:])
        first = core == 0
        return jnp.stack([jnp.where(first, mine, theirs), jnp.where(first, theirs, mine)])[:, None]

    def spread(grad, start, cols):
        part = grad[:, :, start : start + cols].astype(f32)
        return jnp.transpose(part, (1, 0, 2)).reshape(d_rows, chips * cols)

    g_down = g_down.astype(f32)
    result, d_input = give_back(result), give_back(d_input)
    g_rest, g_gate, g_up, g_down, g_mlp_gain, result, d_input = tie(
        g_rest, g_gate, g_up, g_down, g_mlp_gain, result, d_input
    )
    g_qkv = exchange_chips(g_rest[: chips * d_rows].reshape(chips, d_rows, cols_qkv))
    g_out = g_rest[chips * d_rows :].reshape(folds, d_rows, cols_qkv)
    g_out = jnp.transpose(g_out, (1, 0, 2)).reshape(d_rows, width).astype(f32)
    g_query = spread(g_qkv, 0, q_cols)
    g_key = spread(g_qkv, q_cols, kv_cols)
    g_value = spread(g_qkv, q_cols + kv_cols, kv_cols)
    g_attn_gain = of_gain((g_query, g_key, g_value), (w_query, w_key, w_value))
    g_query, g_key, g_value = by_gain(attn_gain, (g_query, g_key, g_value))
    return (
        result,
        d_input,
        g_attn_gain,
        g_query,
        g_key,
        g_value,
        g_out,
        g_mlp_gain,
        g_gate,
        g_up,
        g_down,
    )


def solution(mesh):
    ctx, fsdp = mesh.shape["ctx"], mesh.shape["fsdp"]
    split = Mesh(mesh.devices.reshape(ctx // 2, 2, fsdp), ("chip", "core", "fsdp"))
    ctx_axes = ("chip", "core")
    all_axes = ("chip", "core", "fsdp")
    tokens = P(None, "fsdp", ctx_axes, None)
    marks = P(None, "fsdp", ctx_axes)
    vector, matrix = P(all_axes), P(all_axes, None)
    return jax.shard_map(
        on_device,
        mesh=split,
        in_specs=(
            tokens, marks, marks, tokens, vector, matrix, matrix, matrix, matrix,
            vector, matrix, matrix, matrix,
        ),
        out_specs=(
            tokens, tokens, vector, matrix, matrix, matrix, matrix, vector,
            matrix, matrix, matrix,
        ),
        check_vma=False,
    )
```

```python
import math

import jax
import jax.numpy as jnp
from jax import lax
from jax.sharding import Mesh, PartitionSpec as P

HEADS = 16
KV_HEADS = 8
HEAD = 96
EPS = 1e-05
THETA = 100000.0
f32 = jnp.float32
bf16 = jnp.bfloat16


def rope_tables(position_ids):
    half = HEAD // 2
    ladder = jnp.arange(half).astype(f32) * (2.0 / HEAD)
    inverse = jnp.exp(-math.log(THETA) * ladder)
    angles = position_ids.astype(f32)[:, None] * inverse[None, :]
    return jnp.cos(angles)[:, None, :], jnp.sin(angles)[:, None, :]


def rotate(vectors, cosine, sine):
    half = HEAD // 2
    a, b = vectors[..., :half], vectors[..., half:]
    return jnp.concatenate([a * cosine - b * sine, b * cosine + a * sine], axis=-1)


def unrotate(grads, cosine, sine):
    half = HEAD // 2
    a, b = grads[..., :half], grads[..., half:]
    return jnp.concatenate([a * cosine + b * sine, b * cosine - a * sine], axis=-1)


def rms_scale(values):
    return lax.rsqrt(jnp.mean(values * values, axis=-1, keepdims=True) + EPS)


def norm_back(grad, normed, scale):
    return scale * (grad - normed * jnp.mean(grad * normed, axis=-1, keepdims=True))


def mm(a, b):
    return jnp.dot(a, b, preferred_element_type=f32)


def mm_tn(a, b):
    return jnp.einsum("td,te->de", a, b, preferred_element_type=f32)


def mm_nt(a, b):
    return jnp.einsum("te,de->td", a, b, preferred_element_type=f32)


def on_device(
    block_input,
    positions,
    segments,
    out_cotangent,
    attn_gain,
    w_query,
    w_key,
    w_value,
    w_out,
    mlp_gain,
    w_gate,
    w_up,
    w_down,
):
    chips = lax.axis_size("chip")
    rows_z = lax.axis_size("fsdp")
    chip = lax.axis_index("chip")
    core = lax.axis_index("core")
    place = lax.axis_index("fsdp")
    tok = block_input.shape[2]
    width = block_input.shape[3]
    d_rows = w_query.shape[0]
    q_cols = w_query.shape[1] // chips
    kv_cols = w_key.shape[1] // chips
    ff_cols = w_gate.shape[1] // (2 * chips)
    kv_heads = KV_HEADS // chips
    factor = HEAD ** (-0.5)

    def core_swap(a):
        return lax.ppermute(a, "core", [(0, 1), (1, 0)])

    def chip_xor(a, j):
        return lax.ppermute(a, "chip", [(i, i ^ j) for i in range(chips)])

    def pick(a, index, axis=0):
        return lax.dynamic_index_in_dim(a, index, axis, keepdims=False)

    def gather_chips(a, axis=0):
        return jnp.concatenate([a] + [chip_xor(a, j) for j in range(1, chips)], axis=axis)

    def scatter_chips(a):
        step = a.shape[0] // chips
        total = a[:step]
        for j in range(1, chips):
            total = total + chip_xor(a[j * step : (j + 1) * step].astype(bf16), j).astype(f32)
        return total

    def by_chip(pieces):
        stacked = jnp.stack(pieces)
        bit = 1
        while bit < chips:
            view = stacked.reshape((chips // (2 * bit), 2, bit) + stacked.shape[1:])
            flipped = jnp.flip(view, axis=1)
            stacked = jnp.where((chip & bit) != 0, flipped, view).reshape(stacked.shape)
            bit *= 2
        return stacked

    def exchange_chips(pack):
        pieces = [pick(pack, chip)]
        for j in range(1, chips):
            pieces.append(chip_xor(pick(pack, chip ^ j), j))
        return by_chip(pieces)

    def core_pair(mine, other, axis):
        first = core == 0
        return jnp.stack([jnp.where(first, mine, other), jnp.where(first, other, mine)], axis)

    def both_cores(a):
        return core_pair(a, core_swap(a), 0)

    def chip_slices(weights, cols):
        return jnp.stack(
            [
                jnp.concatenate([w[:, k * n : (k + 1) * n] for w, n in zip(weights, cols)], axis=1)
                for k in range(chips)
            ]
        )

    def tie(*values):
        return lax.optimization_barrier(values)

    def along_z(a, step):
        return lax.ppermute(a, "fsdp", [(i, (i + step) % rows_z) for i in range(rows_z)])

    def ring_first(a):
        return along_z(a, 1), along_z(a, -1)

    def ring_rest(a, right, left):
        found = [(a, 0, 0), (right, -1, 0), (left, 1, 0)]
        for step in range(2, rows_z // 2 + 1):
            if 2 * step == rows_z:
                half = a.shape[-1] // 2
                found.append((along_z(right[..., :half], 1), -step, 0))
                found.append((along_z(left[..., half:], -1), step, half))
            else:
                right, left = along_z(right, 1), along_z(left, -1)
                found += [(right, -step, 0), (left, step, 0)]
        return found

    def assemble(found, groups):
        rows, cols = found[0][0].shape
        whole = jnp.zeros((groups, rows_z, rows // groups, cols), bf16)
        for piece, offset, column in found:
            piece = piece.reshape(groups, 1, rows // groups, piece.shape[-1])
            index = lax.rem(place + offset + rows_z, rows_z)
            whole = lax.dynamic_update_slice(whole, piece, (0, index, 0, column))
        return whole

    def again(found, pieces):
        return [(piece,) + f[1:] for piece, f in zip(pieces, found)]

    def pieces_of(found):
        return [f[0] for f in found]

    def scaled(gain, *weights):
        return [(w.astype(f32) * gain.astype(f32)[:, None]).astype(bf16) for w in weights]

    pack_qkv = chip_slices(
        scaled(attn_gain, w_query, w_key, w_value), (q_cols, kv_cols, kv_cols)
    )
    piece_qkv = exchange_chips(pack_qkv).reshape(-1, pack_qkv.shape[-1])
    marks = jnp.stack([positions[:, 0] // 32, positions[:, 0] % 32, segments[:, 0]], axis=-1)
    marks = jnp.pad(marks.astype(bf16), ((0, 0), (0, 0), (0, 125)))
    pair = jnp.concatenate([out_cotangent[:, 0], block_input[:, 0], marks], axis=-1)
    pair = jnp.concatenate([pick(pair, core), core_swap(pick(pair, 1 - core))])
    lower, upper = w_down[: w_down.shape[0] // 2], w_down[w_down.shape[0] // 2 :]
    rows = jnp.concatenate([w_out, lower])
    gate_up = scaled(mlp_gain, w_gate, w_up)
    pack_gu = jnp.stack(
        [
            jnp.concatenate([w[:, n * ff_cols : (n + 1) * ff_cols] for w in gate_up], axis=1)
            for n in range(2 * chips)
        ]
    ).reshape(chips, 2, d_rows, 2 * ff_cols)
    pair, piece_qkv, pack_gu = tie(pair, piece_qkv, pack_gu)
    dy_low, x_low = pair[:, :width], pair[:, width:]

    qkv_right, qkv_left = ring_first(piece_qkv)
    piece_gu = exchange_chips(pack_gu)
    qkv_right, qkv_left, piece_gu, x_low, rows = tie(qkv_right, qkv_left, piece_gu, x_low, rows)
    rows = lax.all_gather(rows, "fsdp", axis=0)

    near = [j for j in range(1, chips) if j & (j - 1) == 0]
    far = [j for j in range(1, chips) if j & (j - 1) != 0]
    x_parts = {0: x_low, **{j: chip_xor(x_low, j) for j in near}}
    found_qkv = ring_rest(piece_qkv, qkv_right, qkv_left)
    piece_gu = core_pair(pick(piece_gu, core, 1), core_swap(pick(piece_gu, 1 - core, 1)), 1)
    piece_gu = piece_gu.reshape(2 * chips * d_rows, 2 * ff_cols)
    order = sorted(x_parts)
    piece_gu, *late = tie(piece_gu, *[x_parts[j] for j in order], *pieces_of(found_qkv))
    x_parts = dict(zip(order, late))
    x_parts.update({j: chip_xor(x_low, j) for j in far})
    x_all = jnp.concatenate([x_parts[j] for j in range(chips)])
    found_qkv = again(found_qkv, late[len(order) :])
    marks = x_all[:, width : width + 3].astype(f32).T
    pos_all, seg_all = marks[0] * 32.0 + marks[1], marks[2]
    x_all, x_low = x_all[:, :width], x_low[:, :width]
    allowed = (seg_all[:, None] == seg_all[None, :]) & (pos_all[None, :] <= pos_all[:, None])
    cosine, sine = rope_tables(pos_all)
    w_qkv = assemble(found_qkv, chips)
    w_qkv = core_pair(w_qkv, core_swap(w_qkv), 1).reshape(width, -1)
    w_qkv, x_all, dy_low, cosine, sine, allowed = tie(w_qkv, x_all, dy_low, cosine, sine, allowed)
    own = x_low.shape[0]
    seq = x_all.shape[0]

    x_full = x_all.astype(f32)
    h_one = (x_full * rms_scale(x_full)).astype(bf16)
    qkv = mm(h_one, w_qkv)
    q_rot = rotate(qkv[:, :q_cols].reshape(seq, kv_heads * 2, HEAD), cosine, sine)
    q_rot = q_rot.astype(bf16).reshape(seq, kv_heads, 2, HEAD)
    k_rot = rotate(
        qkv[:, q_cols : q_cols + kv_cols].reshape(seq, kv_heads, HEAD), cosine, sine
    ).astype(bf16)
    value = qkv[:, q_cols + kv_cols :].astype(bf16).reshape(seq, kv_heads, HEAD)
    q_rot, rows, dy_low = tie(q_rot, rows, dy_low)
    dy_all = gather_chips(dy_low)
    along_out = rows[:, : w_out.shape[0]].reshape(-1, width)
    out_w = both_cores(along_out).reshape(-1, width)
    scores = jnp.einsum("sgrh,tgh->grst", q_rot, k_rot, preferred_element_type=f32) * factor
    scores = jnp.where(allowed, scores, -1e30)
    raised = jnp.exp(scores - jnp.max(scores, axis=-1, keepdims=True))
    soft = raised / jnp.sum(raised, axis=-1, keepdims=True)
    soft_low = soft.astype(bf16)
    mixed = jnp.einsum("grst,tgh->sgrh", soft_low, value, preferred_element_type=f32)
    mixed = mixed.astype(bf16).reshape(seq, q_cols)
    mixed, out_w = tie(mixed, out_w)
    x_own = x_low.astype(f32)
    middle = x_own + scatter_chips(mm(mixed, out_w))

    dy_both = jnp.concatenate([dy_all, core_swap(dy_all)])
    along_gu = lax.all_gather(piece_gu, "fsdp", axis=0, tiled=True)
    middle, dy_both, upper = tie(middle, dy_both, upper)
    upper_right, upper_left = ring_first(upper)
    scale_two = rms_scale(middle)
    n_two = middle * scale_two
    h_two = gather_chips(n_two.astype(bf16))
    h_two, upper_right, upper_left = tie(h_two, upper_right, upper_left)
    h_both, along_gu = tie(jnp.concatenate([h_two, core_swap(h_two)]), along_gu)
    along_upper = assemble(ring_rest(upper, upper_right, upper_left), 1)[0]
    along_down = jnp.concatenate([rows[:, w_out.shape[0] :], along_upper], axis=1)
    along_down = along_down.reshape(-1, width)
    w_gu = along_gu.reshape(rows_z, 2 * chips, d_rows, 2 * ff_cols)
    w_gu = jnp.transpose(w_gu, (1, 0, 2, 3)).reshape(width, 2 * ff_cols)
    gu = mm(h_both, w_gu)
    gate, up = gu[:, :ff_cols], gu[:, ff_cols:]
    sigma = jax.nn.sigmoid(gate)
    act = (gate * sigma * up).astype(bf16)
    d_act = mm_nt(dy_both, along_down)
    d_gate = (d_act * up * sigma * (1.0 + gate * (1.0 - sigma))).astype(bf16)
    d_up = (d_act * gate * sigma).astype(bf16)
    d_gu = jnp.concatenate([d_gate, d_up], axis=1)
    g_down = mm_tn(act, dy_both).astype(bf16)
    g_down, d_gu = tie(g_down, d_gu)
    g_down = lax.psum_scatter(g_down, "fsdp", scatter_dimension=0, tiled=True)

    def give_partial(rows, weights, product):
        other = core_swap(product(rows[seq:], weights).astype(bf16)).astype(f32)
        return product(rows[:seq], weights) + other

    d_h_two, act = tie(give_partial(d_gu, w_gu, mm_nt), act)
    g_gu = mm_tn(h_both, d_gu).astype(bf16).reshape(2 * chips, rows_z, d_rows, 2 * ff_cols)
    g_gu = jnp.transpose(g_gu, (1, 0, 2, 3)).reshape(width, 2 * ff_cols)
    d_h_two, g_gu = tie(scatter_chips(d_h_two), g_gu)
    g_gu = lax.psum_scatter(g_gu, "fsdp", scatter_dimension=0, tiled=True)

    dy_own = dy_low.astype(f32)
    d_middle = dy_own + norm_back(d_h_two, n_two, scale_two)
    branch = gather_chips(d_middle.astype(bf16))
    partial = give_partial(act, along_down, mm)
    kept, given = partial[:own], partial[own:].astype(bf16)
    branch, kept, given, g_down = tie(branch, kept, given, g_down)

    g_out = mm_tn(mixed, branch).astype(bf16)
    g_out = g_out.reshape(2, g_out.shape[0] // 2, g_out.shape[1])
    g_out = pick(g_out, core) + core_swap(pick(g_out, 1 - core))
    d_mixed = mm_nt(branch, out_w).astype(bf16).reshape(seq, kv_heads, 2, HEAD)
    d_soft = jnp.einsum("sgrh,tgh->grst", d_mixed, value, preferred_element_type=f32)
    d_value = jnp.einsum("grst,sgrh->tgh", soft_low, d_mixed, preferred_element_type=f32)
    inner = jnp.sum(soft * d_soft, axis=-1, keepdims=True)
    d_scores = (soft * (d_soft - inner)).astype(bf16)
    d_q = jnp.einsum("grst,tgh->sgrh", d_scores, k_rot, preferred_element_type=f32) * factor
    d_k = jnp.einsum("grst,sgrh->tgh", d_scores, q_rot, preferred_element_type=f32) * factor
    d_q = unrotate(d_q.reshape(seq, kv_heads * 2, HEAD), cosine, sine)
    d_k = unrotate(d_k, cosine, sine)
    d_qkv = jnp.concatenate(
        [
            d_q.reshape(seq, q_cols).astype(bf16),
            d_k.reshape(seq, kv_cols).astype(bf16),
            d_value.reshape(seq, kv_cols).astype(bf16),
        ],
        axis=1,
    )
    d_qkv, g_out = tie(d_qkv, g_out)
    cols_qkv = d_qkv.shape[1]
    g_qkv = mm_tn(h_one, d_qkv).astype(bf16).reshape(chips, 2, rows_z, d_rows, cols_qkv)
    g_qkv = pick(g_qkv, core, 1) + core_swap(pick(g_qkv, 1 - core, 1))
    g_qkv = jnp.transpose(g_qkv, (1, 0, 2, 3)).reshape(1, rows_z, chips * d_rows, cols_qkv)
    folds = width // cols_qkv
    g_out = g_out.reshape(1, rows_z, d_rows, width)
    g_rest = [g_out[..., k * cols_qkv : (k + 1) * cols_qkv] for k in range(folds)]
    g_rest = jnp.concatenate([g_qkv] + g_rest, axis=2)
    d_h_one = mm_nt(d_qkv, w_qkv)
    g_rest, d_h_one = tie(g_rest.reshape(-1, cols_qkv), d_h_one)
    g_rest = lax.psum_scatter(g_rest, "fsdp", scatter_dimension=0, tiled=True)
    d_h_one, given, g_gu = tie(scatter_chips(d_h_one), given, g_gu)
    g_gu = g_gu.reshape(chips, 2, d_rows, 2 * ff_cols)
    g_gu = core_pair(pick(g_gu, core, 1), core_swap(pick(g_gu, 1 - core, 1)), 1)
    g_gu = exchange_chips(g_gu)
    given, g_gu = tie(given, g_gu)
    result = middle + kept
    for j in range(1, chips):
        result = result + chip_xor(given[(j - 1) * own : j * own], j).astype(f32)
    def spread_ff(grad):
        grad = jnp.transpose(grad.astype(f32), (2, 0, 1, 3))
        return grad.reshape(d_rows, 2 * chips * ff_cols)

    g_gate, g_up = spread_ff(g_gu[..., :ff_cols]), spread_ff(g_gu[..., ff_cols:])

    def of_gain(grads, weights):
        return sum(jnp.sum(g * w.astype(f32), axis=1) for g, w in zip(grads, weights))

    def by_gain(gain, grads):
        return [g * gain.astype(f32)[:, None] for g in grads]

    g_mlp_gain = of_gain((g_gate, g_up), (w_gate, w_up))
    g_gate, g_up = by_gain(mlp_gain, (g_gate, g_up))
    result, g_rest, g_gate, g_up, g_mlp_gain = tie(
        result.astype(bf16), g_rest, g_gate, g_up, g_mlp_gain
    )
    scale_one = rms_scale(x_own)
    n_one = x_own * scale_one
    d_input = (d_middle + norm_back(d_h_one, n_one, scale_one)).astype(bf16)

    def give_back(a):
        mine, theirs = a[:tok], core_swap(a[tok:])
        first = core == 0
        return jnp.stack([jnp.where(first, mine, theirs), jnp.where(first, theirs, mine)])[:, None]

    def spread(grad, start, cols):
        part = grad[:, :, start : start + cols].astype(f32)
        return jnp.transpose(part, (1, 0, 2)).reshape(d_rows, chips * cols)

    g_down = g_down.astype(f32)
    result, d_input = give_back(result), give_back(d_input)
    g_rest, g_gate, g_up, g_down, g_mlp_gain, result, d_input = tie(
        g_rest, g_gate, g_up, g_down, g_mlp_gain, result, d_input
    )
    g_qkv = exchange_chips(g_rest[: chips * d_rows].reshape(chips, d_rows, cols_qkv))
    g_out = g_rest[chips * d_rows :].reshape(folds, d_rows, cols_qkv)
    g_out = jnp.transpose(g_out, (1, 0, 2)).reshape(d_rows, width).astype(f32)
    g_query = spread(g_qkv, 0, q_cols)
    g_key = spread(g_qkv, q_cols, kv_cols)
    g_value = spread(g_qkv, q_cols + kv_cols, kv_cols)
    g_attn_gain = of_gain((g_query, g_key, g_value), (w_query, w_key, w_value))
    g_query, g_key, g_value = by_gain(attn_gain, (g_query, g_key, g_value))
    return (
        result,
        d_input,
        g_attn_gain,
        g_query,
        g_key,
        g_value,
        g_out,
        g_mlp_gain,
        g_gate,
        g_up,
        g_down,
    )


def solution(mesh):
    ctx, fsdp = mesh.shape["ctx"], mesh.shape["fsdp"]
    split = Mesh(mesh.devices.reshape(ctx // 2, 2, fsdp), ("chip", "core", "fsdp"))
    ctx_axes = ("chip", "core")
    all_axes = ("chip", "core", "fsdp")
    tokens = P(None, "fsdp", ctx_axes, None)
    marks = P(None, "fsdp", ctx_axes)
    vector, matrix = P(all_axes), P(all_axes, None)
    return jax.shard_map(
        on_device,
        mesh=split,
        in_specs=(
            tokens, marks, marks, tokens, vector, matrix, matrix, matrix, matrix,
            vector, matrix, matrix, matrix,
        ),
        out_specs=(
            tokens, tokens, vector, matrix, matrix, matrix, matrix, vector,
            matrix, matrix, matrix,
        ),
        check_vma=False,
    )
```
